32 devices in a mesh: blk: 8 (over z, y), head: 4 (over x, core).
Axes of the slice: x: 2, y: 2, z: 4, core: 2. Of those that a mesh axis runs over, the one named last changes fastest.
Arguments:
- tokens: bfloat16 [2, 12288, 768], P(None, ('blk', 'head')), may hold values from -6 to 6
- w_query: bfloat16 [768, 768], P(('blk', 'head')), may hold values from -0.3125 to 0.3125
- w_key: bfloat16 [768, 768], P(('blk', 'head')), may hold values from -0.3125 to 0.3125
- w_value: bfloat16 [768, 768], P(('blk', 'head')), may hold values from -0.21875 to 0.21875
- w_out: bfloat16 [768, 768], P(('blk', 'head')), may hold values from -0.625 to 0.625
- conv_kernel: bfloat16 [12, 33], P('head'), may hold values from -0.5 to 0.5
- norm1_gain: bfloat16 [768], P(('blk', 'head')), may hold values from 0.25 to 1.75
- w_up: bfloat16 [768, 3072], P(('blk', 'head')), may hold values from -0.21875 to 0.21875
- w_down: bfloat16 [3072, 768], P(('blk', 'head')), may hold values from -0.21875 to 0.21875
- norm2_gain: bfloat16 [768], P(('blk', 'head')), may hold values from 0.25 to 1.75
- cotangent: bfloat16 [2, 12288, 768], P(None, ('blk', 'head')), may hold values from -6 to 6
Outputs:
- layer_out: bfloat16 [2, 12288, 768], P(None, ('blk', 'head'))
- grad_tokens: bfloat16 [2, 12288, 768], P(None, ('blk', 'head'))
- grad_query: float32 [768, 768], P(('blk', 'head'))
- grad_key: float32 [768, 768], P(('blk', 'head'))
- grad_value: float32 [768, 768], P(('blk', 'head'))
- grad_out: float32 [768, 768], P(('blk', 'head'))
- grad_conv: float32 [12, 33], P('head')
- grad_norm1: float32 [768], P(('blk', 'head'))
- grad_up: float32 [768, 3072], P(('blk', 'head'))
- grad_down: float32 [3072, 768], P(('blk', 'head'))
- grad_norm2: float32 [768], P(('blk', 'head'))
The draws below stay inside these ranges and needn't reach their ends.
All inputs are finite; a program needn't handle non-finite values.
Results may differ from the reference program's by a relative error of at most 0.015.
The reference program's roundings to bfloat16 on the way count: a program that leaves them out, or rounds other values in their place, can miss the bound.
Values may be sent and summed in bfloat16 or wider, within the bound.
No kernel may reach another device: no remote copies, remote signals or barrier semaphores. Data moves between devices by JAX's collectives and lax.ppermute only.
A program may use at most 192 MiB of HBM per device.

```python
import jax
import jax.numpy as jnp
from jax import lax

D = 768
H = 12
HD = 64
FF = 3072
M = 64
KW = 33
NEWTON = 6
SEQS = 2
LEN = 12288


def draw_tokens(key, part):
    rough_key = jax.random.fold_in(key, 11)
    span_key = jax.random.fold_in(key, 12)
    rough = jax.random.normal(rough_key, (SEQS, LEN, D), jnp.float32) * 0.6
    spans = jax.random.normal(span_key, (SEQS, M, D), jnp.float32) * 0.8
    whole = rough + jnp.repeat(spans, LEN // M, axis=1)
    return jnp.clip(whole, -6.0, 6.0).astype(jnp.bfloat16)


def levels(stream_key, dims, pieces, least, top_value):
    def one(dim, blocks):
        draws = jax.random.uniform(jax.random.fold_in(jax.random.fold_in(stream_key, 6), dim), (blocks,), jnp.float32, least / len(pieces), top_value / len(pieces))
        return jnp.repeat(jnp.exp(draws), dims[dim] // blocks).reshape((-1,) + (1,) * (len(dims) - dim - 1))

    level = one(*pieces[0])
    for cut in pieces[1:]:
        level = level * one(*cut)
    return level


def normal_values(own_key, dims, scale, limit, pieces=(), kind=jnp.bfloat16):
    values = scale * jax.random.normal(own_key, dims, jnp.float32)
    if pieces:
        values = values * levels(own_key, dims, pieces, -0.22, 0.18)
    return jnp.clip(values, -limit, limit).astype(kind)


def setup_inputs(seed: int = 0) -> dict:
    seeds = jax.random.split(jax.random.key(seed), 12)
    tokens = draw_tokens(jax.random.fold_in(seeds[11], 71), 0)
    w_query = normal_values(seeds[1], (D, D), (D // 2) ** -0.5, 0.3125, ((0, 32),))
    w_key = normal_values(seeds[2], (D, D), (D // 2) ** -0.5, 0.3125, ((0, 32),))
    w_value = normal_values(seeds[3], (D, D), D ** -0.5, 0.21875, ((0, 32),))
    w_out = normal_values(seeds[4], (D, D), (D // 8) ** -0.5, 0.625, ((0, 32),))
    conv_kernel = normal_values(seeds[5], (H, KW), (KW * 4) ** -0.5, 0.5, ((0, 4),))
    norm1_gain = jnp.clip(1.0 + 0.15 * jax.random.normal(seeds[6], (D,), jnp.float32), 0.25, 1.75).astype(jnp.bfloat16)
    w_up = normal_values(seeds[7], (D, FF), D ** -0.5, 0.21875, ((0, 32),))
    w_down = normal_values(seeds[8], (FF, D), (FF // 4) ** -0.5, 0.21875, ((0, 32),))
    norm2_gain = jnp.clip(1.0 + 0.15 * jax.random.normal(seeds[9], (D,), jnp.float32), 0.25, 1.75).astype(jnp.bfloat16)
    cotangent = normal_values(seeds[10], (SEQS, LEN, D), 1.0, 6.0, ((1, 32),))
    return dict(tokens=tokens, w_query=w_query, w_key=w_key, w_value=w_value, w_out=w_out, conv_kernel=conv_kernel, norm1_gain=norm1_gain, w_up=w_up, w_down=w_down, norm2_gain=norm2_gain, cotangent=cotangent)


@jax.custom_vjp
def low(v):
    return lax.optimization_barrier(v.astype(jnp.bfloat16)).astype(jnp.float32)

@jax.custom_vjp
def low_back(v):
    return v

def low_keep(v):
    return (low(v), None)

def low_pass(kept, grad):
    return (grad,)

def back_keep(v):
    return (v, None)

def back_low(kept, grad):
    return (low(grad),)
low.defvjp(low_keep, low_pass)
low_back.defvjp(back_keep, back_low)
precision_highest = lax.Precision.HIGHEST
epsilon = 1e-05

def layer_norm(hidden, gain):
    center = hidden - lax.optimization_barrier(jnp.mean(hidden, axis=-1, keepdims=True))
    spread = lax.optimization_barrier(jnp.mean(center * center, axis=-1, keepdims=True))
    return center * lax.rsqrt(spread + epsilon) * gain

def inverse_newton(kernel):
    column = lax.optimization_barrier(jnp.sum(kernel, axis=-2))
    largest = lax.optimization_barrier(jnp.max(column, axis=-1))
    identity = jnp.eye(kernel.shape[-1], dtype=kernel.dtype)
    approx = jnp.swapaxes(kernel, -1, -2) / largest[..., None, None]
    for iteration in range(NEWTON):
        product = jnp.matmul(kernel, approx, precision=precision_highest)
        inner = 7.0 * identity - product
        inner = 15.0 * identity - jnp.matmul(product, inner, precision=precision_highest)
        inner = 13.0 * identity - jnp.matmul(product, inner, precision=precision_highest)
        approx = 0.25 * jnp.matmul(approx, inner, precision=precision_highest)
    return approx

def forward(tokens, w_query, w_key, w_value, w_out, conv_kernel, norm1_gain, w_up, w_down, norm2_gain):
    sequences, length, width = tokens.shape
    segment = length // M
    reach = KW // 2
    scale = HD ** (-0.25)

    def project(source_tensor, square_matrix):
        return jnp.einsum('qgr,rj->qgj', source_tensor, square_matrix, precision=precision_highest)
    shape = (sequences, length, H, HD)
    queries = low(low_back(project(tokens, w_query) * scale)).reshape(shape)
    keys = low(low_back(project(tokens, w_key) * scale)).reshape(shape)
    values = low(low_back(project(tokens, w_value))).reshape(shape)
    query_land = low(lax.optimization_barrier(jnp.mean(queries.reshape(sequences, M, segment, H, HD), axis=2)))
    key_land = low(lax.optimization_barrier(jnp.mean(keys.reshape(sequences, M, segment, H, HD), axis=2)))
    score_one = low_back(jnp.einsum('snhd,smhd->shnm', queries, key_land, precision=precision_highest))
    kernel_one = low(jax.nn.softmax(score_one, axis=-1))
    kernel_two = jax.nn.softmax(jnp.einsum('smhd,sjhd->shmj', query_land, key_land, precision=precision_highest), axis=-1)
    score_three = low_back(jnp.einsum('smhd,snhd->shmn', query_land, keys, precision=precision_highest))
    kernel_three = low(jax.nn.softmax(score_three, axis=-1))
    summary = jnp.einsum('shmn,snhd->shmd', kernel_three, values, precision=precision_highest)
    mixed = low(jnp.einsum('shmj,shjd->shmd', inverse_newton(kernel_two), summary, precision=precision_highest))
    attend = jnp.einsum('shnm,shmd->snhd', kernel_one, mixed, precision=precision_highest)
    padded = jnp.pad(values, ((0, 0), (reach, reach), (0, 0), (0, 0)))
    convolved = jnp.zeros(shape, jnp.float32)
    for offset in range(KW):
        convolved = convolved + padded[:, offset:offset + length] * conv_kernel[:, offset][:, None]
    heads_out = low(low_back(attend + convolved)).reshape(sequences, length, width)
    branch = low_back(project(heads_out, w_out))
    norm_one = layer_norm(tokens + branch, norm1_gain)
    upper = low_back(jnp.einsum('snd,df->snf', low(norm_one), w_up, precision=precision_highest))
    active = low(jax.nn.gelu(upper, approximate=False))
    down = low_back(jnp.einsum('snf,fd->snd', active, w_down, precision=precision_highest))
    return layer_norm(norm_one + down, norm2_gain)

def reference(tokens, w_query, w_key, w_value, w_out, conv_kernel, norm1_gain, w_up, w_down, norm2_gain, cotangent):
    inputs = [item.astype(jnp.float32) for item in (tokens, w_query, w_key, w_value, w_out, conv_kernel, norm1_gain, w_up, w_down, norm2_gain)]
    result, pullback = jax.vjp(forward, *inputs)
    grads = pullback(cotangent.astype(jnp.float32))
    return (result.astype(jnp.bfloat16), grads[0].astype(jnp.bfloat16), grads[1], grads[2], grads[3], grads[4], grads[5], grads[6], grads[7], grads[8], grads[9])
```

```python
import functools

import jax
import jax.numpy as jnp
from jax import lax
from jax.experimental import pallas as pl
from jax.experimental.pallas import tpu as pltpu
from jax.sharding import PartitionSpec as P

HD = 64
M = 64
KW = 33
NEWTON = 6
REACH = KW // 2
AX = ("blk", "head")
EPS = 1e-05
GW = 256
HP = GW // HD
CT = 128
CE = CT + 2 * REACH

bf16 = jnp.bfloat16
f32 = jnp.float32
HIGHEST = lax.Precision.HIGHEST


def nn(a, b):
    return lax.dot_general(a, b, (((1,), (0,)), ((), ())), preferred_element_type=f32)


def nt(a, b):
    return lax.dot_general(a, b, (((1,), (1,)), ((), ())), preferred_element_type=f32)


def tn(a, b):
    return lax.dot_general(a, b, (((0,), (0,)), ((), ())), preferred_element_type=f32)


def exact(a, b, dims=((1,), (0,))):
    return lax.dot_general(a, b, (dims, ((), ())), preferred_element_type=f32, precision=HIGHEST)


def iota(shape, dim):
    return lax.broadcasted_iota(jnp.int32, shape, dim)


def vmem_call(kernel, outs, args, scalars=0, scratch=(), limit=40):
    specs = [pl.BlockSpec(memory_space=pltpu.SMEM)] * scalars
    specs += [pl.BlockSpec(memory_space=pltpu.VMEM)] * (len(args) - scalars)
    return pl.pallas_call(
        kernel,
        out_shape=outs,
        in_specs=specs,
        out_specs=jax.tree.map(lambda _: pl.BlockSpec(memory_space=pltpu.VMEM), outs),
        scratch_shapes=list(scratch),
        compiler_params=pltpu.CompilerParams(vmem_limit_bytes=limit << 20),
    )(*args)


def shape_of(dims, dtype):
    return jax.ShapeDtypeStruct(tuple(dims), dtype)


def cube_masks(n):
    masks = [1 << b for b in range(n.bit_length() - 1)]
    if len(masks) >= 2:
        masks[-1] |= masks[-2]
    return masks


def coefficients(v, n):
    bits = [(v >> b) & 1 for b in range(n.bit_length() - 1)]
    if len(bits) >= 2:
        bits[-2] = bits[-2] ^ bits[-1]
    return bits


def scatter_order(n, core, turn):
    rest = [b for b in range(n.bit_length() - 1) if b != core]
    return (rest, [rest[1], rest[0], *rest[2:]], [*rest[2:], *rest[:2]])[turn]


def gather_order(n, core, turn):
    return list(reversed(scatter_order(n, core, turn)))


def swap(x, n, dim):
    mask = cube_masks(n)[dim]
    return lax.ppermute(x, AX, [(i, i ^ mask) for i in range(n)])


def gather_slot(v, n, core, turn):
    bits = coefficients(v, n)
    slot = 0
    for place, dim in enumerate(gather_order(n, core, turn)):
        slot = slot + (bits[dim] << place)
    return slot


def scatter_slot(v, n, core, turn):
    bits = coefficients(v, n)
    slot = 0
    for place, dim in enumerate(reversed(scatter_order(n, core, turn))):
        slot = slot + (bits[dim] << place)
    return slot


def cube_gather(piece, n, core):
    buf = piece[None]
    first, second = gather_order(n, core, 0), gather_order(n, core, 1)
    for dim in first[:-2]:
        buf = jnp.concatenate([buf, swap(buf, n, dim)], axis=0)
    half = piece.shape[1] // 2
    bufs = [buf[:, :, :half], buf[:, :, half:]]
    for dims in zip(first[-2:], second[-2:]):
        got = [swap(x, n, dim) for x, dim in zip(bufs, dims)]
        bufs = [jnp.concatenate(pair, axis=0) for pair in zip(bufs, got)]
    return bufs + [swap(x, n, core) for x in bufs]


def merged(jobs, last):
    shapes = []
    for pairs in jobs:
        slots = pairs[0][0].shape[0]
        joint = (sum(k.shape[1] for k, _ in pairs), pairs[0][0].shape[2])
        if last:
            shapes.append(shape_of((slots,) + joint, f32))
        else:
            shapes += [shape_of((slots // 2,) + joint, t) for t in (f32, bf16)]
    args = [x for pairs in jobs for pair in pairs for x in pair]
    outs = vmem_call(
        functools.partial(merge_kernel, [len(pairs) for pairs in jobs], last), shapes, args
    )
    return outs if last else list(zip(outs[0::2], outs[1::2]))


def cube_scatter(jobs, n, core):
    orders = [[core, *scatter_order(n, core, turn)] for turn in range(len(jobs))]
    jobs = [[(k, swap(s, n, core)) for k, s in job] for job in jobs]
    for step in range(1, len(orders[0])):
        state = merged(jobs, False)
        jobs = [[(k, swap(s, n, o[step]))] for (k, s), o in zip(state, orders)]
        if step == 2:
            jobs = [jobs[0] + jobs[1]] + jobs[2:]
            orders = orders[:1] + orders[2:]
    return [x[0] for x in merged(jobs, True)]


def emit(acc, first_row, rows, stride, keep, send, rows_at, me, n, core, turn, count=None, first=0):
    count = n if count is None else count
    mine = me & 1
    span = slice(rows_at, rows_at + rows)

    def step(i, c):
        d = 2 * i
        slot = scatter_slot(jnp.bitwise_xor(me - mine, first + d), n, core, turn)
        low = pl.multiple_of(first_row + (d + mine) * stride, 8)
        high = pl.multiple_of(first_row + (d + 1 - mine) * stride, 8)
        keep[slot, span, :] = acc[pl.ds(low, rows), :].astype(bf16)
        send[slot, span, :] = acc[pl.ds(high, rows), :].astype(bf16)
        return c

    lax.fori_loop(0, count // 2, step, 0)


def aligned(i, size):
    return pl.ds(pl.multiple_of(i * size, size), size)


def block_mask():
    return (iota((GW, GW), 0) // HD) == (iota((GW, GW), 1) // HD)


def block_diagonal(x):
    wide = jnp.concatenate([x] * HP, axis=0)
    return jnp.where(block_mask(), wide, jnp.zeros_like(wide))


def diagonal_half(x, j):
    return x[j * HD : (j + 1) * HD, 128 * (j // 2) : 128 * (j // 2) + 128]


def low_lanes(x, j):
    return pltpu.roll(x, HD, 1) if j % 2 else x


def high_lanes(x, j):
    return x if j % 2 else pltpu.roll(x, HD, 1)


def block_from_slots(read):
    rows = []
    lane = iota((HD, 128), 1)
    for j in range(HP):
        half = jnp.where(lane < HD, read(j), 0.0)
        if j % 2:
            half = pltpu.roll(half, HD, 1)
        zero = jnp.zeros_like(half)
        rows.append(jnp.concatenate([half, zero] if j < 2 else [zero, half], axis=1))
    return jnp.concatenate(rows, axis=0).astype(bf16)


def qkv_kernel(cfg, me_ref, x_ref, *refs):
    n, core, hyper, rows, parts, scale, segment, heads_dev, head_size = cfg
    ins, refs = refs[:4], refs[4:]
    q_ref, k_ref, v_ref, land_ref, toep_ref, peot_ref, gain_ref, wq, wk, wv = refs
    me = me_ref[0]
    width = x_ref.shape[1]
    if hyper:
        mine = me & 1
        half = width // 2

        def pieces(pair, turn, span, lanes):
            slot = gather_slot(jnp.bitwise_xor(me - mine, 2 * pair), n, core, turn)
            own = ins[turn][slot, span, lanes]
            other = ins[2 + turn][slot, span, lanes]
            return jnp.where(mine == 0, own, other), jnp.where(mine == 0, other, own)

        def place_rows(pair, c):
            to = pl.ds(pl.multiple_of(2 * rows * pair, 16), 2 * rows)
            for turn in range(2):
                lanes = slice(turn * half, (turn + 1) * half)
                for unit, out in enumerate((wq, wk, wv)):
                    span = slice(unit * rows, (unit + 1) * rows)
                    out[to, lanes] = jnp.concatenate(pieces(pair, turn, span, slice(None)), axis=0)
            return c

        lax.fori_loop(0, n // 2, place_rows, 0)

        def small_rows(d):
            return pieces(d // 2, 0, slice(3 * rows, 3 * rows + 8), slice(0, GW))[d % 2]

    else:
        for out, piece in zip((wq, wk, wv), ins):
            out[...] = piece[...]

        def small_rows(d):
            return ins[3][d, :, 0:GW]

    q_ref[...] = (nn(x_ref[...], wq[...]) * scale).astype(bf16)
    k_ref[...] = (nn(x_ref[...], wk[...]) * scale).astype(bf16)
    v_ref[...] = nn(x_ref[...], wv[...]).astype(bf16)
    pieces_land = []
    each = x_ref.shape[0] // (2 * parts)
    for ref in (q_ref, k_ref):
        for at_row in range(2 * parts):
            span = ref[at_row * each : (at_row + 1) * each, :].astype(f32)
            pieces_land.append(jnp.sum(span, axis=0, keepdims=True) * (1.0 / segment))
    if parts < 2:
        pieces_land.append(jnp.zeros((8 - 4 * parts, width), f32))
    shared = jnp.concatenate(pieces_land, axis=0).astype(land_ref.dtype)
    for d in range(n):
        land_ref[d] = shared
    place = (iota((128, width), 1) % rows == iota((128, width), 0)).astype(bf16)
    gains = jnp.zeros(gain_ref.shape, f32)
    for d in range(n):
        small = small_rows(d)
        inside = iota((8, width), 1) // rows == d
        gains = gains + jnp.where(inside, nn(small[:, 0:128], place), 0.0)
        if d < head_size:
            taps = small.astype(f32)
            for i in range(heads_dev):
                for row, out in ((i, toep_ref), (heads_dev + i, peot_ref)):
                    spread = jnp.broadcast_to(taps[row : row + 1, :], (CT, GW))
                    spread = pltpu.roll(spread, 0, 1, stride=1, stride_axis=0)
                    out[d * heads_dev + i] = spread[:, 0:CE].astype(bf16)
    gain_ref[...] = gains


def newton_kernel(heads, me_ref, ql_ref, kl_ref, inv_ref, keep_ref, two_ref):
    unit = lax.rem(me_ref[0], 2 * heads)
    second = unit >= heads
    head = jnp.where(second, unit - heads, unit)
    width = ql_ref.shape[1]
    pick = (iota((width, HD), 0) == iota((width, HD), 1) + head * HD).astype(bf16)

    def mine(ref):
        rows = jnp.where(second, ref[M : 2 * M, :].astype(f32), ref[0:M, :].astype(f32))
        return nn(rows.astype(bf16), pick).astype(bf16)

    query, key = mine(ql_ref), mine(kl_ref)
    score = nt(query, key)
    e = jnp.exp(score - jnp.max(score, axis=1, keepdims=True))
    kernel = e / jnp.sum(e, axis=1, keepdims=True)
    column = jnp.sum(kernel, axis=0, keepdims=True)
    largest = jnp.max(column, axis=1, keepdims=True)
    eye = (iota((M, M), 0) == iota((M, M), 1)).astype(f32)
    z = kernel.T / largest
    two_ref[0] = kernel
    two_ref[1] = column + jnp.zeros_like(kernel)
    two_ref[2] = query.astype(f32)
    two_ref[3] = key.astype(f32)
    for step in range(NEWTON):
        p = exact(kernel, z)
        a = 7.0 * eye - p
        b = 15.0 * eye - exact(p, a)
        c = 13.0 * eye - exact(p, b)
        keep_ref[step, 0] = z
        keep_ref[step, 1] = p
        keep_ref[step, 2] = a
        keep_ref[step, 3] = b
        keep_ref[step, 4] = c
        z = 0.25 * exact(z, c)
    inv_ref[...] = z


def newton_back_kernel(
    heads, me_ref, dinv_ref, inv_ref, keep_ref, two_ref, dq_ref, dk_ref
):
    turned = ((0,), (0,))
    across = ((1,), (1,))
    kernel = two_ref[0]
    dz = dinv_ref[...]
    dkernel = jnp.zeros_like(kernel)
    for step in reversed(range(NEWTON)):
        z, p, a, b, c = (keep_ref[step, i] for i in range(5))
        dc = 0.25 * exact(z, dz, turned)
        db = -exact(p, dc, turned)
        da = -exact(p, db, turned)
        dp = -exact(dc, b, across) - exact(db, a, across) - da
        dkernel = dkernel + exact(dp, z, across)
        dz = 0.25 * exact(dz, c, across) + exact(kernel, dp, turned)
    column = two_ref[1]
    largest = jnp.max(column[0:1, :], axis=1, keepdims=True)
    dkernel = dkernel + dz.T / largest
    dlargest = -jnp.sum(dz * kernel.T, keepdims=True) / (largest * largest)
    top = (column == largest).astype(f32)
    ties = jnp.sum(top[0:1, :], axis=1, keepdims=True)
    dkernel = dkernel + dlargest * top / ties
    dscore = kernel * (dkernel - jnp.sum(dkernel * kernel, axis=1, keepdims=True))
    dquery = exact(dscore, two_ref[3])
    dkey = exact(dscore, two_ref[2], turned)
    unit = me_ref[0]
    width = dq_ref.shape[2]
    second = lax.rem(unit, 2 * heads) >= heads
    head = jnp.where(second, unit - heads, unit)
    place = (iota((HD, width), 1) == iota((HD, width), 0) + head * HD).astype(f32)
    live = unit < 2 * heads
    for out, value in ((dq_ref, dquery), (dk_ref, dkey)):
        wide = exact(jnp.where(live, value, 0.0), place)
        out[0] = jnp.where(second, 0.0, wide)
        out[1] = jnp.where(second, wide, 0.0)


def score3_kernel(heads, parts, k_ref, v_ref, got_ref, ql_ref, kl_ref, p_ref, out_ref, lands):
    tokens = k_ref.shape[0] // 2
    n = out_ref.shape[0]
    width = k_ref.shape[1]
    for d in range(n):
        got = got_ref[d].astype(f32)
        for i in range(4):
            lands[i, d * parts : (d + 1) * parts, :] = got[i * parts : (i + 1) * parts]
    for i, out in ((0, ql_ref), (2, kl_ref)):
        both = lands[i : i + 2]
        if n * parts != M:
            both = jnp.sum(both.reshape(2, M, n * parts // M, width), axis=2)
        out[...] = both.reshape(2 * M, width).astype(bf16)
    for u in range(2 * heads, n):
        out_ref[u] = jnp.zeros((HD, 128), bf16)
    lane = iota((HD, 128), 1)

    @pl.loop(0, 2)
    def _(s):
        for g in range(k_ref.shape[1] // GW):
            lanes = slice(g * GW, (g + 1) * GW)
            rows = aligned(s, tokens)
            land = block_diagonal(ql_ref[aligned(s, M), lanes])
            score = nt(land, k_ref[rows, lanes])
            top = jnp.max(score, axis=1, keepdims=True).astype(bf16).astype(f32)
            e = jnp.exp(score - top)
            total = jnp.sum(e, axis=1, keepdims=True)
            low = e.astype(bf16)
            p_ref[s, g] = low
            part = nn(low, v_ref[rows, lanes])
            for j in range(HP):
                span = slice(j * HD, (j + 1) * HD)
                t = total[span]
                t_high = t.astype(bf16).astype(f32)
                slot = jnp.where(lane < HD, low_lanes(diagonal_half(part, j), j), 0.0)
                slot = jnp.where(lane == HD, top[span], slot)
                slot = jnp.where(lane == HD + 1, t_high, slot)
                slot = jnp.where(lane == HD + 2, t - t_high, slot)
                out_ref[s * heads + g * HP + j] = slot.astype(bf16)


def combine_kernel(got_ref, inv_ref, out_ref, sum_ref):
    n = got_ref.shape[0]
    lane = iota((M, 128), 1)
    top = lax.fori_loop(
        1,
        n,
        lambda d, m: jnp.maximum(m, got_ref[d].astype(f32)),
        got_ref[0].astype(f32),
    )[:, HD : HD + 1]

    def add(d, acc):
        slot = got_ref[d].astype(f32)
        return acc + jnp.exp(slot[:, HD : HD + 1] - top) * slot

    acc = lax.fori_loop(0, n, add, jnp.zeros((M, 128), f32))
    total = acc[:, HD + 1 : HD + 2] + acc[:, HD + 2 : HD + 3]
    total = jnp.where(total > 0.0, total, 1.0)
    summary = jnp.where(lane < HD, acc / total, 0.0)
    sum_ref[...] = summary
    mixed = exact(inv_ref[...], summary)
    high = total.astype(bf16).astype(f32)
    slot = jnp.where(lane < HD, mixed, 0.0)
    slot = jnp.where(lane == HD, top, slot)
    slot = jnp.where(lane == HD + 1, high, slot)
    slot = jnp.where(lane == HD + 2, total - high, slot)
    slot = slot.astype(bf16)
    for d in range(n):
        out_ref[d] = slot


def fill_extended(ext, ref, low_ref, high_ref, tokens):
    for s in range(2):
        ext[s, 0:REACH, :] = low_ref[s]
        ext[s, REACH : REACH + tokens, :] = ref[s * tokens : (s + 1) * tokens, :]
        ext[s, REACH + tokens : 2 * REACH + tokens, :] = high_ref[s]


def convolve(ext, toep_ref, s, g, tile):
    piece = ext[s, tile * CT : tile * CT + CE, g * GW : (g + 1) * GW]
    lane = iota((CT, GW), 1) // HD
    out = nn(toep_ref[g * HP], piece)
    for j in range(1, HP):
        out = jnp.where(lane == j, nn(toep_ref[g * HP + j], piece), out)
    return out


def softmax1(land, queries):
    tokens = queries.shape[0]
    score = nt(land, queries).reshape(HP, M, tokens)
    e = jnp.exp(score - jnp.max(score, axis=1, keepdims=True))
    return (e / jnp.sum(e, axis=1, keepdims=True)).reshape(GW, tokens)


def attend_kernel(
    heads, q_ref, v_ref, low_ref, high_ref, kl_ref, mixed_ref, toep_ref, out_ref, mbd_ref, ext
):
    tokens = q_ref.shape[0] // 2
    fill_extended(ext, v_ref, low_ref, high_ref, tokens)

    @pl.loop(0, 2)
    def _(s):
        for g in range(q_ref.shape[1] // GW):
            lanes = slice(g * GW, (g + 1) * GW)
            rows = aligned(s, tokens)
            land = block_diagonal(kl_ref[aligned(s, M), lanes])
            k1 = softmax1(land, q_ref[rows, lanes]).astype(bf16)
            mbd = block_from_slots(lambda j: mixed_ref[s * heads + g * HP + j].astype(f32))
            mbd_ref[s, g] = mbd
            attended = tn(k1, mbd)
            for tile in range(tokens // CT):
                span = slice(tile * CT, (tile + 1) * CT)
                both = attended[span] + convolve(ext, toep_ref, s, g, tile)
                at = pl.ds(pl.multiple_of(s * tokens + tile * CT, CT), CT)
                out_ref[at, lanes] = both.astype(bf16)


def norm(h):
    center = h - jnp.mean(h, axis=1, keepdims=True)
    rstd = lax.rsqrt(jnp.mean(center * center, axis=1, keepdims=True) + EPS)
    return center * rstd, rstd


def norm_back(dx, hat, rstd):
    return rstd * (
        dx - jnp.mean(dx, axis=1, keepdims=True) - hat * jnp.mean(dx * hat, axis=1, keepdims=True)
    )


RT = 64


def row_tiles(total, body):
    def step(i, c):
        body(pl.ds(pl.multiple_of(i * RT, RT), RT))
        return c

    lax.fori_loop(0, total // RT, step, 0, unroll=2)


def ffn_kernel(chunks, heads_ref, x_ref, gain_ref, cot_ref, *refs):
    weights, refs = refs[:-14], refs[-14:]
    act_ref, du_ref, n1b_ref, out_ref, dd_ref, db_ref, dh1_ref, dheads_ref, gn_ref = refs[:9]
    hat1, rstd1, down, n1, dh2 = refs[9:]
    total, width = x_ref.shape

    if len(weights) == 1:
        (all_ref,) = weights
        per = all_ref.shape[0] // chunks

        def w_up(c):
            return all_ref[:, chunks + c].reshape(width, width)

        def w_down(c):
            return all_ref[pl.ds(c * per, per), 0:chunks].reshape(width, width)

        def w_out():
            return all_ref[:, 2 * chunks].reshape(width, width)

    else:
        wo_ref, wu_ref, wd_ref = weights
        w_up = lambda c: wu_ref[c]
        w_down = lambda c: wd_ref[c]
        w_out = lambda: wo_ref[...]
    g1 = gain_ref[6:7, :]
    g2 = gain_ref[7:8, :]
    gn_ref[...] = jnp.zeros_like(gn_ref)
    down[...] = nn(heads_ref[...], w_out())

    def first(r):
        hat, rstd = norm(x_ref[r, :].astype(f32) + down[r, :])
        hat1[r, :] = hat
        rstd1[r, :] = jnp.broadcast_to(rstd, (RT, 128))
        value = hat * g1
        n1[r, :] = value
        n1b_ref[r, :] = value.astype(bf16)
        down[r, :] = jnp.zeros((RT, width), f32)

    row_tiles(total, first)

    @pl.loop(0, chunks)
    def _(c):
        up = nn(n1b_ref[...], w_up(c))
        cdf = 0.5 * (1.0 + lax.erf(up * (0.5**0.5)))
        density = jnp.exp(-0.5 * up * up) * 0.3989422804014327
        act = (up * cdf).astype(bf16)
        act_ref[c] = act
        du_ref[c] = (cdf + up * density).astype(bf16)
        down[...] += nn(act, w_down(c))

    def second(r):
        hat, rstd = norm(n1[r, :] + down[r, :])
        out_ref[r, :] = (hat * g2).astype(bf16)
        g = cot_ref[r, :].astype(f32)
        gn_ref[1:2, :] += jnp.sum(g * hat, axis=0, keepdims=True)
        d = norm_back(g * g2, hat, rstd)
        dh2[r, :] = d
        dd_ref[r, :] = d.astype(bf16)

    row_tiles(total, second)

    @pl.loop(0, chunks)
    def _(c):
        part = (nt(dd_ref[...], w_down(c)) * du_ref[c].astype(f32)).astype(bf16)
        du_ref[c] = part
        dh2[...] += nt(part, w_up(c))

    def third(r):
        hat = hat1[r, :]
        d = dh2[r, :]
        gn_ref[0:1, :] += jnp.sum(d * hat, axis=0, keepdims=True)
        d = norm_back(d * g1, hat, rstd1[r, :][:, 0:1])
        dh1_ref[r, :] = d
        db_ref[r, :] = d.astype(bf16)

    row_tiles(total, third)
    dheads_ref[...] = nt(db_ref[...], w_out()).astype(bf16)


def ffn_grads_kernel(cfg, me_ref, act_ref, du_ref, n1b_ref, dd_ref, heads_ref, db_ref, *refs):
    n, core, hyper, rows, chunks = cfg
    outs, acc = refs[:-1], refs[-1]
    per = n // chunks

    @pl.loop(0, chunks)
    def _(c):
        acc[...] = tn(act_ref[c], dd_ref[...])
        if hyper:
            part = acc[...].astype(bf16).reshape(per, chunks * rows, acc.shape[1])
            outs[0][pl.ds(c * per, per), chunks * rows : 2 * chunks * rows, :] = part
        else:
            outs[1][c] = acc[...]

    for c in range(chunks):
        acc[...] = tn(n1b_ref[...], du_ref[c])
        if hyper:
            part = acc[...].astype(bf16).reshape(n, rows, acc.shape[1])
            outs[0][:, c * rows : (c + 1) * rows, :] = part
        else:
            outs[0][:, c * acc.shape[1] : (c + 1) * acc.shape[1]] = acc[...]
    acc[...] = tn(heads_ref[...], db_ref[...])
    if hyper:
        emit(acc, 0, rows, rows, outs[1], outs[2], 0, me_ref[0], n, core, 2)
    else:
        outs[2][...] = acc[...]


def attend_back_kernel(heads, dh_ref, mbd_ref, kl_ref, q_ref, dq_ref, dkl_ref, out_ref):
    tokens = q_ref.shape[0] // 2
    n = out_ref.shape[0]
    for u in range(2 * heads, n):
        out_ref[u] = jnp.zeros((HD, 128), bf16)
    lane = iota((HD, 128), 1)
    mask = block_mask()

    @pl.loop(0, 2)
    def _(s):
        for g in range(q_ref.shape[1] // GW):
            lanes = slice(g * GW, (g + 1) * GW)
            rows = aligned(s, tokens)
            dh = dh_ref[rows, lanes]
            land = block_diagonal(kl_ref[aligned(s, M), lanes])
            k1 = softmax1(land, q_ref[rows, lanes])
            low = k1.astype(bf16)
            dk1 = nt(mbd_ref[s, g], dh)
            row = jnp.sum((k1 * dk1).reshape(HP, M, tokens), axis=1, keepdims=True)
            centered = (dk1.reshape(HP, M, tokens) - row).reshape(GW, tokens)
            ds = (k1 * centered).astype(bf16)
            dq_ref[rows, lanes] = tn(ds, land)
            dland = jnp.where(mask, nn(ds, q_ref[rows, lanes]), 0.0)
            dkl_ref[s, :, lanes] = jnp.sum(dland.reshape(HP, M, GW), axis=0)
            dmixed = nn(low, dh)
            for j in range(HP):
                part = low_lanes(diagonal_half(dmixed, j), j)
                rest = part - part.astype(bf16).astype(f32)
                slot = jnp.where(lane < HD, part, pltpu.roll(rest, HD, 1))
                out_ref[s * heads + g * HP + j] = slot.astype(bf16)


def conv_back_kernel(
    dh_ref, dlow_ref, dhigh_ref, v_ref, low_ref, high_ref, peot_ref, dv_ref, gc_ref, dext, ext, gram
):
    tokens = v_ref.shape[0] // 2
    groups = v_ref.shape[1] // GW
    fill_extended(dext, dh_ref, dlow_ref, dhigh_ref, tokens)
    fill_extended(ext, v_ref, low_ref, high_ref, tokens)
    lane = iota((CT, GW), 1) // HD
    gc_ref[...] = jnp.zeros_like(gc_ref)
    back = (iota((CT, CT), 0) + iota((CT, CT), 1) == CT - 1).astype(f32)
    for g in range(groups):
        lanes = slice(g * GW, (g + 1) * GW)
        gram[...] = jnp.zeros_like(gram)

        @pl.loop(0, 2)
        def _(s):
            for tile in range(tokens // CT):
                at = pl.ds(pl.multiple_of(s * tokens + tile * CT, CT), CT)
                dv_ref[at, lanes] = convolve(dext, peot_ref, s, g, tile)
                dh = dh_ref[at, lanes]
                each = jnp.concatenate(
                    [jnp.where(lane == j, dh, jnp.zeros_like(dh)) for j in range(HP)], axis=0
                )
                gram[:, 0:CE] += nt(each, ext[s, tile * CT : tile * CT + CE, lanes])
        for j in range(HP):
            turned = exact(back, gram[j * CT : (j + 1) * CT, :])
            rolled = pltpu.roll(turned, 0, 1, stride=1, stride_axis=0)
            gc_ref[g * HP + j : g * HP + j + 1, :] = jnp.sum(rolled, axis=0, keepdims=True)


def owner_back_kernel(got_ref, inv_ref, sum_ref, out_ref, dinv_ref):
    n = got_ref.shape[0]
    lane = iota((M, 128), 1)
    acc = lax.fori_loop(
        0, n, lambda d, a: a + got_ref[d].astype(f32), jnp.zeros((M, 128), f32)
    )
    dmixed = jnp.where(lane < HD, acc + pltpu.roll(acc, HD, 1), 0.0)
    dinv_ref[...] = exact(dmixed, sum_ref[...], ((1,), (1,)))
    dsum = exact(inv_ref[...], dmixed, ((0,), (0,))).astype(bf16).astype(f32)
    row = jnp.sum(dsum * sum_ref[...], axis=1, keepdims=True)
    high = row.astype(bf16).astype(f32)
    slot = jnp.where(lane < HD, dsum, 0.0)
    slot = jnp.where(lane == HD, high, slot)
    slot = jnp.where(lane == HD + 1, row - high, slot)
    slot = slot.astype(bf16)
    for d in range(n):
        out_ref[d] = slot


def score3_back_kernel(
    heads, parts, sent_ref, stat_ref, dsum_ref, p_ref, k_ref, v_ref, ql_ref, dvc_ref, dq2_ref, dk2_ref,
    dk1_ref, dk_ref, dv_ref, out_ref, dql,
):
    tokens = k_ref.shape[0] // 2
    n = out_ref.shape[0]
    mask = block_mask()

    @pl.loop(0, 2)
    def _(s):
        for g in range(k_ref.shape[1] // GW):
            lanes = slice(g * GW, (g + 1) * GW)
            rows = aligned(s, tokens)
            factors, terms = [], []
            for j in range(HP):
                u = s * heads + g * HP + j
                local = sent_ref[u].astype(f32)[:, HD : HD + 1]
                stat = stat_ref[u].astype(f32)
                total = stat[:, HD + 1 : HD + 2] + stat[:, HD + 2 : HD + 3]
                factors.append(jnp.exp(local - stat[:, HD : HD + 1]) / total)
                d = dsum_ref[u].astype(f32)
                terms.append(d[:, HD : HD + 1] + d[:, HD + 1 : HD + 2])
            k3 = p_ref[s, g].astype(f32) * jnp.concatenate(factors, axis=0)
            dbd = block_from_slots(lambda j: dsum_ref[s * heads + g * HP + j].astype(f32))
            dk3 = nt(dbd, v_ref[rows, lanes])
            ds = (k3 * (dk3 - jnp.concatenate(terms, axis=0))).astype(bf16)
            dland = jnp.where(mask, nn(ds, k_ref[rows, lanes]), 0.0)
            dql[s, :, lanes] = jnp.sum(dland.reshape(HP, M, GW), axis=0) + dq2_ref[s, :, lanes]
            land = block_diagonal(ql_ref[aligned(s, M), lanes])
            dk_ref[rows, lanes] = tn(ds, land)
            dv_ref[rows, lanes] = (dvc_ref[rows, lanes] + tn(k3.astype(bf16), dbd)).astype(bf16)
    for d in range(n):
        first = d * parts * M // (n * parts)
        span = slice(first, first + parts)
        pieces = [dql[0, span, :], dql[1, span, :]]
        pieces += [dk2_ref[s, span, :] + dk1_ref[s, span, :] for s in range(2)]
        if parts < 2:
            pieces.append(jnp.zeros((8 - 4 * parts, dql.shape[2]), f32))
        out_ref[d] = jnp.concatenate(pieces, axis=0).astype(bf16)


def final_kernel(
    cfg, me_ref, got_ref, x_ref, dq1_ref, dk3_ref, dv_ref, dh1_ref, wq, wk, wv, small_ref, *refs
):
    n, core, hyper, rows, parts, scale, segment = cfg
    outs = refs[:-3]
    dq, dk, acc = refs[-3:]
    dx_ref = outs[0]
    grads = outs[1:]
    me = me_ref[0]
    tokens = x_ref.shape[0] // 2
    land = lax.fori_loop(
        0, n, lambda d, a: a + got_ref[d].astype(f32), jnp.zeros((8, x_ref.shape[1]), f32)
    )
    land = land * (1.0 / segment)
    each = tokens // parts
    for s in range(2):
        for l in range(parts):
            span = slice(s * tokens + l * each, s * tokens + (l + 1) * each)
            at = s * parts + l
            dq[span, :] = (dq1_ref[span, :] + land[at : at + 1, :]).astype(bf16)
            at = (2 + s) * parts + l
            dk[span, :] = (dk3_ref[span, :] + land[at : at + 1, :]).astype(bf16)
    both = nt(dq[...], wq[...]) + nt(dk[...], wk[...])
    dx_ref[...] = (dh1_ref[...] + scale * both + nt(dv_ref[...], wv[...])).astype(bf16)
    for turn, (ref, factor) in enumerate(((dq, scale), (dk, scale), (dv_ref, 1.0))):
        acc[...] = tn(x_ref[...], ref[...]) * factor
        if hyper:
            keep, send = grads[2 * turn : 2 * turn + 2]
            emit(acc, 0, rows, rows, keep, send, 0, me, n, core, turn)
        else:
            grads[turn][...] = acc[...]
    if hyper:
        mine = me & 1
        span = slice(rows, rows + 8)

        def step(i, c):
            slot = scatter_slot(jnp.bitwise_xor(me - mine, 2 * i), n, core, 0)
            grads[0][slot, span, 0:GW] = small_ref[2 * i + mine]
            grads[1][slot, span, 0:GW] = small_ref[2 * i + 1 - mine]
            return c

        lax.fori_loop(0, n // 2, step, 0)


def merge_kernel(counts, last, *refs):
    outs = refs[2 * sum(counts) :]
    at = 0
    for job, count in enumerate(counts):
        ins = refs[2 * at : 2 * (at + count)]
        at += count
        row = 0
        for keep, got in zip(ins[0::2], ins[1::2]):
            span = slice(row, row + keep.shape[1])
            row += keep.shape[1]
            if last:
                outs[job][0, span] = keep[0].astype(f32) + got[0].astype(f32)
                continue
            half = keep.shape[0] // 2
            kept, sent = outs[2 * job], outs[2 * job + 1]

            @pl.loop(0, half)
            def _(j):
                kept[j, span] = keep[j].astype(f32) + got[j].astype(f32)
                sent[j, span] = (
                    keep[half + j].astype(f32) + got[half + j].astype(f32)
                ).astype(bf16)


def exchange(x):
    return lax.all_to_all(x, AX, 0, 0, tiled=True)


def per_device(
    tokens, w_query, w_key, w_value, w_out, conv_kernel, norm1_gain, w_up, w_down, norm2_gain, cotangent
):
    sequences, held, width = tokens.shape
    blk, head = lax.axis_size("blk"), lax.axis_size("head")
    n = blk * head
    heads_dev = conv_kernel.shape[0]
    heads = heads_dev * head
    rows = w_query.shape[0]
    hidden = w_up.shape[1]
    chunks = hidden // width
    segment = held * n // M
    parts = max(1, held // segment)
    groups = width // GW
    hyper = rows % 8 == 0 and n == 32
    core = 0 if n <= 32 else head.bit_length() - 1
    scale = HD**-0.25
    total = sequences * held
    me = (lax.axis_index("blk") * head + lax.axis_index("head")).astype(jnp.int32)
    me = me.reshape(1)
    x = tokens.reshape(total, width)

    taps = jnp.concatenate([conv_kernel, conv_kernel[:, ::-1]], axis=0)
    extras = jnp.concatenate(
        [
            jnp.pad(taps, ((0, 0), (0, width - KW))),
            jnp.pad(jnp.stack([norm1_gain, norm2_gain]), ((0, 0), (0, width - rows))),
        ],
        axis=0,
    )
    if hyper:
        pieces = cube_gather(
            jnp.concatenate([w_query, w_key, w_value, extras], axis=0), n, core
        )
        up_parts = [w_up[:, k * width : (k + 1) * width] for k in range(chunks)]
        later = jnp.concatenate([w_down] + up_parts + [w_out], axis=0)
        later, _ = lax.optimization_barrier((later, pieces))
        later = lax.all_gather(later, AX, axis=0).reshape(n, 2 * chunks + 1, rows, width)
        weights = (later,)
    else:
        pieces = [
            lax.all_gather(w, AX, axis=0, tiled=True) for w in (w_query, w_key, w_value)
        ] + [lax.all_gather(extras, AX, axis=0)]
        wo = lax.all_gather(w_out, AX, axis=0, tiled=True)
        wu = lax.all_gather(w_up, AX, axis=0, tiled=True)
        wu = wu.reshape(width, chunks, width).transpose(1, 0, 2)
        wd = lax.all_gather(w_down, AX, axis=0, tiled=True).reshape(chunks, width, width)
        weights = (wo, wu, wd)

    cfg = (n, core, hyper, rows, parts, scale, segment, heads_dev, head)
    square_low = shape_of((total, width), bf16)
    square_full = shape_of((total, width), f32)
    weight = shape_of((width, width), bf16)
    toeplitz = shape_of((heads, CT, CE), bf16)
    queries, keys, values, lands, toep, peot, gains, wq, wk, wv = vmem_call(
        functools.partial(qkv_kernel, cfg),
        (
            square_low, square_low, square_low,
            shape_of((n, 8, width), bf16 if held >= segment else f32),
            toeplitz, toeplitz, shape_of((8, width), f32), weight, weight, weight,
        ),
        (me, x, *pieces),
        scalars=1,
    )
    lands = exchange(lands)
    ahead = [(i, i + 1) for i in range(n - 1)]
    behind = [(i + 1, i) for i in range(n - 1)]

    def halo(y):
        y = y.reshape(sequences, held, width)
        low = lax.ppermute(y[:, held - REACH :], AX, ahead)
        high = lax.ppermute(y[:, :REACH], AX, behind)
        return low, high

    v_low, v_high = halo(values)
    matrix = shape_of((M, M), f32)
    slots = shape_of((n, M, 128), bf16)
    land = shape_of((2 * M, width), bf16)
    q_land, k_land, p3, sent = vmem_call(
        functools.partial(score3_kernel, heads, parts),
        (land, land, shape_of((2, groups, GW, held), bf16), slots),
        (keys, values, lands),
        scratch=[pltpu.VMEM((4, n * parts, width), f32)],
    )
    got_sums = exchange(sent)
    inverse, newton_keep, kernel_two = vmem_call(
        functools.partial(newton_kernel, heads),
        (matrix, shape_of((NEWTON, 5, M, M), f32), shape_of((4, M, M), f32)),
        (me, q_land, k_land),
        scalars=1,
    )
    stat, summary = vmem_call(
        combine_kernel, (slots, shape_of((M, 128), f32)), (got_sums, inverse)
    )
    stat = exchange(stat)
    heads_out, mbd = vmem_call(
        functools.partial(attend_kernel, heads),
        (square_low, shape_of((2, groups, GW, GW), bf16)),
        (queries, values, v_low, v_high, k_land, stat, toep),
        scratch=[pltpu.VMEM((2, held + 2 * REACH, width), bf16)],
    )
    wide = shape_of((chunks, total, width), bf16)
    act, d_upper, n1b, layer_out, d_down, d_branch, d_h1, d_heads, gain_sums = vmem_call(
        functools.partial(ffn_kernel, chunks),
        (
            wide, wide, square_low, square_low, square_low, square_low, square_full, square_low,
            shape_of((8, width), f32),
        ),
        (heads_out, x, gains, cotangent.reshape(total, width), *weights),
        scratch=[
            pltpu.VMEM((total, width), f32),
            pltpu.VMEM((total, 128), f32),
            pltpu.VMEM((total, width), f32),
            pltpu.VMEM((total, width), f32),
            pltpu.VMEM((total, width), f32),
        ],
        limit=48,
    )
    d_low, d_high = halo(d_heads)
    spread = shape_of((2, M, width), f32)
    d_q1, d_kl1, sent_back = vmem_call(
        functools.partial(attend_back_kernel, heads),
        (square_full, spread, slots),
        (d_heads, mbd, k_land, queries),
    )
    got_back = exchange(sent_back)
    if hyper:
        grad_shapes = [shape_of((n, 2 * chunks * rows, width), bf16)]
        grad_shapes += [shape_of((n // 2, rows, width), bf16)] * 2
    else:
        grad_shapes = [shape_of((width, hidden), f32), shape_of((chunks, width, width), f32)]
    else_shapes = [] if hyper else [shape_of((width, width), f32)]
    grads = vmem_call(
        functools.partial(ffn_grads_kernel, (n, core, hyper, rows, chunks)),
        grad_shapes + else_shapes,
        (me, act, d_upper, n1b, d_down, heads_out, d_branch),
        scalars=1,
        scratch=[pltpu.VMEM((width, width), f32)],
    )
    got_back, grads = lax.optimization_barrier((got_back, grads))
    d_sum, d_inverse = vmem_call(
        owner_back_kernel, (slots, matrix), (got_back, inverse, summary)
    )
    d_sum = exchange(d_sum)
    extended = pltpu.VMEM((2, held + 2 * REACH, width), bf16)
    d_vc, conv_sums = vmem_call(
        conv_back_kernel,
        (square_full, shape_of((heads + (-heads) % 8, GW), f32)),
        (d_heads, d_low, d_high, values, v_low, v_high, peot),
        scratch=[extended, extended, pltpu.VMEM((HP * CT, GW), f32)],
    )
    d_ql2, d_kl2 = vmem_call(
        functools.partial(newton_back_kernel, heads),
        (spread, spread),
        (me, d_inverse, inverse, newton_keep, kernel_two),
        scalars=1,
    )
    d_k3, d_values, sent_land = vmem_call(
        functools.partial(score3_back_kernel, heads, parts),
        (square_full, square_low, shape_of((n, 8, width), bf16)),
        (sent, stat, d_sum, p3, keys, values, q_land, d_vc, d_ql2, d_kl2, d_kl1),
        scratch=[pltpu.VMEM((2, M, width), f32)],
    )
    got_land = exchange(sent_land)
    if hyper:
        early = lax.psum_scatter(grads[0], AX, scatter_dimension=0, tiled=False)
    small = gain_sums[0:2].reshape(2, n, rows).transpose(1, 0, 2).reshape(n, 2 * rows)
    tap_sums = conv_sums[:heads, CT - 1 : CT - 1 + KW].reshape(head, heads_dev * KW)
    tap_sums = jnp.broadcast_to(tap_sums[None], (blk, head, heads_dev * KW)).reshape(n, -1)
    small = jnp.concatenate([small, tap_sums], axis=1)
    small = jnp.pad(small, ((0, 0), (0, GW - small.shape[1])))
    if hyper:
        final_shapes = [
            shape_of((n // 2, rows + extra, width), bf16) for extra in (8, 0, 0) for _ in range(2)
        ]
    else:
        final_shapes = [shape_of((width, width), f32)] * 3
    outs = vmem_call(
        functools.partial(final_kernel, (n, core, hyper, rows, parts, scale, segment)),
        [square_low] + final_shapes,
        (
            me, got_land, x, d_q1, d_k3, d_values, d_h1, wq, wk, wv,
            jnp.broadcast_to(small[:, None], (n, 8, GW)).astype(bf16),
        ),
        scalars=1,
        scratch=[pltpu.VMEM((total, width), bf16)] * 2 + [pltpu.VMEM((width, width), f32)],
        limit=20,
    )
    d_tokens = outs[0].reshape(tokens.shape)
    projections = outs[1:]
    if hyper:
        shares = cube_scatter(
            [
                [(projections[0], projections[1])],
                [(projections[2], projections[3])],
                [(projections[4], projections[5]), (grads[1], grads[2])],
            ],
            n,
            core,
        )
        grad_query, small = shares[0][:rows], shares[0][rows]
        grad_key = shares[0][rows + 8 :]
        grad_value, grad_out = shares[1][:rows], shares[1][rows:]
        early = early.astype(f32)
        grad_up = early[: chunks * rows].reshape(chunks, rows, width).transpose(1, 0, 2)
        grad_up = grad_up.reshape(rows, hidden)
        grad_down = early[chunks * rows :]
    else:

        def scatter(g):
            return lax.psum_scatter(g, AX, scatter_dimension=0, tiled=True)

        grad_up, grad_out = scatter(grads[0]), scatter(grads[2])
        grad_down = scatter(grads[1].reshape(hidden, width))
        grad_query, grad_key, grad_value = (scatter(g) for g in projections)
        small = scatter(small)[0]
    return (
        layer_out.reshape(tokens.shape),
        d_tokens,
        grad_query,
        grad_key,
        grad_value,
        grad_out,
        small[2 * rows : 2 * rows + heads_dev * KW].reshape(heads_dev, KW),
        small[:rows],
        grad_up,
        grad_down,
        small[rows : 2 * rows],
    )


def solution(mesh):
    lined = P(None, AX, None)
    rowed = P(AX, None)
    gain = P(AX)
    taps = P("head", None)
    in_specs = (lined, rowed, rowed, rowed, rowed, taps, gain, rowed, rowed, gain, lined)
    out_specs = (lined, lined, rowed, rowed, rowed, rowed, taps, gain, rowed, rowed, gain)
    return jax.shard_map(
        per_device, mesh=mesh, in_specs=in_specs, out_specs=out_specs, check_vma=False
    )
```

```python
import functools

import jax
import jax.numpy as jnp
from jax import lax
from jax.experimental import pallas as pl
from jax.experimental.pallas import tpu as pltpu
from jax.sharding import PartitionSpec as P

HD = 64
M = 64
KW = 33
NEWTON = 6
REACH = KW // 2
AX = ("blk", "head")
EPS = 1e-05
GW = 256
HP = GW // HD
CT = 128
CE = CT + 2 * REACH

bf16 = jnp.bfloat16
f32 = jnp.float32
HIGHEST = lax.Precision.HIGHEST


def nn(a, b):
    return lax.dot_general(a, b, (((1,), (0,)), ((), ())), preferred_element_type=f32)


def nt(a, b):
    return lax.dot_general(a, b, (((1,), (1,)), ((), ())), preferred_element_type=f32)


def tn(a, b):
    return lax.dot_general(a, b, (((0,), (0,)), ((), ())), preferred_element_type=f32)


def exact(a, b, dims=((1,), (0,))):
    return lax.dot_general(a, b, (dims, ((), ())), preferred_element_type=f32, precision=HIGHEST)


def iota(shape, dim):
    return lax.broadcasted_iota(jnp.int32, shape, dim)


class Fetched:
    def __init__(self, source, buf, sems, parts):
        self.buf, self.shape, self.dtype = buf, buf.shape, buf.dtype
        self.copies = [
            pltpu.make_async_copy(source.at[part], buf.at[part], sem)
            for part, sem in zip(parts, sems)
        ]
        self.waiting = list(range(len(parts)))
        for copy in self.copies:
            copy.start()

    def ready(self, *which):
        for i in which or tuple(self.waiting):
            if i in self.waiting:
                self.copies[i].wait()
                self.waiting.remove(i)

    def __getitem__(self, index):
        self.ready()
        return self.buf[index]


class Stored:
    def __init__(self, target, buf, sems, parts):
        self.buf, self.shape, self.dtype = buf, buf.shape, buf.dtype
        self.copies = [
            pltpu.make_async_copy(buf.at[part], target.at[part], sem)
            for part, sem in zip(parts, sems)
        ]
        self.left = list(range(len(parts)))

    def done(self, *which):
        for i in which or tuple(self.left):
            if i in self.left:
                self.copies[i].start()
                self.left.remove(i)

    def __getitem__(self, index):
        return self.buf[index]

    def __setitem__(self, index, value):
        self.buf[index] = value


def ready(*refs):
    for ref in refs:
        if isinstance(ref, Fetched):
            ref.ready()


def done(*refs):
    for ref in refs:
        if isinstance(ref, Stored):
            ref.done()


def resident_call(kernel, outs, args):
    vmem = pl.BlockSpec(memory_space=pltpu.VMEM)
    return pl.pallas_call(
        kernel,
        out_shape=outs,
        in_specs=[vmem] * len(args),
        out_specs=jax.tree.map(lambda _: vmem, outs),
        compiler_params=pltpu.CompilerParams(vmem_limit_bytes=8 << 20),
    )(*args)


def vmem_call(kernel, outs, args, scalars=0, scratch=(), parts=None, out_parts=None):
    parts, out_parts = parts or {}, out_parts or {}
    arrays = args[scalars:]
    whole = [(slice(None),)]
    pieces = [parts.get(i, whole) for i in range(len(arrays))]
    results = jax.tree.leaves(outs)
    buffers = [pltpu.VMEM(a.shape, a.dtype) for a in [*arrays, *results]]
    out_pieces = [out_parts.get(i, whole) for i in range(len(results))]
    semaphores = pltpu.SemaphoreType.DMA((sum(len(p) for p in pieces + out_pieces),))

    def run(*refs):
        refs = list(refs)
        take = lambda k: [refs.pop(0) for _ in range(k)]
        ins, sources, targets = take(scalars), take(len(arrays)), take(len(results))
        kept, in_bufs, out_bufs = take(len(scratch)), take(len(arrays)), take(len(results))
        (sems,) = refs
        free = iter(range(sum(len(p) for p in pieces + out_pieces)))
        own = lambda piece: [sems.at[next(free)] for _ in piece]
        for source, buf, piece in zip(sources, in_bufs, pieces):
            ins.append(Fetched(source, buf, own(piece), piece))
        stored = [
            Stored(target, buf, own(piece), piece)
            for target, buf, piece in zip(targets, out_bufs, out_pieces)
        ]
        kernel(*ins, *stored, *kept)
        ready(*ins)
        done(*stored)
        for ref in stored:
            for copy in ref.copies:
                copy.wait()

    hbm = pl.BlockSpec(memory_space=pl.ANY)
    return pl.pallas_call(
        run,
        out_shape=outs,
        in_specs=[pl.BlockSpec(memory_space=pltpu.SMEM)] * scalars + [hbm] * len(arrays),
        out_specs=jax.tree.map(lambda _: hbm, outs),
        scratch_shapes=list(scratch) + buffers + [semaphores],
        compiler_params=pltpu.CompilerParams(vmem_limit_bytes=60 << 20),
    )(*args)


def shape_of(dims, dtype):
    return jax.ShapeDtypeStruct(tuple(dims), dtype)


def cube_masks(n):
    masks = [1 << b for b in range(n.bit_length() - 1)]
    if len(masks) >= 2:
        masks[-1] |= masks[-2]
    return masks


def coefficients(v, n):
    bits = [(v >> b) & 1 for b in range(n.bit_length() - 1)]
    if len(bits) >= 2:
        bits[-2] = bits[-2] ^ bits[-1]
    return bits


def scatter_order(n, core, turn):
    rest = [b for b in range(n.bit_length() - 1) if b != core]
    return (rest, [rest[1], rest[0], *rest[2:]], [*rest[2:], *rest[:2]])[turn]


def gather_order(n, core, turn):
    return list(reversed(scatter_order(n, core, turn)))


def swap(x, n, dim):
    mask = cube_masks(n)[dim]
    return lax.ppermute(x, AX, [(i, i ^ mask) for i in range(n)])


def gather_slot(v, n, core, turn):
    bits = coefficients(v, n)
    slot = 0
    for place, dim in enumerate(gather_order(n, core, turn)):
        slot = slot + (bits[dim] << place)
    return slot


def scatter_slot(v, n, core, turn):
    bits = coefficients(v, n)
    slot = 0
    for place, dim in enumerate(reversed(scatter_order(n, core, turn))):
        slot = slot + (bits[dim] << place)
    return slot


def cube_gather(piece, n, core):
    buf = piece[None]
    first, second = gather_order(n, core, 0), gather_order(n, core, 1)
    for dim in first[:-2]:
        buf = jnp.concatenate([buf, swap(buf, n, dim)], axis=0)
    half = piece.shape[1] // 2
    mid = buf
    bufs = [buf[:, :, :half], buf[:, :, half:]]
    for dims in zip(first[-2:], second[-2:]):
        got = [swap(x, n, dim) for x, dim in zip(bufs, dims)]
        bufs = [jnp.concatenate(pair, axis=0) for pair in zip(bufs, got)]
    return bufs + [swap(x, n, core) for x in bufs], mid


def merged(jobs, call):
    shapes = []
    for pairs in jobs:
        slots = pairs[0][0].shape[0]
        joint = (sum(k.shape[1] for k, _ in pairs), pairs[0][0].shape[2])
        shapes += [shape_of((slots // 2,) + joint, t) for t in (f32, bf16)]
    args = [x for pairs in jobs for pair in pairs for x in pair]
    kernel = functools.partial(merge_kernel, [len(pairs) for pairs in jobs])
    outs = call(kernel, shapes, args)
    return list(zip(outs[0::2], outs[1::2]))


def cube_scatter(jobs, splits, n, core):
    orders = [[core, *scatter_order(n, core, turn)] for turn in range(len(jobs))]
    jobs = [[(k, swap(s, n, core)) for k, s in job] for job in jobs]
    for step in range(1, len(orders[0])):
        state = merged(jobs, vmem_call if step == 1 else resident_call)
        if step == 3:
            orders = orders[:1] + orders[2:]
        jobs = [[(k, swap(s, n, o[step]))] for (k, s), o in zip(state, orders)]
        if step == 2:
            jobs = [jobs[0] + jobs[1]] + jobs[2:]
    width = jobs[0][0][0].shape[2]
    shapes = [shape_of((count, width), f32) for split in splits for count in split]
    args = [x for pairs in jobs for pair in pairs for x in pair]
    return resident_call(functools.partial(last_kernel, splits), shapes, args)


def emit(acc, first_row, rows, stride, keep, send, rows_at, me, n, core, turn, count=None, first=0):
    count = n if count is None else count
    mine = me & 1
    span = slice(rows_at, rows_at + rows)

    def step(i, c):
        d = 2 * i
        slot = scatter_slot(jnp.bitwise_xor(me - mine, first + d), n, core, turn)
        low = pl.multiple_of(first_row + (d + mine) * stride, 8)
        high = pl.multiple_of(first_row + (d + 1 - mine) * stride, 8)
        keep[slot, span, :] = acc[pl.ds(low, rows), :].astype(bf16)
        send[slot, span, :] = acc[pl.ds(high, rows), :].astype(bf16)
        return c

    lax.fori_loop(0, count // 2, step, 0)


def aligned(i, size):
    return pl.ds(pl.multiple_of(i * size, size), size)


def block_mask():
    return (iota((GW, GW), 0) // HD) == (iota((GW, GW), 1) // HD)


def block_diagonal(x):
    wide = jnp.concatenate([x] * HP, axis=0)
    return jnp.where(block_mask(), wide, jnp.zeros_like(wide))


def diagonal_half(x, j):
    return x[j * HD : (j + 1) * HD, 128 * (j // 2) : 128 * (j // 2) + 128]


def low_lanes(x, j):
    return pltpu.roll(x, HD, 1) if j % 2 else x


def high_lanes(x, j):
    return x if j % 2 else pltpu.roll(x, HD, 1)


SLOT = HD // 2 + 8


def packed(x):
    half = HD // 2
    lane = iota((half, 128), 1)
    return jnp.where(lane < HD, x[0:half], pltpu.roll(x[half:HD], HD, 1))


def unpacked(x):
    half = HD // 2
    both = jnp.concatenate([x[0:half], pltpu.roll(x[0:half], HD, 1)], axis=0)
    return jnp.where(iota((HD, 128), 1) < HD, both, 0.0)


def stacked(rows, height=8):
    rows = list(rows) + [jnp.zeros_like(rows[0])] * (height - len(rows))
    return jnp.concatenate(rows, axis=0)


def identity(size):
    return (iota((size, size), 0) == iota((size, size), 1)).astype(bf16)


def block_from_slots(read):
    rows = []
    for j in range(HP):
        half = unpacked(read(j).astype(f32))
        if j % 2:
            half = pltpu.roll(half, HD, 1)
        zero = jnp.zeros_like(half)
        rows.append(jnp.concatenate([half, zero] if j < 2 else [zero, half], axis=1))
    return jnp.concatenate(rows, axis=0).astype(bf16)


def prepare_kernel(chunks, taps_ref, gains_ref, wq, wk, wv, wo, wu, wd, now_ref, later_ref, ext):
    rows, width = wq.shape
    heads_dev, reach = taps_ref.shape
    ext[...] = jnp.zeros_like(ext)
    ext[0:heads_dev, 0:reach] = taps_ref[...].astype(f32)
    back = (iota((128, 128), 0) + iota((128, 128), 1) == KW - 1).astype(bf16)
    turned = nn(ext[...].astype(bf16), back)
    ext[heads_dev : 2 * heads_dev, :] = turned[0:heads_dev]
    ext[6:8, 0:rows] = gains_ref[...].astype(f32)
    for i, w in enumerate((wq, wk, wv)):
        now_ref[i * rows : (i + 1) * rows, :] = w[...]
    now_ref[3 * rows : 3 * rows + 8, 0:128] = ext[...].astype(bf16)
    now_ref[3 * rows : 3 * rows + 8, 128:] = jnp.zeros((8, width - 128), bf16)
    done(now_ref)
    later_ref[0 : chunks * rows, :] = wd[...]
    for k in range(chunks):
        at = (chunks + k) * rows
        later_ref[at : at + rows, :] = wu[:, k * width : (k + 1) * width]
    later_ref[2 * chunks * rows : (2 * chunks + 1) * rows, :] = wo[...]


def piece_pair(ins, turn, pair, span, lanes, me, n, core):
    mine = me & 1
    slot = gather_slot(jnp.bitwise_xor(me - mine, 2 * pair), n, core, turn)
    own = ins[turn][slot, span, lanes]
    other = ins[2 + turn][slot, span, lanes]
    return jnp.where(mine == 0, own, other), jnp.where(mine == 0, other, own)


def natural(ins, units, me, n, core, rows, width):
    half = width // 2

    def place_rows(pair, c):
        to = pl.ds(pl.multiple_of(2 * rows * pair, 16), 2 * rows)
        for turn in range(2):
            for unit, out in units:
                span = slice(unit * rows, (unit + 1) * rows)
                both = piece_pair(ins, turn, pair, span, slice(None), me, n, core)
                out[to, turn * half : (turn + 1) * half] = jnp.concatenate(both, axis=0)
        return c

    lax.fori_loop(0, n // 2, place_rows, 0)


def query_key_kernel(cfg, me_ref, x_ref, *refs):
    n, core, hyper, rows, parts, scale, segment, heads_dev, head_size = cfg
    ins, refs = refs[:4], refs[4:]
    q_ref, k_ref, land_ref, wq, wk = refs
    me = me_ref[0]
    width = x_ref.shape[1]
    ready(*ins)
    if hyper:
        natural(ins, ((0, wq), (1, wk)), me, n, core, rows, width)
    else:
        for out, piece in zip((wq, wk), ins):
            out[...] = piece[...]
    done(wq, wk)
    q_ref[...] = (nn(x_ref[...], wq[...]) * scale).astype(bf16)
    done(q_ref)
    k_ref[...] = (nn(x_ref[...], wk[...]) * scale).astype(bf16)
    done(k_ref)
    pieces = []
    each = x_ref.shape[0] // (2 * parts)
    for ref in (q_ref, k_ref):
        for at_row in range(2 * parts):
            span = ref[at_row * each : (at_row + 1) * each, :].astype(f32)
            pieces.append(jnp.sum(span, axis=0, keepdims=True) * (1.0 / segment))
    if parts < 2:
        pieces.append(jnp.zeros((8 - 4 * parts, width), f32))
    shared = jnp.concatenate(pieces, axis=0).astype(land_ref.dtype)
    for d in range(n):
        land_ref[d] = shared


def value_kernel(cfg, me_ref, x_ref, *refs):
    n, core, hyper, rows, parts, scale, segment, heads_dev, head_size = cfg
    ins, refs = refs[:4], refs[4:]
    v_ref, toep_ref, peot_ref, gain_ref, wv = refs
    me = me_ref[0]
    width = x_ref.shape[1]
    ready(*ins)
    if hyper:
        natural(ins, ((2, wv),), me, n, core, rows, width)

        def small_rows(d):
            span = slice(3 * rows, 3 * rows + 8)
            return piece_pair(ins, 0, d // 2, span, slice(0, GW), me, n, core)[d % 2]

    else:
        wv[...] = ins[2][...]

        def small_rows(d):
            return ins[3][d, :, 0:GW]

    done(wv)
    v_ref[...] = nn(x_ref[...], wv[...]).astype(bf16)
    done(v_ref)
    place = (iota((128, width), 1) % rows == iota((128, width), 0)).astype(bf16)
    gains = jnp.zeros(gain_ref.shape, f32)
    for d in range(n):
        small = small_rows(d)
        inside = iota((8, width), 1) // rows == d
        gains = gains + jnp.where(inside, nn(small[:, 0:128], place), 0.0)
        if d < head_size:
            taps = small.astype(f32)
            for i in range(heads_dev):
                for row, out in ((i, toep_ref), (heads_dev + i, peot_ref)):
                    spread = jnp.broadcast_to(taps[row : row + 1, :], (CT, GW))
                    spread = pltpu.roll(spread, 0, 1, stride=1, stride_axis=0)
                    out[d * heads_dev + i] = spread[:, 0:CE].astype(bf16)
    gain_ref[...] = gains


def newton_kernel(heads, me_ref, ql_ref, kl_ref, inv_ref, keep_ref, two_ref):
    unit = lax.rem(me_ref[0], 2 * heads)
    second = unit >= heads
    head = jnp.where(second, unit - heads, unit)
    width = ql_ref.shape[1]
    pick = (iota((width, HD), 0) == iota((width, HD), 1) + head * HD).astype(bf16)

    def mine(ref):
        rows = jnp.where(second, ref[M : 2 * M, :].astype(f32), ref[0:M, :].astype(f32))
        return nn(rows.astype(bf16), pick).astype(bf16)

    query, key = mine(ql_ref), mine(kl_ref)
    score = nt(query, key)
    e = jnp.exp(score - jnp.max(score, axis=1, keepdims=True))
    kernel = e / jnp.sum(e, axis=1, keepdims=True)
    column = jnp.sum(kernel, axis=0, keepdims=True)
    largest = jnp.max(column, axis=1, keepdims=True)
    eye = (iota((M, M), 0) == iota((M, M), 1)).astype(f32)
    z = kernel.T / largest
    two_ref[0] = kernel
    two_ref[1] = column + jnp.zeros_like(kernel)
    two_ref[2] = query.astype(f32)
    two_ref[3] = key.astype(f32)
    for step in range(NEWTON):
        p = exact(kernel, z)
        a = 7.0 * eye - p
        b = 15.0 * eye - exact(p, a)
        c = 13.0 * eye - exact(p, b)
        keep_ref[step, 0] = z
        keep_ref[step, 1] = p
        keep_ref[step, 2] = a
        keep_ref[step, 3] = b
        keep_ref[step, 4] = c
        z = 0.25 * exact(z, c)
    inv_ref[...] = z


def newton_back_kernel(
    heads, me_ref, dinv_ref, inv_ref, keep_ref, two_ref, dq_ref, dk_ref
):
    turned = ((0,), (0,))
    across = ((1,), (1,))
    ready(keep_ref)
    kernel = two_ref[0]
    dz = dinv_ref[...]
    dkernel = jnp.zeros_like(kernel)
    for step in reversed(range(NEWTON)):
        z, p, a, b, c = (keep_ref[step, i] for i in range(5))
        dc = 0.25 * exact(z, dz, turned)
        db = -exact(p, dc, turned)
        da = -exact(p, db, turned)
        dp = -exact(dc, b, across) - exact(db, a, across) - da
        dkernel = dkernel + exact(dp, z, across)
        dz = 0.25 * exact(dz, c, across) + exact(kernel, dp, turned)
    column = two_ref[1]
    largest = jnp.max(column[0:1, :], axis=1, keepdims=True)
    dkernel = dkernel + dz.T / largest
    dlargest = -jnp.sum(dz * kernel.T, keepdims=True) / (largest * largest)
    top = (column == largest).astype(f32)
    ties = jnp.sum(top[0:1, :], axis=1, keepdims=True)
    dkernel = dkernel + dlargest * top / ties
    dscore = kernel * (dkernel - jnp.sum(dkernel * kernel, axis=1, keepdims=True))
    dquery = exact(dscore, two_ref[3])
    dkey = exact(dscore, two_ref[2], turned)
    unit = me_ref[0]
    width = dq_ref.shape[2]
    second = lax.rem(unit, 2 * heads) >= heads
    head = jnp.where(second, unit - heads, unit)
    place = (iota((HD, width), 1) == iota((HD, width), 0) + head * HD).astype(f32)
    live = unit < 2 * heads
    for out, value in ((dq_ref, dquery), (dk_ref, dkey)):
        wide = exact(jnp.where(live, value, 0.0), place)
        out[0] = jnp.where(second, 0.0, wide)
        out[1] = jnp.where(second, wide, 0.0)


def score3_kernel(heads, parts, k_ref, v_ref, got_ref, ql_ref, kl_ref, p_ref, out_ref, lands):
    tokens = k_ref.shape[0] // 2
    n = out_ref.shape[0]
    width = k_ref.shape[1]
    ready(got_ref)
    for d in range(n):
        got = got_ref[d].astype(f32)
        for i in range(4):
            lands[i, d * parts : (d + 1) * parts, :] = got[i * parts : (i + 1) * parts]
    for i, out in ((0, ql_ref), (2, kl_ref)):
        both = lands[i : i + 2]
        if n * parts != M:
            both = jnp.sum(both.reshape(2, M, n * parts // M, width), axis=2)
        out[...] = both.reshape(2 * M, width).astype(bf16)
    for u in range(2 * heads, n):
        out_ref[u] = jnp.zeros((SLOT, 128), bf16)
    ready(k_ref, v_ref)
    done(ql_ref, kl_ref)

    @pl.loop(0, 2)
    def _(s):
        for g in range(k_ref.shape[1] // GW):
            lanes = slice(g * GW, (g + 1) * GW)
            rows = aligned(s, tokens)
            land = block_diagonal(ql_ref[aligned(s, M), lanes])
            score = nt(land, k_ref[rows, lanes])
            top = jnp.max(score, axis=1, keepdims=True).astype(bf16).astype(f32)
            e = jnp.exp(score - top)
            total = jnp.sum(e, axis=1, keepdims=True)
            low = e.astype(bf16)
            p_ref[s, g] = low
            part = nn(low, v_ref[rows, lanes])
            high = total.astype(bf16).astype(f32)
            which = iota((GW, 8), 1)
            stats = jnp.where(which == 0, top, 0.0)
            stats = jnp.where(which == 1, high, stats)
            stats = jnp.where(which == 2, total - high, stats).astype(bf16)
            stats = tn(stats, identity(GW))
            for j in range(HP):
                slot = packed(low_lanes(diagonal_half(part, j), j))
                stat = low_lanes(stats[:, 128 * (j // 2) : 128 * (j // 2) + 128], j)
                slot = jnp.concatenate([slot, stat], axis=0)
                out_ref[s * heads + g * HP + j] = slot.astype(bf16)


def combine_kernel(got_ref, inv_ref, out_ref, sum_ref):
    n = got_ref.shape[0]
    half = HD // 2
    ready(got_ref)
    tops = jnp.concatenate([got_ref[d, half : half + 8].astype(f32)[0:1] for d in range(n)], axis=0)
    top = jnp.max(tops, axis=0, keepdims=True)
    weights = jnp.exp(tops - top)
    sums = []
    for d in range(n):
        stat = got_ref[d, half : half + 8].astype(f32)
        sums.append(stat[1:2] + stat[2:3])
    total = jnp.sum(weights * jnp.concatenate(sums, axis=0), axis=0, keepdims=True)
    total = jnp.where(total > 0.0, total, 1.0)
    weights = (weights / total).T
    lane = iota((half, 128), 1)
    acc = jnp.zeros((half, 128), f32)
    for d in range(n):
        by = weights[:, d : d + 1]
        by = jnp.where(lane < HD, by[0:half], by[half:HD])
        acc = acc + by * got_ref[d, 0:half].astype(f32)
    summary = unpacked(acc)
    sum_ref[...] = summary
    mixed = exact(inv_ref[...], summary)
    high = total.astype(bf16).astype(f32)
    slot = jnp.concatenate([packed(mixed), stacked([top, high, total - high])], axis=0)
    slot = slot.astype(bf16)
    for d in range(n):
        out_ref[d] = slot


def fill_extended(ext, ref, low_ref, high_ref, tokens):
    for s in range(2):
        ext[s, 0:REACH, :] = low_ref[s]
        ext[s, REACH : REACH + tokens, :] = ref[s * tokens : (s + 1) * tokens, :]
        ext[s, REACH + tokens : 2 * REACH + tokens, :] = high_ref[s]


def convolve(ext, toep_ref, s, g, tile):
    piece = ext[s, tile * CT : tile * CT + CE, g * GW : (g + 1) * GW]
    lane = iota((CT, GW), 1) // HD
    out = nn(toep_ref[g * HP], piece)
    for j in range(1, HP):
        out = jnp.where(lane == j, nn(toep_ref[g * HP + j], piece), out)
    return out


def softmax1(land, queries):
    tokens = queries.shape[0]
    score = nt(land, queries).reshape(HP, M, tokens)
    e = jnp.exp(score - jnp.max(score, axis=1, keepdims=True))
    return (e / jnp.sum(e, axis=1, keepdims=True)).reshape(GW, tokens)


def kernel1_kernel(q_ref, v_ref, low_ref, high_ref, kl_ref, toep_ref, conv_ref, k1_ref, ext):
    tokens = q_ref.shape[0] // 2
    fill_extended(ext, v_ref, low_ref, high_ref, tokens)
    ready(q_ref, kl_ref, toep_ref)

    @pl.loop(0, 2)
    def _(s):
        for g in range(q_ref.shape[1] // GW):
            lanes = slice(g * GW, (g + 1) * GW)
            rows = aligned(s, tokens)
            land = block_diagonal(kl_ref[aligned(s, M), lanes])
            k1_ref[s, g] = softmax1(land, q_ref[rows, lanes]).astype(bf16)
            for tile in range(tokens // CT):
                at = pl.ds(pl.multiple_of(s * tokens + tile * CT, CT), CT)
                conv_ref[at, lanes] = convolve(ext, toep_ref, s, g, tile)


def attend_kernel(heads, k1_ref, conv_ref, mixed_ref, out_ref, mbd_ref):
    tokens = conv_ref.shape[0] // 2
    ready(k1_ref, conv_ref, mixed_ref)

    @pl.loop(0, 2)
    def _(s):
        for g in range(conv_ref.shape[1] // GW):
            lanes = slice(g * GW, (g + 1) * GW)
            rows = aligned(s, tokens)
            mbd = block_from_slots(lambda j: mixed_ref[s * heads + g * HP + j, 0 : HD // 2])
            mbd_ref[s, g] = mbd
            both = tn(k1_ref[s, g], mbd) + conv_ref[rows, lanes]
            out_ref[rows, lanes] = both.astype(bf16)


def norm(h):
    center = h - jnp.mean(h, axis=1, keepdims=True)
    rstd = lax.rsqrt(jnp.mean(center * center, axis=1, keepdims=True) + EPS)
    return center * rstd, rstd


def norm_back(dx, hat, rstd):
    return rstd * (
        dx - jnp.mean(dx, axis=1, keepdims=True) - hat * jnp.mean(dx * hat, axis=1, keepdims=True)
    )


RT = 64


def row_tiles(total, body):
    def step(i, c):
        body(pl.ds(pl.multiple_of(i * RT, RT), RT))
        return c

    lax.fori_loop(0, total // RT, step, 0, unroll=2)


def ffn_kernel(chunks, heads_ref, x_ref, gain_ref, cot_ref, *refs):
    weights, refs = refs[:-13], refs[-13:]
    act_ref, du_ref, n1b_ref, out_ref, dd_ref, db_ref, dh1_ref, dheads_ref, gn_ref = refs[:9]
    hat1, rstd1, down, dh2 = refs[9:]
    total, width = x_ref.shape

    if len(weights) == 1:
        (fetched,) = weights
        all_ref = fetched.buf
        per = all_ref.shape[0] // chunks

        def w_up(c):
            return all_ref[:, chunks + c].reshape(width, width)

        def w_down(c):
            return all_ref[pl.ds(c * per, per), 0:chunks].reshape(width, width)

        def w_out():
            return all_ref[:, 2 * chunks].reshape(width, width)

        out_ready, up_ready, down_ready = (functools.partial(fetched.ready, i) for i in range(3))
    else:
        wo_ref, wu_ref, wd_ref = weights
        w_up = lambda c: wu_ref[c]
        w_down = lambda c: wd_ref[c]
        w_out = lambda: wo_ref[...]
        out_ready, up_ready, down_ready = (functools.partial(ready, w) for w in weights)
    ready(gain_ref)
    g1 = gain_ref[6:7, :]
    g2 = gain_ref[7:8, :]
    gn_ref[...] = jnp.zeros_like(gn_ref)
    out_ready()
    ready(x_ref)
    down[...] = nn(heads_ref[...], w_out())

    def first(r):
        hat, rstd = norm(x_ref[r, :].astype(f32) + down[r, :])
        hat1[r, :] = hat
        rstd1[r, :] = jnp.broadcast_to(rstd, (RT, 128))
        value = hat * g1
        n1b_ref[r, :] = value.astype(bf16)
        down[r, :] = value

    row_tiles(total, first)
    done(n1b_ref)
    up_ready()
    down_ready()
    ready(cot_ref)

    @pl.loop(0, chunks)
    def _(c):
        up = nn(n1b_ref[...], w_up(c))
        cdf = 0.5 * (1.0 + lax.erf(up * (0.5**0.5)))
        density = jnp.exp(-0.5 * up * up) * 0.3989422804014327
        act = (up * cdf).astype(bf16)
        act_ref[c] = act
        du_ref[c] = (cdf + up * density).astype(bf16)
        down[...] += nn(act, w_down(c))

    done(act_ref)

    def second(r):
        hat, rstd = norm(down[r, :])
        out_ref[r, :] = (hat * g2).astype(bf16)
        g = cot_ref[r, :].astype(f32)
        gn_ref[1:2, :] += jnp.sum(g * hat, axis=0, keepdims=True)
        d = norm_back(g * g2, hat, rstd)
        dh2[r, :] = d
        dd_ref[r, :] = d.astype(bf16)

    row_tiles(total, second)
    done(out_ref, dd_ref)

    @pl.loop(0, chunks)
    def _(c):
        part = (nt(dd_ref[...], w_down(c)) * du_ref[c].astype(f32)).astype(bf16)
        du_ref[c] = part
        dh2[...] += nt(part, w_up(c))

    done(du_ref)

    def third(r):
        hat = hat1[r, :]
        d = dh2[r, :]
        gn_ref[0:1, :] += jnp.sum(d * hat, axis=0, keepdims=True)
        d = norm_back(d * g1, hat, rstd1[r, :][:, 0:1])
        dh1_ref[r, :] = d
        db_ref[r, :] = d.astype(bf16)

    row_tiles(total, third)
    done(dh1_ref, db_ref, gn_ref)
    dheads_ref[...] = nt(db_ref[...], w_out()).astype(bf16)


def ffn_grads_kernel(cfg, me_ref, act_ref, dd_ref, n1b_ref, du_ref, heads_ref, db_ref, *refs):
    n, core, hyper, rows, chunks = cfg
    outs, acc = refs[:-1], refs[-1]
    per = n // chunks
    width = acc.shape[1]
    ready(act_ref, dd_ref)

    @pl.loop(0, chunks)
    def _(c):
        acc[...] = tn(act_ref[c], dd_ref[...])
        if hyper:
            part = acc[...].astype(bf16).reshape(per, chunks, rows, width)
            outs[0][pl.ds(c * per, per), chunks : 2 * chunks] = part
        else:
            outs[1][c] = acc[...]

    if hyper:
        outs[0].done(0)
    ready(n1b_ref, du_ref)

    @pl.loop(0, chunks)
    def _(c):
        acc[...] = tn(n1b_ref[...], du_ref[c])
        if hyper:
            outs[0][:, c] = acc[...].astype(bf16).reshape(n, rows, width)
        else:
            outs[0][c] = acc[...]

    if hyper:
        outs[0].done(1)
    acc[...] = tn(heads_ref[...], db_ref[...])
    if hyper:
        outs[0][:, 2 * chunks] = acc[...].astype(bf16).reshape(n, rows, width)
    else:
        outs[2][...] = acc[...]


def attend_back_kernel(heads, dh_ref, k1_ref, mbd_ref, kl_ref, q_ref, dq_ref, dkl_ref, out_ref):
    tokens = q_ref.shape[0] // 2
    n = out_ref.shape[0]
    for u in range(2 * heads, n):
        out_ref[u] = jnp.zeros((HD // 2, 128), bf16)
    mask = block_mask()
    ready(dh_ref, k1_ref, mbd_ref, kl_ref, q_ref)

    @pl.loop(0, 2)
    def _(s):
        for g in range(q_ref.shape[1] // GW):
            lanes = slice(g * GW, (g + 1) * GW)
            rows = aligned(s, tokens)
            dh = dh_ref[rows, lanes]
            land = block_diagonal(kl_ref[aligned(s, M), lanes])
            low = k1_ref[s, g]
            k1 = low.astype(f32)
            dk1 = nt(mbd_ref[s, g], dh)
            row = jnp.sum((k1 * dk1).reshape(HP, M, tokens), axis=1, keepdims=True)
            centered = (dk1.reshape(HP, M, tokens) - row).reshape(GW, tokens)
            ds = (k1 * centered).astype(bf16)
            dq_ref[rows, lanes] = tn(ds, land)
            dland = jnp.where(mask, nn(ds, q_ref[rows, lanes]), 0.0)
            dkl_ref[s, :, lanes] = jnp.sum(dland.reshape(HP, M, GW), axis=0)
            dmixed = nn(low, dh)
            for j in range(HP):
                slot = packed(low_lanes(diagonal_half(dmixed, j), j))
                out_ref[s * heads + g * HP + j] = slot.astype(bf16)


def conv_back_kernel(
    dh_ref, dlow_ref, dhigh_ref, v_ref, low_ref, high_ref, peot_ref, dv_ref, gc_ref, dext, ext, gram
):
    tokens = v_ref.shape[0] // 2
    groups = v_ref.shape[1] // GW
    fill_extended(dext, dh_ref, dlow_ref, dhigh_ref, tokens)
    fill_extended(ext, v_ref, low_ref, high_ref, tokens)
    ready(peot_ref)
    lane = iota((CT, GW), 1) // HD
    ready(dh_ref)
    gc_ref[...] = jnp.zeros_like(gc_ref)
    back = (iota((CT, CT), 0) + iota((CT, CT), 1) == CT - 1).astype(f32)
    for g in range(groups):
        lanes = slice(g * GW, (g + 1) * GW)
        gram[...] = jnp.zeros_like(gram)

        @pl.loop(0, 2)
        def _(s):
            for tile in range(tokens // CT):
                at = pl.ds(pl.multiple_of(s * tokens + tile * CT, CT), CT)
                dv_ref[at, lanes] = convolve(dext, peot_ref, s, g, tile)
                dh = dh_ref[at, lanes]
                each = jnp.concatenate(
                    [jnp.where(lane == j, dh, jnp.zeros_like(dh)) for j in range(HP)], axis=0
                )
                gram[:, 0:CE] += nt(each, ext[s, tile * CT : tile * CT + CE, lanes])
        for j in range(HP):
            turned = exact(back, gram[j * CT : (j + 1) * CT, :])
            rolled = pltpu.roll(turned, 0, 1, stride=1, stride_axis=0)
            gc_ref[g * HP + j : g * HP + j + 1, :] = jnp.sum(rolled, axis=0, keepdims=True)


def owner_back_kernel(got_ref, inv_ref, sum_ref, out_ref, dinv_ref):
    n = got_ref.shape[0]
    ready(got_ref)
    dmixed = unpacked(
        lax.fori_loop(
            0, n, lambda d, a: a + got_ref[d].astype(f32), jnp.zeros((HD // 2, 128), f32)
        )
    )
    dsum = exact(inv_ref[...], dmixed, ((0,), (0,))).astype(bf16).astype(f32)
    ones = jnp.ones((8, 128), f32)
    row = exact(ones, dsum * sum_ref[...], ((1,), (1,)))[0:1]
    row = jnp.concatenate([row, jnp.zeros_like(row)], axis=1)
    high = row.astype(bf16).astype(f32)
    slot = jnp.concatenate([packed(dsum), stacked([high, row - high])], axis=0).astype(bf16)
    for d in range(n):
        out_ref[d] = slot
    done(out_ref)
    dinv_ref[...] = exact(dmixed, sum_ref[...], ((1,), (1,)))


def score3_back_kernel(
    heads, parts, sent_ref, stat_ref, dsum_ref, p_ref, k_ref, v_ref, ql_ref, dq2_ref, dk2_ref,
    dk1_ref, dk_ref, dv_ref, out_ref, dql,
):
    tokens = k_ref.shape[0] // 2
    n = out_ref.shape[0]
    mask = block_mask()
    ready(sent_ref, stat_ref, dsum_ref, p_ref, k_ref, v_ref, ql_ref, dq2_ref)

    @pl.loop(0, 2)
    def _(s):
        for g in range(k_ref.shape[1] // GW):
            lanes = slice(g * GW, (g + 1) * GW)
            rows = aligned(s, tokens)
            factors, terms = [], []
            for j in range(HP):
                u = s * heads + g * HP + j
                stat_rows = slice(HD // 2, HD // 2 + 8)
                local = sent_ref[u, stat_rows].astype(f32)[0:1]
                stat = stat_ref[u, stat_rows].astype(f32)
                factors.append(jnp.exp(local - stat[0:1]) / (stat[1:2] + stat[2:3]))
                d = dsum_ref[u, stat_rows].astype(f32)
                terms.append(d[0:1] + d[1:2])

            def joined(parts):
                lane = iota((1, 128), 1)
                halves = [
                    jnp.where(lane < HD, parts[j], pltpu.roll(parts[j + 1], HD, 1))
                    for j in range(0, HP, 2)
                ]
                return jnp.concatenate(halves, axis=1)

            rows_in = []
            for value in (joined(factors), joined(terms)):
                for _ in range(3):
                    term = value.astype(bf16).astype(f32)
                    rows_in.append(term)
                    value = value - term
            columns = nt(identity(GW), stacked(rows_in).astype(bf16))
            factor = columns[:, 0:1] + columns[:, 1:2] + columns[:, 2:3]
            term = columns[:, 3:4] + columns[:, 4:5] + columns[:, 5:6]
            k3 = p_ref[s, g].astype(f32) * factor
            dbd = block_from_slots(lambda j: dsum_ref[s * heads + g * HP + j, 0 : HD // 2])
            dk3 = nt(dbd, v_ref[rows, lanes])
            ds = (k3 * (dk3 - term)).astype(bf16)
            dland = jnp.where(mask, nn(ds, k_ref[rows, lanes]), 0.0)
            dql[s, :, lanes] = jnp.sum(dland.reshape(HP, M, GW), axis=0) + dq2_ref[s, :, lanes]
            land = block_diagonal(ql_ref[aligned(s, M), lanes])
            dk_ref[rows, lanes] = tn(ds, land)
            dv_ref[rows, lanes] = tn(k3.astype(bf16), dbd)
    for d in range(n):
        first = d * parts * M // (n * parts)
        span = slice(first, first + parts)
        pieces = [dql[0, span, :], dql[1, span, :]]
        pieces += [dk2_ref[s, span, :] + dk1_ref[s, span, :] for s in range(2)]
        if parts < 2:
            pieces.append(jnp.zeros((8 - 4 * parts, dql.shape[2]), f32))
        out_ref[d] = jnp.concatenate(pieces, axis=0).astype(bf16)


def two_terms(x):
    high = x.astype(bf16)
    return high, (x - high.astype(f32)).astype(bf16)


def final_kernel(
    cfg, me_ref, x_ref, dv3_ref, dvc_ref, dk3_ref, dq1_ref, wv, wk, wq, dh1_ref, *refs
):
    n, core, hyper, rows, parts, scale, segment = cfg
    dx_ref, sums_ref, gq_ref, gk_ref = refs[:4]
    outs, acc = refs[4:-1], refs[-1]
    tokens = x_ref.shape[0] // 2
    each = tokens // parts
    dv = (dvc_ref[...] + dv3_ref[...]).astype(bf16)
    acc[...] = tn(x_ref[...], dv)
    if hyper:
        emit(acc, 0, rows, rows, outs[0], outs[1], 0, me_ref[0], n, core, 2)
    else:
        outs[0][...] = acc[...]
    done(*outs)
    for s in range(2):
        for l in range(parts):
            span = slice(s * tokens + l * each, s * tokens + (l + 1) * each)
            at = s * parts + l
            sums_ref[at : at + 1, :] = jnp.sum(
                x_ref[span, :].astype(f32), axis=0, keepdims=True
            )
    dk = dk3_ref[...].astype(bf16)
    gk_ref[...] = tn(x_ref[...], dk) * scale
    done(gk_ref, sums_ref)
    both = nt(dk, wk[...])
    dq = dq1_ref[...].astype(bf16)
    gq_ref[...] = tn(x_ref[...], dq) * scale
    done(gq_ref)
    both = both + nt(dq, wq[...])
    dx_ref[...] = dh1_ref[...] + nt(dv, wv[...]) + scale * both


def landmark_sums(got_ref, factor):
    ready(got_ref)
    n, _, width = got_ref.shape
    zero = jnp.zeros((8, width), f32)
    return factor * lax.fori_loop(0, n, lambda d, a: a + got_ref[d].astype(f32), zero)


def landmark_kernel(cfg, me_ref, got_ref, sums_ref, gq_ref, gk_ref, small_ref, *refs):
    n, core, hyper, rows, parts, scale, segment = cfg
    outs, acc = refs[:-1], refs[-1]
    me = me_ref[0]
    count = 2 * parts
    land = landmark_sums(got_ref, scale / segment)
    s_high, s_low = two_terms(sums_ref[0:count, :])
    left = jnp.concatenate([s_high, s_low, s_high], axis=0)
    for turn, (ref, base) in enumerate(((gq_ref, 0), (gk_ref, count))):
        high, low = two_terms(land[base : base + count, :])
        acc[...] = ref[...] + tn(left, jnp.concatenate([high, high, low], axis=0))
        if hyper:
            keep, send = outs[2 * turn : 2 * turn + 2]
            emit(acc, 0, rows, rows, keep, send, 0, me, n, core, turn)
        else:
            outs[turn][...] = acc[...]
    if hyper:
        ready(small_ref)
        mine = me & 1
        span = slice(rows, rows + 8)

        def step(i, c):
            slot = scatter_slot(jnp.bitwise_xor(me - mine, 2 * i), n, core, 0)
            outs[0][slot, span, 0:GW] = small_ref[2 * i + mine]
            outs[1][slot, span, 0:GW] = small_ref[2 * i + 1 - mine]
            return c

        lax.fori_loop(0, n // 2, step, 0)


def tokens_kernel(cfg, got_ref, wq, wk, dx_ref, out_ref):
    n, core, hyper, rows, parts, scale, segment = cfg
    tokens = dx_ref.shape[0] // 2
    each = tokens // parts
    count = 2 * parts
    land = landmark_sums(got_ref, scale / segment)
    change = 0.0
    for base, w in ((0, wq), (count, wk)):
        both = nt(jnp.concatenate(two_terms(land[base : base + count, :]), axis=0), w[...])
        change = change + both[0:count] + both[count : 2 * count]
    for s in range(2):
        for l in range(parts):
            span = slice(s * tokens + l * each, s * tokens + (l + 1) * each)
            at = s * parts + l
            out_ref[span, :] = (dx_ref[span, :] + change[at : at + 1, :]).astype(bf16)


def merge_kernel(counts, *refs):
    ready(*refs[: 2 * sum(counts)])
    outs = refs[2 * sum(counts) :]
    at = 0
    for job, count in enumerate(counts):
        ins = refs[2 * at : 2 * (at + count)]
        at += count
        row = 0
        kept, sent = outs[2 * job], outs[2 * job + 1]
        for keep, got in zip(ins[0::2], ins[1::2]):
            span = slice(row, row + keep.shape[1])
            row += keep.shape[1]
            half = keep.shape[0] // 2

            @pl.loop(0, half)
            def _(j):
                kept[j, span] = keep[j].astype(f32) + got[j].astype(f32)
                sent[j, span] = (
                    keep[half + j].astype(f32) + got[half + j].astype(f32)
                ).astype(bf16)

        done(sent)


def last_kernel(splits, *refs):
    ins, outs = refs[: 2 * len(splits)], list(refs[2 * len(splits) :])
    for i, split in enumerate(splits):
        keep, got = ins[2 * i], ins[2 * i + 1]
        row = 0
        for count in split:
            span = slice(row, row + count)
            outs.pop(0)[...] = keep[0, span].astype(f32) + got[0, span].astype(f32)
            row += count


def unpack_kernel(chunks, got_ref, up_ref, down_ref, out_ref):
    out_ref[...] = got_ref[2 * chunks].astype(f32)
    rows, width = got_ref.shape[1:]
    for c in range(chunks):
        up_ref[:, c * width : (c + 1) * width] = got_ref[c].astype(f32)
        down_ref[c * rows : (c + 1) * rows, :] = got_ref[chunks + c].astype(f32)


def exchange(x):
    return lax.all_to_all(x, AX, 0, 0, tiled=True)


def per_device(
    tokens, w_query, w_key, w_value, w_out, conv_kernel, norm1_gain, w_up, w_down, norm2_gain, cotangent
):
    sequences, held, width = tokens.shape
    blk, head = lax.axis_size("blk"), lax.axis_size("head")
    n = blk * head
    heads_dev = conv_kernel.shape[0]
    heads = heads_dev * head
    rows = w_query.shape[0]
    hidden = w_up.shape[1]
    chunks = hidden // width
    segment = held * n // M
    parts = max(1, held // segment)
    groups = width // GW
    hyper = rows % 8 == 0 and n == 32
    core = 0 if n <= 32 else head.bit_length() - 1
    scale = HD**-0.25
    total = sequences * held
    me = (lax.axis_index("blk") * head + lax.axis_index("head")).astype(jnp.int32)
    me = me.reshape(1)
    x = tokens.reshape(total, width)

    if hyper:
        now, later = vmem_call(
            functools.partial(prepare_kernel, chunks),
            (
                shape_of((3 * rows + 8, width), bf16),
                shape_of(((2 * chunks + 1) * rows, width), bf16),
            ),
            (
                conv_kernel, jnp.stack([norm1_gain, norm2_gain]),
                w_query, w_key, w_value, w_out, w_up, w_down,
            ),
            scratch=[pltpu.VMEM((8, 128), f32)],
        )
        pieces, mid = cube_gather(now, n, core)
        later, _ = lax.optimization_barrier((later, mid))
        later = lax.all_gather(later, AX, axis=0).reshape(n, 2 * chunks + 1, rows, width)
        weights = (later,)
        weight_parts = {
            4: [
                (slice(None), slice(2 * chunks, None)),
                (slice(None), slice(chunks, 2 * chunks)),
                (slice(None), slice(0, chunks)),
            ]
        }
    else:
        taps = jnp.concatenate([conv_kernel, conv_kernel[:, ::-1]], axis=0)
        both = jnp.stack([norm1_gain, norm2_gain])
        extras = jnp.concatenate(
            [
                jnp.pad(taps, ((0, 0), (0, width - KW))),
                jnp.pad(both, ((0, 0), (0, width - rows))),
            ],
            axis=0,
        )
        pieces = [
            lax.all_gather(w, AX, axis=0, tiled=True) for w in (w_query, w_key, w_value)
        ] + [lax.all_gather(extras, AX, axis=0)]
        wo = lax.all_gather(w_out, AX, axis=0, tiled=True)
        wu = lax.all_gather(w_up, AX, axis=0, tiled=True)
        wu = wu.reshape(width, chunks, width).transpose(1, 0, 2)
        wd = lax.all_gather(w_down, AX, axis=0, tiled=True).reshape(chunks, width, width)
        weights = (wo, wu, wd)
        weight_parts = None

    cfg = (n, core, hyper, rows, parts, scale, segment, heads_dev, head)
    square_low = shape_of((total, width), bf16)
    square_full = shape_of((total, width), f32)
    weight = shape_of((width, width), bf16)
    weight_full = shape_of((width, width), f32)
    toeplitz = shape_of((heads, CT, CE), bf16)
    queries, keys, lands, wq, wk = vmem_call(
        functools.partial(query_key_kernel, cfg),
        (
            square_low, square_low, shape_of((n, 8, width), bf16 if held >= segment else f32),
            weight, weight,
        ),
        (me, x, *pieces),
        scalars=1,
    )
    lands = exchange(lands)
    values, toep, peot, gains, wv = vmem_call(
        functools.partial(value_kernel, cfg),
        (square_low, toeplitz, toeplitz, shape_of((8, width), f32), weight),
        (me, x, *pieces),
        scalars=1,
    )
    lands, values = lax.optimization_barrier((lands, values))
    ahead = [(i, i + 1) for i in range(n - 1)]
    behind = [(i + 1, i) for i in range(n - 1)]

    def halo(y):
        y = y.reshape(sequences, held, width)
        low = lax.ppermute(y[:, held - REACH :], AX, ahead)
        high = lax.ppermute(y[:, :REACH], AX, behind)
        return low, high

    matrix = shape_of((M, M), f32)
    slots = shape_of((n, SLOT, 128), bf16)
    half_slots = shape_of((n, HD // 2, 128), bf16)
    land = shape_of((2 * M, width), bf16)
    q_land, k_land, p3, sent = vmem_call(
        functools.partial(score3_kernel, heads, parts),
        (land, land, shape_of((2, groups, GW, held), bf16), slots),
        (keys, values, lands),
        scratch=[pltpu.VMEM((4, n * parts, width), f32)],
    )
    got_sums = exchange(sent)
    inverse, newton_keep, kernel_two = vmem_call(
        functools.partial(newton_kernel, heads),
        (matrix, shape_of((NEWTON, 5, M, M), f32), shape_of((4, M, M), f32)),
        (me, q_land, k_land),
        scalars=1,
    )
    stat, summary = vmem_call(
        combine_kernel, (slots, shape_of((M, 128), f32)), (got_sums, inverse)
    )
    stat = exchange(stat)
    v_low, v_high = halo(values)
    convolved, k1 = vmem_call(
        kernel1_kernel,
        (square_full, shape_of((2, groups, GW, held), bf16)),
        (queries, values, v_low, v_high, k_land, toep),
        scratch=[pltpu.VMEM((2, held + 2 * REACH, width), bf16)],
    )
    stat, k1 = lax.optimization_barrier((stat, k1))
    heads_out, mbd = vmem_call(
        functools.partial(attend_kernel, heads),
        (square_low, shape_of((2, groups, GW, GW), bf16)),
        (k1, convolved, stat),
    )
    wide = shape_of((chunks, total, width), bf16)
    act, d_upper, n1b, layer_out, d_down, d_branch, d_h1, d_heads, gain_sums = vmem_call(
        functools.partial(ffn_kernel, chunks),
        (
            wide, wide, square_low, square_low, square_low, square_low, square_full, square_low,
            shape_of((8, width), f32),
        ),
        (heads_out, x, gains, cotangent.reshape(total, width), *weights),
        scratch=[
            pltpu.VMEM((total, width), f32),
            pltpu.VMEM((total, 128), f32),
            pltpu.VMEM((total, width), f32),
            pltpu.VMEM((total, width), f32),
        ],
        parts=weight_parts,
    )
    if hyper:
        grad_shapes = [shape_of((n, 2 * chunks + 1, rows, width), bf16)]
        units = (slice(chunks, 2 * chunks), slice(0, chunks), slice(2 * chunks, None))
        grad_parts = {0: [(slice(None), unit) for unit in units]}
    else:
        grad_shapes = [shape_of((chunks, width, width), f32)] * 2
        grad_parts = None
    else_shapes = [] if hyper else [weight_full]
    grads = vmem_call(
        functools.partial(ffn_grads_kernel, (n, core, hyper, rows, chunks)),
        grad_shapes + else_shapes,
        (me, act, d_down, n1b, d_upper, heads_out, d_branch),
        scalars=1,
        scratch=[pltpu.VMEM((width, width), f32)],
        out_parts=grad_parts,
    )
    d_heads, grads = lax.optimization_barrier((d_heads, grads))
    d_low, d_high = halo(d_heads)
    spread = shape_of((2, M, width), f32)
    d_q1, d_kl1, sent_back = vmem_call(
        functools.partial(attend_back_kernel, heads),
        (square_full, spread, half_slots),
        (d_heads, k1, mbd, k_land, queries),
    )
    got_back = exchange(sent_back)
    extended = pltpu.VMEM((2, held + 2 * REACH, width), bf16)
    d_vc, conv_sums = vmem_call(
        conv_back_kernel,
        (square_full, shape_of((heads + (-heads) % 8, GW), f32)),
        (d_heads, d_low, d_high, values, v_low, v_high, peot),
        scratch=[extended, extended, pltpu.VMEM((HP * CT, GW), f32)],
    )
    got_back, d_vc = lax.optimization_barrier((got_back, d_vc))
    d_sum, d_inverse = vmem_call(
        owner_back_kernel, (slots, matrix), (got_back, inverse, summary)
    )
    d_sum = exchange(d_sum)
    d_ql2, d_kl2 = vmem_call(
        functools.partial(newton_back_kernel, heads),
        (spread, spread),
        (me, d_inverse, inverse, newton_keep, kernel_two),
        scalars=1,
    )
    d_k3, d_v3, sent_land = vmem_call(
        functools.partial(score3_back_kernel, heads, parts),
        (square_full, square_full, shape_of((n, 8, width), bf16)),
        (sent, stat, d_sum, p3, keys, values, q_land, d_ql2, d_kl2, d_kl1),
        scratch=[pltpu.VMEM((2, M, width), f32)],
    )
    got_land = exchange(sent_land)
    if hyper:
        early = lax.psum_scatter(grads[0], AX, scatter_dimension=0, tiled=False)
    small = gain_sums[0:2].reshape(2, n, rows).transpose(1, 0, 2).reshape(n, 2 * rows)
    tap_sums = conv_sums[:heads, CT - 1 : CT - 1 + KW].reshape(head, heads_dev * KW)
    tap_sums = jnp.broadcast_to(tap_sums[None], (blk, head, heads_dev * KW)).reshape(n, -1)
    small = jnp.concatenate([small, tap_sums], axis=1)
    small = jnp.pad(small, ((0, 0), (0, GW - small.shape[1])))
    extra_rows = (8, 0, 0)
    if hyper:
        slot_shapes = [
            [shape_of((n // 2, rows + extra, width), bf16)] * 2 for extra in extra_rows
        ]
    else:
        slot_shapes = [[shape_of((width, width), f32)]] * 3
    final_cfg = (n, core, hyper, rows, parts, scale, segment)
    d_x, x_sums, g_query, g_key, *value_slots = vmem_call(
        functools.partial(final_kernel, final_cfg),
        [square_full, shape_of((8, width), f32)] + [shape_of((width, width), f32)] * 2 + slot_shapes[2],
        (me, x, d_v3, d_vc, d_k3, d_q1, wv, wk, wq, d_h1),
        scalars=1,
        scratch=[pltpu.VMEM((width, width), f32)],
    )
    projections = vmem_call(
        functools.partial(landmark_kernel, final_cfg),
        slot_shapes[0] + slot_shapes[1],
        (
            me, got_land, x_sums, g_query, g_key,
            jnp.broadcast_to(small[:, None], (n, 8, GW)).astype(bf16),
        ),
        scalars=1,
        scratch=[pltpu.VMEM((width, width), f32)],
    )
    projections = list(projections) + value_slots
    after, _ = lax.optimization_barrier((got_land, projections))
    d_tokens = vmem_call(
        functools.partial(tokens_kernel, final_cfg), square_low, (after, wq, wk, d_x)
    )
    d_tokens = d_tokens.reshape(tokens.shape)
    if hyper:
        grad_up, grad_down, grad_out = vmem_call(
            functools.partial(unpack_kernel, chunks),
            (
                shape_of((rows, hidden), f32), shape_of((chunks * rows, width), f32),
                shape_of((rows, width), f32),
            ),
            (early,),
        )
        grad_query, small, grad_key, grad_value = cube_scatter(
            [
                [(projections[0], projections[1])],
                [(projections[2], projections[3])],
                [(projections[4], projections[5])],
            ],
            ((rows, 8, rows), (rows,)),
            n,
            core,
        )
        small = small[0]
    else:

        def scatter(g):
            return lax.psum_scatter(g, AX, scatter_dimension=0, tiled=True)

        grad_out = scatter(grads[2])
        grad_up = scatter(grads[0].transpose(1, 0, 2).reshape(width, hidden))
        grad_down = scatter(grads[1].reshape(hidden, width))
        grad_query, grad_key, grad_value = (scatter(g) for g in projections)
        small = scatter(small)[0]
    return (
        layer_out.reshape(tokens.shape),
        d_tokens,
        grad_query,
        grad_key,
        grad_value,
        grad_out,
        small[2 * rows : 2 * rows + heads_dev * KW].reshape(heads_dev, KW),
        small[:rows],
        grad_up,
        grad_down,
        small[rows : 2 * rows],
    )


def solution(mesh):
    lined = P(None, AX, None)
    rowed = P(AX, None)
    gain = P(AX)
    taps = P("head", None)
    in_specs = (lined, rowed, rowed, rowed, rowed, taps, gain, rowed, rowed, gain, lined)
    out_specs = (lined, lined, rowed, rowed, rowed, rowed, taps, gain, rowed, rowed, gain)
    return jax.shard_map(
        per_device, mesh=mesh, in_specs=in_specs, out_specs=out_specs, check_vma=False
    )
```

```python
import functools

import jax
import jax.numpy as jnp
from jax import lax
from jax.experimental import pallas as pl
from jax.experimental.pallas import tpu as pltpu
from jax.sharding import PartitionSpec as P

HD = 64
M = 64
KW = 33
NEWTON = 6
REACH = KW // 2
AX = ("blk", "head")
EPS = 1e-05
GW = 256
HP = GW // HD
CT = 128
CE = CT + 2 * REACH

bf16 = jnp.bfloat16
f32 = jnp.float32
HIGHEST = lax.Precision.HIGHEST


def nn(a, b):
    return lax.dot_general(a, b, (((1,), (0,)), ((), ())), preferred_element_type=f32)


def nt(a, b):
    return lax.dot_general(a, b, (((1,), (1,)), ((), ())), preferred_element_type=f32)


def tn(a, b):
    return lax.dot_general(a, b, (((0,), (0,)), ((), ())), preferred_element_type=f32)


def exact(a, b, dims=((1,), (0,))):
    return lax.dot_general(a, b, (dims, ((), ())), preferred_element_type=f32, precision=HIGHEST)


def iota(shape, dim):
    return lax.broadcasted_iota(jnp.int32, shape, dim)


class Fetched:
    def __init__(self, source, buf, sems, parts):
        self.buf, self.shape, self.dtype = buf, buf.shape, buf.dtype
        self.copies = [
            pltpu.make_async_copy(source.at[part], buf.at[part], sem)
            for part, sem in zip(parts, sems)
        ]
        self.waiting = list(range(len(parts)))
        for copy in self.copies:
            copy.start()

    def ready(self, *which):
        for i in which or tuple(self.waiting):
            if i in self.waiting:
                self.copies[i].wait()
                self.waiting.remove(i)

    def __getitem__(self, index):
        self.ready()
        return self.buf[index]


class Stored:
    def __init__(self, target, buf, sems, parts):
        self.buf, self.shape, self.dtype = buf, buf.shape, buf.dtype
        self.copies = [
            pltpu.make_async_copy(buf.at[part], target.at[part], sem)
            for part, sem in zip(parts, sems)
        ]
        self.left = list(range(len(parts)))

    def done(self, *which):
        for i in which or tuple(self.left):
            if i in self.left:
                self.copies[i].start()
                self.left.remove(i)

    def __getitem__(self, index):
        return self.buf[index]

    def __setitem__(self, index, value):
        self.buf[index] = value


def ready(*refs):
    for ref in refs:
        if isinstance(ref, Fetched):
            ref.ready()


def done(*refs):
    for ref in refs:
        if isinstance(ref, Stored):
            ref.done()


def resident_call(kernel, outs, args):
    vmem = pl.BlockSpec(memory_space=pltpu.VMEM)
    return pl.pallas_call(
        kernel,
        out_shape=outs,
        in_specs=[vmem] * len(args),
        out_specs=jax.tree.map(lambda _: vmem, outs),
        compiler_params=pltpu.CompilerParams(vmem_limit_bytes=8 << 20),
    )(*args)


def vmem_call(kernel, outs, args, scalars=0, scratch=(), parts=None, out_parts=None, lent=None):
    lent = lent or {}
    parts, out_parts = parts or {}, out_parts or {}
    arrays = args[scalars:]
    whole = [(slice(None),)]
    pieces = [parts.get(i, whole) for i in range(len(arrays))]
    results = jax.tree.leaves(outs)
    own_results = [r for i, r in enumerate(results) if i not in lent]
    buffers = [pltpu.VMEM(a.shape, a.dtype) for a in [*arrays, *own_results]]
    out_pieces = [out_parts.get(i, whole) for i in range(len(results))]
    semaphores = pltpu.SemaphoreType.DMA((sum(len(p) for p in pieces + out_pieces),))

    def run(*refs):
        refs = list(refs)
        take = lambda k: [refs.pop(0) for _ in range(k)]
        ins, sources, targets = take(scalars), take(len(arrays)), take(len(results))
        kept, in_bufs, own_bufs = take(len(scratch)), take(len(arrays)), take(len(own_results))
        out_bufs = [
            in_bufs[lent[i]] if i in lent else own_bufs.pop(0) for i in range(len(results))
        ]
        (sems,) = refs
        free = iter(range(sum(len(p) for p in pieces + out_pieces)))
        own = lambda piece: [sems.at[next(free)] for _ in piece]
        for source, buf, piece in zip(sources, in_bufs, pieces):
            ins.append(Fetched(source, buf, own(piece), piece))
        stored = [
            Stored(target, buf, own(piece), piece)
            for target, buf, piece in zip(targets, out_bufs, out_pieces)
        ]
        kernel(*ins, *stored, *kept)
        ready(*ins)
        done(*stored)
        for ref in stored:
            for copy in ref.copies:
                copy.wait()

    hbm = pl.BlockSpec(memory_space=pl.ANY)
    return pl.pallas_call(
        run,
        out_shape=outs,
        in_specs=[pl.BlockSpec(memory_space=pltpu.SMEM)] * scalars + [hbm] * len(arrays),
        out_specs=jax.tree.map(lambda _: hbm, outs),
        scratch_shapes=list(scratch) + buffers + [semaphores],
        compiler_params=pltpu.CompilerParams(vmem_limit_bytes=60 << 20),
    )(*args)


def shape_of(dims, dtype):
    return jax.ShapeDtypeStruct(tuple(dims), dtype)


def cube_masks(n):
    masks = [1 << b for b in range(n.bit_length() - 1)]
    if len(masks) >= 2:
        masks[-1] |= masks[-2]
    return masks


def coefficients(v, n):
    bits = [(v >> b) & 1 for b in range(n.bit_length() - 1)]
    if len(bits) >= 2:
        bits[-2] = bits[-2] ^ bits[-1]
    return bits


def scatter_order(n, core, turn):
    rest = [b for b in range(n.bit_length() - 1) if b != core]
    return (rest, [rest[1], rest[0], *rest[2:]], [*rest[2:], *rest[:2]])[turn]


def gather_order(n, core, turn):
    return list(reversed(scatter_order(n, core, turn)))


def swap(x, n, dim):
    mask = cube_masks(n)[dim]
    return lax.ppermute(x, AX, [(i, i ^ mask) for i in range(n)])


def gather_slot(v, n, core, turn):
    bits = coefficients(v, n)
    slot = 0
    for place, dim in enumerate(gather_order(n, core, turn)):
        slot = slot + (bits[dim] << place)
    return slot


def scatter_slot(v, n, core, turn):
    bits = coefficients(v, n)
    slot = 0
    for place, dim in enumerate(reversed(scatter_order(n, core, turn))):
        slot = slot + (bits[dim] << place)
    return slot


def cube_gather(piece, n, core):
    buf = piece[None]
    first, second = gather_order(n, core, 0), gather_order(n, core, 1)
    for dim in first[:-2]:
        buf = jnp.concatenate([buf, swap(buf, n, dim)], axis=0)
    half = piece.shape[1] // 2
    mid = buf
    bufs = [buf[:, :, :half], buf[:, :, half:]]
    for dims in zip(first[-2:], second[-2:]):
        got = [swap(x, n, dim) for x, dim in zip(bufs, dims)]
        bufs = [jnp.concatenate(pair, axis=0) for pair in zip(bufs, got)]
    return bufs + [swap(x, n, core) for x in bufs], mid


def merged(jobs, call):
    shapes = []
    for pairs in jobs:
        slots = pairs[0][0].shape[0]
        joint = (sum(k.shape[1] for k, _ in pairs), pairs[0][0].shape[2])
        shapes += [shape_of((slots // 2,) + joint, t) for t in (f32, bf16)]
    args = [x for pairs in jobs for pair in pairs for x in pair]
    kernel = functools.partial(merge_kernel, [len(pairs) for pairs in jobs])
    outs = call(kernel, shapes, args)
    return list(zip(outs[0::2], outs[1::2]))


def cube_scatter(jobs, splits, n, core):
    orders = [[core, *scatter_order(n, core, turn)] for turn in range(len(jobs))]
    jobs = [[(k, swap(s, n, core)) for k, s in job] for job in jobs]
    for step in range(1, len(orders[0])):
        state = merged(jobs, vmem_call if step == 1 else resident_call)
        if step == 3:
            orders = orders[:1] + orders[2:]
        jobs = [[(k, swap(s, n, o[step]))] for (k, s), o in zip(state, orders)]
        if step == 2:
            jobs = [jobs[0] + jobs[1]] + jobs[2:]
    width = jobs[0][0][0].shape[2]
    shapes = [shape_of((count, width), f32) for split in splits for count in split]
    args = [x for pairs in jobs for pair in pairs for x in pair]
    return resident_call(functools.partial(last_kernel, splits), shapes, args)


def emit(acc, first_row, rows, stride, keep, send, rows_at, me, n, core, turn, count=None, first=0):
    count = n if count is None else count
    mine = me & 1
    span = slice(rows_at, rows_at + rows)

    def step(i, c):
        d = 2 * i
        slot = scatter_slot(jnp.bitwise_xor(me - mine, first + d), n, core, turn)
        low = pl.multiple_of(first_row + (d + mine) * stride, 8)
        high = pl.multiple_of(first_row + (d + 1 - mine) * stride, 8)
        keep[slot, span, :] = acc[pl.ds(low, rows), :].astype(bf16)
        send[slot, span, :] = acc[pl.ds(high, rows), :].astype(bf16)
        return c

    lax.fori_loop(0, count // 2, step, 0)


def aligned(i, size):
    return pl.ds(pl.multiple_of(i * size, size), size)


def block_mask():
    return (iota((GW, GW), 0) // HD) == (iota((GW, GW), 1) // HD)


def block_diagonal(x):
    wide = jnp.concatenate([x] * HP, axis=0)
    return jnp.where(block_mask(), wide, jnp.zeros_like(wide))


def diagonal_half(x, j):
    return x[j * HD : (j + 1) * HD, 128 * (j // 2) : 128 * (j // 2) + 128]


def low_lanes(x, j):
    return pltpu.roll(x, HD, 1) if j % 2 else x


def high_lanes(x, j):
    return x if j % 2 else pltpu.roll(x, HD, 1)


SLOT = HD // 2 + 8


def packed(x):
    half = HD // 2
    lane = iota((half, 128), 1)
    return jnp.where(lane < HD, x[0:half], pltpu.roll(x[half:HD], HD, 1))


def unpacked(x):
    half = HD // 2
    both = jnp.concatenate([x[0:half], pltpu.roll(x[0:half], HD, 1)], axis=0)
    return jnp.where(iota((HD, 128), 1) < HD, both, 0.0)


def stacked(rows, height=8):
    rows = list(rows) + [jnp.zeros_like(rows[0])] * (height - len(rows))
    return jnp.concatenate(rows, axis=0)


def identity(size):
    return (iota((size, size), 0) == iota((size, size), 1)).astype(bf16)


def block_from_slots(read):
    rows = []
    for j in range(HP):
        half = unpacked(read(j).astype(f32))
        if j % 2:
            half = pltpu.roll(half, HD, 1)
        zero = jnp.zeros_like(half)
        rows.append(jnp.concatenate([half, zero] if j < 2 else [zero, half], axis=1))
    return jnp.concatenate(rows, axis=0).astype(bf16)


def prepare_kernel(chunks, taps_ref, gains_ref, wq, wk, wv, wo, wu, wd, now_ref, later_ref, ext):
    rows, width = wq.shape
    heads_dev, reach = taps_ref.shape
    ext[...] = jnp.zeros_like(ext)
    ext[0:heads_dev, 0:reach] = taps_ref[...].astype(f32)
    back = (iota((128, 128), 0) + iota((128, 128), 1) == KW - 1).astype(bf16)
    turned = nn(ext[...].astype(bf16), back)
    ext[heads_dev : 2 * heads_dev, :] = turned[0:heads_dev]
    ext[6:8, 0:rows] = gains_ref[...].astype(f32)
    for i, w in enumerate((wq, wk, wv)):
        now_ref[i * rows : (i + 1) * rows, :] = w[...]
    now_ref[3 * rows : 3 * rows + 8, 0:128] = ext[...].astype(bf16)
    now_ref[3 * rows : 3 * rows + 8, 128:] = jnp.zeros((8, width - 128), bf16)
    done(now_ref)
    later_ref[0 : chunks * rows, :] = wd[...]
    for k in range(chunks):
        at = (chunks + k) * rows
        later_ref[at : at + rows, :] = wu[:, k * width : (k + 1) * width]
    later_ref[2 * chunks * rows : (2 * chunks + 1) * rows, :] = wo[...]


def piece_pair(ins, turn, pair, span, lanes, me, n, core):
    mine = me & 1
    slot = gather_slot(jnp.bitwise_xor(me - mine, 2 * pair), n, core, turn)
    own = ins[turn][slot, span, lanes]
    other = ins[2 + turn][slot, span, lanes]
    return jnp.where(mine == 0, own, other), jnp.where(mine == 0, other, own)


def natural(ins, units, me, n, core, rows, width):
    half = width // 2

    def place_rows(pair, c):
        to = pl.ds(pl.multiple_of(2 * rows * pair, 16), 2 * rows)
        for turn in range(2):
            for unit, out in units:
                span = slice(unit * rows, (unit + 1) * rows)
                both = piece_pair(ins, turn, pair, span, slice(None), me, n, core)
                out[to, turn * half : (turn + 1) * half] = jnp.concatenate(both, axis=0)
        return c

    lax.fori_loop(0, n // 2, place_rows, 0)


def query_key_kernel(cfg, me_ref, x_ref, *refs):
    n, core, hyper, rows, parts, scale, segment, heads_dev, head_size = cfg
    ins, refs = refs[:4], refs[4:]
    q_ref, k_ref, land_ref, wqk = refs
    me = me_ref[0]
    width = x_ref.shape[1]
    ready(*ins)
    if hyper:
        natural(ins, ((0, wqk.buf.at[0]), (1, wqk.buf.at[1])), me, n, core, rows, width)
    else:
        for unit, piece in enumerate(ins[:2]):
            wqk[unit] = piece[...]
    done(wqk)
    q_ref[...] = (nn(x_ref[...], wqk[0]) * scale).astype(bf16)
    done(q_ref)
    k_ref[...] = (nn(x_ref[...], wqk[1]) * scale).astype(bf16)
    done(k_ref)
    pieces = []
    each = x_ref.shape[0] // (2 * parts)
    for ref in (q_ref, k_ref):
        for at_row in range(2 * parts):
            span = ref[at_row * each : (at_row + 1) * each, :].astype(f32)
            pieces.append(jnp.sum(span, axis=0, keepdims=True) * (1.0 / segment))
    if parts < 2:
        pieces.append(jnp.zeros((8 - 4 * parts, width), f32))
    shared = jnp.concatenate(pieces, axis=0).astype(land_ref.dtype)
    for d in range(n):
        land_ref[d] = shared


def value_kernel(cfg, me_ref, x_ref, *refs):
    n, core, hyper, rows, parts, scale, segment, heads_dev, head_size = cfg
    ins, refs = refs[:4], refs[4:]
    v_ref, toep_ref, peot_ref, gain_ref, wv = refs
    me = me_ref[0]
    width = x_ref.shape[1]
    ready(*ins)
    if hyper:
        natural(ins, ((2, wv),), me, n, core, rows, width)

        def small_pair(pair):
            span = slice(3 * rows, 3 * rows + 8)
            return piece_pair(ins, 0, pair, span, slice(0, GW), me, n, core)

    else:
        wv[...] = ins[2][...]

        def small_pair(pair):
            return ins[3][2 * pair, :, 0:GW], ins[3][2 * pair + 1, :, 0:GW]

    done(wv)
    v_ref[...] = nn(x_ref[...], wv[...]).astype(bf16)
    done(v_ref)
    place = (iota((128, width), 1) % rows == iota((128, width), 0)).astype(bf16)

    def add(d, small, gains):
        inside = iota((8, width), 1) // rows == d
        return gains + jnp.where(inside, nn(small[:, 0:128], place), 0.0)

    def add_pair(pair, gains):
        first, second = small_pair(pair)
        return add(2 * pair + 1, second, add(2 * pair, first, gains))

    gain_ref[...] = lax.fori_loop(0, n // 2, add_pair, jnp.zeros(gain_ref.shape, f32))
    for d in range(head_size):
        taps = small_pair(d // 2)[d % 2].astype(f32)
        for i in range(heads_dev):
            for row, out in ((i, toep_ref), (heads_dev + i, peot_ref)):
                spread = jnp.broadcast_to(taps[row : row + 1, :], (CT, GW))
                spread = pltpu.roll(spread, 0, 1, stride=1, stride_axis=0)
                out[d * heads_dev + i] = spread[:, 0:CE].astype(bf16)


def newton_kernel(heads, me_ref, ql_ref, kl_ref, inv_ref, keep_ref, two_ref):
    unit = lax.rem(me_ref[0], 2 * heads)
    second = unit >= heads
    head = jnp.where(second, unit - heads, unit)
    width = ql_ref.shape[1]
    pick = (iota((width, HD), 0) == iota((width, HD), 1) + head * HD).astype(bf16)

    def mine(ref):
        rows = jnp.where(second, ref[M : 2 * M, :].astype(f32), ref[0:M, :].astype(f32))
        return nn(rows.astype(bf16), pick).astype(bf16)

    query, key = mine(ql_ref), mine(kl_ref)
    score = nt(query, key)
    e = jnp.exp(score - jnp.max(score, axis=1, keepdims=True))
    kernel = e / jnp.sum(e, axis=1, keepdims=True)
    column = jnp.sum(kernel, axis=0, keepdims=True)
    largest = jnp.max(column, axis=1, keepdims=True)
    eye = (iota((M, M), 0) == iota((M, M), 1)).astype(f32)
    z = kernel.T / largest
    two_ref[0] = kernel
    two_ref[1] = column + jnp.zeros_like(kernel)
    two_ref[2] = query.astype(f32)
    two_ref[3] = key.astype(f32)

    def iterate(step, z):
        p = exact(kernel, z)
        a = 7.0 * eye - p
        b = 15.0 * eye - exact(p, a)
        c = 13.0 * eye - exact(p, b)
        for i, value in enumerate((z, p, a, b, c)):
            keep_ref[step, i] = value
        return 0.25 * exact(z, c)

    inv_ref[...] = lax.fori_loop(0, NEWTON, iterate, z)


def newton_back_kernel(
    heads, me_ref, dinv_ref, inv_ref, keep_ref, two_ref, dq_ref, dk_ref
):
    turned = ((0,), (0,))
    across = ((1,), (1,))
    ready(keep_ref)
    kernel = two_ref[0]

    def iterate(i, state):
        dz, dkernel = state
        step = NEWTON - 1 - i
        z, p, a, b, c = (keep_ref[step, k] for k in range(5))
        dc = 0.25 * exact(z, dz, turned)
        db = -exact(p, dc, turned)
        da = -exact(p, db, turned)
        dp = -exact(dc, b, across) - exact(db, a, across) - da
        dkernel = dkernel + exact(dp, z, across)
        return 0.25 * exact(dz, c, across) + exact(kernel, dp, turned), dkernel

    dz, dkernel = lax.fori_loop(0, NEWTON, iterate, (dinv_ref[...], jnp.zeros_like(kernel)))
    column = two_ref[1]
    largest = jnp.max(column[0:1, :], axis=1, keepdims=True)
    dkernel = dkernel + dz.T / largest
    dlargest = -jnp.sum(dz * kernel.T, keepdims=True) / (largest * largest)
    top = (column == largest).astype(f32)
    ties = jnp.sum(top[0:1, :], axis=1, keepdims=True)
    dkernel = dkernel + dlargest * top / ties
    dscore = kernel * (dkernel - jnp.sum(dkernel * kernel, axis=1, keepdims=True))
    dquery = exact(dscore, two_ref[3])
    dkey = exact(dscore, two_ref[2], turned)
    unit = me_ref[0]
    width = dq_ref.shape[2]
    second = lax.rem(unit, 2 * heads) >= heads
    head = jnp.where(second, unit - heads, unit)
    place = (iota((HD, width), 1) == iota((HD, width), 0) + head * HD).astype(f32)
    live = unit < 2 * heads
    for out, value in ((dq_ref, dquery), (dk_ref, dkey)):
        wide = exact(jnp.where(live, value, 0.0), place)
        out[0] = jnp.where(second, 0.0, wide)
        out[1] = jnp.where(second, wide, 0.0)


def score3_kernel(heads, parts, k_ref, v_ref, got_ref, ql_ref, kl_ref, p_ref, out_ref, lands):
    tokens = k_ref.shape[0] // 2
    n = out_ref.shape[0]
    width = k_ref.shape[1]
    ready(got_ref)
    for d in range(n):
        got = got_ref[d].astype(f32)
        for i in range(4):
            lands[i, d * parts : (d + 1) * parts, :] = got[i * parts : (i + 1) * parts]
    for i, out in ((0, ql_ref), (2, kl_ref)):
        both = lands[i : i + 2]
        if n * parts != M:
            both = jnp.sum(both.reshape(2, M, n * parts // M, width), axis=2)
        out[...] = both.reshape(2 * M, width).astype(bf16)
    for u in range(2 * heads, n):
        out_ref[u] = jnp.zeros((SLOT, 128), bf16)
    ready(k_ref, v_ref)
    done(ql_ref, kl_ref)

    @pl.loop(0, 2)
    def _(s):
        for g in range(k_ref.shape[1] // GW):
            lanes = slice(g * GW, (g + 1) * GW)
            rows = aligned(s, tokens)
            land = block_diagonal(ql_ref[aligned(s, M), lanes])
            score = nt(land, k_ref[rows, lanes])
            top = jnp.max(score, axis=1, keepdims=True).astype(bf16).astype(f32)
            e = jnp.exp(score - top)
            total = jnp.sum(e, axis=1, keepdims=True)
            low = e.astype(bf16)
            p_ref[s, g] = low
            part = nn(low, v_ref[rows, lanes])
            high = total.astype(bf16).astype(f32)
            which = iota((GW, 8), 1)
            stats = jnp.where(which == 0, top, 0.0)
            stats = jnp.where(which == 1, high, stats)
            stats = jnp.where(which == 2, total - high, stats).astype(bf16)
            stats = tn(stats, identity(GW))
            for j in range(HP):
                slot = packed(low_lanes(diagonal_half(part, j), j))
                stat = low_lanes(stats[:, 128 * (j // 2) : 128 * (j // 2) + 128], j)
                slot = jnp.concatenate([slot, stat], axis=0)
                out_ref[s * heads + g * HP + j] = slot.astype(bf16)


def combine_kernel(got_ref, inv_ref, out_ref, sum_ref):
    n = got_ref.shape[0]
    half = HD // 2
    ready(got_ref)
    tops = jnp.concatenate([got_ref[d, half : half + 8].astype(f32)[0:1] for d in range(n)], axis=0)
    top = jnp.max(tops, axis=0, keepdims=True)
    weights = jnp.exp(tops - top)
    sums = []
    for d in range(n):
        stat = got_ref[d, half : half + 8].astype(f32)
        sums.append(stat[1:2] + stat[2:3])
    total = jnp.sum(weights * jnp.concatenate(sums, axis=0), axis=0, keepdims=True)
    total = jnp.where(total > 0.0, total, 1.0)
    weights = (weights / total).T
    lane = iota((half, 128), 1)
    acc = jnp.zeros((half, 128), f32)
    for d in range(n):
        by = weights[:, d : d + 1]
        by = jnp.where(lane < HD, by[0:half], by[half:HD])
        acc = acc + by * got_ref[d, 0:half].astype(f32)
    summary = unpacked(acc)
    sum_ref[...] = summary
    mixed = exact(inv_ref[...], summary)
    high = total.astype(bf16).astype(f32)
    slot = jnp.concatenate([packed(mixed), stacked([top, high, total - high])], axis=0)
    slot = slot.astype(bf16)
    for d in range(n):
        out_ref[d] = slot


def fill_extended(ext, ref, low_ref, high_ref, tokens):
    for s in range(2):
        ext[s, 0:REACH, :] = low_ref[s]
        ext[s, REACH : REACH + tokens, :] = ref[s * tokens : (s + 1) * tokens, :]
        ext[s, REACH + tokens : 2 * REACH + tokens, :] = high_ref[s]


def convolve(ext, toep_ref, s, g, tile):
    piece = ext[s, tile * CT : tile * CT + CE, aligned(g, GW)]
    lane = iota((CT, GW), 1) // HD
    out = nn(toep_ref[g * HP], piece)
    for j in range(1, HP):
        out = jnp.where(lane == j, nn(toep_ref[g * HP + j], piece), out)
    return out


def softmax1(land, queries):
    tokens = queries.shape[0]
    score = nt(land, queries).reshape(HP, M, tokens)
    e = jnp.exp(score - jnp.max(score, axis=1, keepdims=True))
    return (e / jnp.sum(e, axis=1, keepdims=True)).reshape(GW, tokens)


def kernel1_kernel(q_ref, v_ref, low_ref, high_ref, kl_ref, toep_ref, conv_ref, k1_ref, ext):
    tokens = q_ref.shape[0] // 2
    fill_extended(ext, v_ref, low_ref, high_ref, tokens)
    ready(q_ref, kl_ref, toep_ref)

    @pl.loop(0, 2)
    def _(s):
        for g in range(q_ref.shape[1] // GW):
            lanes = slice(g * GW, (g + 1) * GW)
            rows = aligned(s, tokens)
            land = block_diagonal(kl_ref[aligned(s, M), lanes])
            k1_ref[s, g] = softmax1(land, q_ref[rows, lanes]).astype(bf16)
            for tile in range(tokens // CT):
                at = pl.ds(pl.multiple_of(s * tokens + tile * CT, CT), CT)
                conv_ref[at, lanes] = convolve(ext, toep_ref, s, g, tile)


def norm(h):
    center = h - jnp.mean(h, axis=1, keepdims=True)
    rstd = lax.rsqrt(jnp.mean(center * center, axis=1, keepdims=True) + EPS)
    return center * rstd, rstd


def norm_back(dx, hat, rstd):
    return rstd * (
        dx - jnp.mean(dx, axis=1, keepdims=True) - hat * jnp.mean(dx * hat, axis=1, keepdims=True)
    )


RT = 128


def row_tiles(total, body):
    def step(i, c):
        body(pl.ds(pl.multiple_of(i * RT, RT), RT))
        return c

    lax.fori_loop(0, total // RT, step, 0, unroll=2)


def layer_kernel(chunks, heads, k1_ref, conv_ref, mixed_ref, x_ref, gain_ref, cot_ref, *refs):
    scratch, refs = refs[-9:], refs[:-9]
    heads_ref, act, du, n1b, dd, db, hat1, rstd1, acc = scratch
    hyper = len(refs) == 7
    weights, refs = (refs[:1], refs[1:]) if hyper else (refs[:3], refs[3:])
    mbd_ref, out_ref, dh1_ref, dheads_ref, gn_ref = refs[:5]
    grads = refs[5:]
    total, width = x_ref.shape
    tokens = total // 2

    if hyper:
        (fetched,) = weights
        all_ref = fetched.buf
        n, _, rows, _ = all_ref.shape
        per = n // chunks

        def w_up(c):
            return all_ref[:, chunks + c].reshape(width, width)

        def w_down(c):
            return all_ref[pl.ds(c * per, per), 0:chunks].reshape(width, width)

        def w_out():
            return all_ref[:, 2 * chunks].reshape(width, width)

        def put_up(c, g):
            all_ref[:, chunks + c] = g.reshape(n, rows, width)

        def put_down(c, g):
            all_ref[pl.ds(c * per, per), 0:chunks] = g.reshape(per, chunks, rows, width)

        def put_out(g):
            all_ref[:, 2 * chunks] = g.reshape(n, rows, width)

        out_ready, up_ready, down_ready = (functools.partial(fetched.ready, i) for i in range(3))
        out_done, up_done, down_done = (functools.partial(grads[0].done, i) for i in range(3))
    else:
        wo_ref, wu_ref, wd_ref = (w.buf for w in weights)
        w_up = lambda c: wu_ref[c]
        w_down = lambda c: wd_ref[c]
        w_out = lambda: wo_ref[...]

        def put_up(c, g):
            wu_ref[c] = g

        def put_down(c, g):
            wd_ref[c] = g

        def put_out(g):
            wo_ref[...] = g

        out_ready, up_ready, down_ready = (w.ready for w in weights)
        out_done, up_done, down_done = (g.done for g in grads)

    ready(k1_ref, conv_ref, mixed_ref)
    down = conv_ref.buf

    @pl.loop(0, 2)
    def _(s):
        for g in range(width // GW):
            lanes = slice(g * GW, (g + 1) * GW)
            span = aligned(s, tokens)
            mbd = block_from_slots(lambda j: mixed_ref[s * heads + g * HP + j, 0 : HD // 2])
            mbd_ref[s, g] = mbd
            heads_ref[span, lanes] = (tn(k1_ref[s, g], mbd) + down[span, lanes]).astype(bf16)

    done(mbd_ref)
    ready(gain_ref)
    g1 = gain_ref[6:7, :]
    g2 = gain_ref[7:8, :]
    gn_ref[...] = jnp.zeros(gn_ref.shape, f32)
    out_ready()
    ready(x_ref)
    down[...] = nn(heads_ref[...], w_out())

    def first(r):
        hat, rstd = norm(x_ref[r, :].astype(f32) + down[r, :])
        hat1[r, :] = hat
        rstd1[r, :] = jnp.broadcast_to(rstd, (RT, 128))
        value = hat * g1
        n1b[r, :] = value.astype(bf16)
        down[r, :] = value

    row_tiles(total, first)
    up_ready()
    down_ready()
    ready(cot_ref)

    @pl.loop(0, chunks)
    def _(c):
        up = nn(n1b[...], w_up(c))
        cdf = 0.5 * (1.0 + lax.erf(up * (0.5**0.5)))
        density = jnp.exp(-0.5 * up * up) * 0.3989422804014327
        value = (up * cdf).astype(bf16)
        act[c] = value
        du[c] = (cdf + up * density).astype(bf16)
        down[...] += nn(value, w_down(c))

    dh2 = dh1_ref.buf

    def second(r):
        hat, rstd = norm(down[r, :])
        out_ref[r, :] = (hat * g2).astype(bf16)
        g = cot_ref[r, :].astype(f32)
        gn_ref[1:2, :] += jnp.sum(g * hat, axis=0, keepdims=True)
        d = norm_back(g * g2, hat, rstd)
        dh2[r, :] = d
        dd[r, :] = d.astype(bf16)

    row_tiles(total, second)
    done(out_ref)

    @pl.loop(0, chunks)
    def _(c):
        part = (nt(dd[...], w_down(c)) * du[c].astype(f32)).astype(bf16)
        du[c] = part
        dh2[...] += nt(part, w_up(c))

    def third(r):
        hat = hat1[r, :]
        d = dh2[r, :]
        gn_ref[0:1, :] += jnp.sum(d * hat, axis=0, keepdims=True)
        d = norm_back(d * g1, hat, rstd1[r, :][:, 0:1])
        dh2[r, :] = d
        db[r, :] = d.astype(bf16)

    row_tiles(total, third)
    done(dh1_ref, gn_ref)
    dheads_ref[...] = nt(db[...], w_out()).astype(bf16)
    done(dheads_ref)

    @pl.loop(0, chunks)
    def _(c):
        acc[...] = tn(act[c], dd[...])
        put_down(c, acc[...].astype(bf16))

    down_done()

    @pl.loop(0, chunks)
    def _(c):
        acc[...] = tn(n1b[...], du[c])
        put_up(c, acc[...].astype(bf16))

    up_done()
    acc[...] = tn(heads_ref[...], db[...])
    put_out(acc[...].astype(bf16))
    out_done()


def attend_back_kernel(heads, dh_ref, k1_ref, mbd_ref, kl_ref, q_ref, dq_ref, dkl_ref, out_ref):
    tokens = q_ref.shape[0] // 2
    n = out_ref.shape[0]
    for u in range(2 * heads, n):
        out_ref[u] = jnp.zeros((HD // 2, 128), bf16)
    mask = block_mask()
    ready(dh_ref, k1_ref, mbd_ref, kl_ref, q_ref)

    @pl.loop(0, 2)
    def _(s):
        for g in range(q_ref.shape[1] // GW):
            lanes = slice(g * GW, (g + 1) * GW)
            rows = aligned(s, tokens)
            dh = dh_ref[rows, lanes]
            land = block_diagonal(kl_ref[aligned(s, M), lanes])
            low = k1_ref[s, g]
            k1 = low.astype(f32)
            dk1 = nt(mbd_ref[s, g], dh)
            row = jnp.sum((k1 * dk1).reshape(HP, M, tokens), axis=1, keepdims=True)
            centered = (dk1.reshape(HP, M, tokens) - row).reshape(GW, tokens)
            ds = (k1 * centered).astype(bf16)
            dq_ref[rows, lanes] = tn(ds, land)
            dland = jnp.where(mask, nn(ds, q_ref[rows, lanes]), 0.0)
            dkl_ref[s, :, lanes] = jnp.sum(dland.reshape(HP, M, GW), axis=0)
            dmixed = nn(low, dh)
            for j in range(HP):
                slot = packed(low_lanes(diagonal_half(dmixed, j), j))
                out_ref[s * heads + g * HP + j] = slot.astype(bf16)


def conv_back_kernel(
    dh_ref, dlow_ref, dhigh_ref, v_ref, low_ref, high_ref, peot_ref, dv_ref, gc_ref, dext, ext, gram
):
    tokens = v_ref.shape[0] // 2
    groups = v_ref.shape[1] // GW
    fill_extended(dext, dh_ref, dlow_ref, dhigh_ref, tokens)
    fill_extended(ext, v_ref, low_ref, high_ref, tokens)
    ready(peot_ref)
    lane = iota((CT, GW), 1) // HD
    ready(dh_ref)
    back = (iota((CT, CT), 0) + iota((CT, CT), 1) == CT - 1).astype(f32)

    @pl.loop(0, groups)
    def _(g):
        lanes = aligned(g, GW)
        gram[...] = jnp.zeros_like(gram)

        @pl.loop(0, 2)
        def _(s):
            for tile in range(tokens // CT):
                at = pl.ds(pl.multiple_of(s * tokens + tile * CT, CT), CT)
                dv_ref[at, lanes] = convolve(dext, peot_ref, s, g, tile)
                dh = dh_ref[at, lanes]
                each = jnp.concatenate(
                    [jnp.where(lane == j, dh, jnp.zeros_like(dh)) for j in range(HP)], axis=0
                )
                gram[:, 0:CE] += nt(each, ext[s, tile * CT : tile * CT + CE, lanes])

        rows = []
        for j in range(HP):
            turned = exact(back, gram[j * CT : (j + 1) * CT, :])
            rolled = pltpu.roll(turned, 0, 1, stride=1, stride_axis=0)
            rows.append(jnp.sum(rolled, axis=0, keepdims=True))
        gc_ref[g] = jnp.concatenate(rows, axis=0)


def owner_back_kernel(got_ref, inv_ref, sum_ref, out_ref, dinv_ref):
    n = got_ref.shape[0]
    ready(got_ref)
    dmixed = unpacked(
        lax.fori_loop(
            0, n, lambda d, a: a + got_ref[d].astype(f32), jnp.zeros((HD // 2, 128), f32)
        )
    )
    dsum = exact(inv_ref[...], dmixed, ((0,), (0,))).astype(bf16).astype(f32)
    ones = jnp.ones((8, 128), f32)
    row = exact(ones, dsum * sum_ref[...], ((1,), (1,)))[0:1]
    row = jnp.concatenate([row, jnp.zeros_like(row)], axis=1)
    high = row.astype(bf16).astype(f32)
    slot = jnp.concatenate([packed(dsum), stacked([high, row - high])], axis=0).astype(bf16)
    for d in range(n):
        out_ref[d] = slot
    done(out_ref)
    dinv_ref[...] = exact(dmixed, sum_ref[...], ((1,), (1,)))


def score3_back_kernel(
    heads, parts, sent_ref, stat_ref, dsum_ref, p_ref, k_ref, v_ref, ql_ref, dq2_ref, dk2_ref,
    dk1_ref, dk_ref, dv_ref, out_ref, dql,
):
    tokens = k_ref.shape[0] // 2
    n = out_ref.shape[0]
    mask = block_mask()
    ready(sent_ref, stat_ref, dsum_ref, p_ref, k_ref, v_ref, ql_ref, dq2_ref)

    @pl.loop(0, 2)
    def _(s):
        for g in range(k_ref.shape[1] // GW):
            lanes = slice(g * GW, (g + 1) * GW)
            rows = aligned(s, tokens)
            factors, terms = [], []
            for j in range(HP):
                u = s * heads + g * HP + j
                stat_rows = slice(HD // 2, HD // 2 + 8)
                local = sent_ref[u, stat_rows].astype(f32)[0:1]
                stat = stat_ref[u, stat_rows].astype(f32)
                factors.append(jnp.exp(local - stat[0:1]) / (stat[1:2] + stat[2:3]))
                d = dsum_ref[u, stat_rows].astype(f32)
                terms.append(d[0:1] + d[1:2])

            def joined(parts):
                lane = iota((1, 128), 1)
                halves = [
                    jnp.where(lane < HD, parts[j], pltpu.roll(parts[j + 1], HD, 1))
                    for j in range(0, HP, 2)
                ]
                return jnp.concatenate(halves, axis=1)

            rows_in = []
            for value in (joined(factors), joined(terms)):
                for _ in range(3):
                    term = value.astype(bf16).astype(f32)
                    rows_in.append(term)
                    value = value - term
            columns = nt(identity(GW), stacked(rows_in).astype(bf16))
            factor = columns[:, 0:1] + columns[:, 1:2] + columns[:, 2:3]
            term = columns[:, 3:4] + columns[:, 4:5] + columns[:, 5:6]
            k3 = p_ref[s, g].astype(f32) * factor
            dbd = block_from_slots(lambda j: dsum_ref[s * heads + g * HP + j, 0 : HD // 2])
            dk3 = nt(dbd, v_ref[rows, lanes])
            ds = (k3 * (dk3 - term)).astype(bf16)
            dland = jnp.where(mask, nn(ds, k_ref[rows, lanes]), 0.0)
            dql[s, :, lanes] = jnp.sum(dland.reshape(HP, M, GW), axis=0) + dq2_ref[s, :, lanes]
            land = block_diagonal(ql_ref[aligned(s, M), lanes])
            dk_ref[rows, lanes] = tn(ds, land)
            dv_ref[rows, lanes] = tn(k3.astype(bf16), dbd)
    for d in range(n):
        first = d * parts * M // (n * parts)
        span = slice(first, first + parts)
        pieces = [dql[0, span, :], dql[1, span, :]]
        pieces += [dk2_ref[s, span, :] + dk1_ref[s, span, :] for s in range(2)]
        if parts < 2:
            pieces.append(jnp.zeros((8 - 4 * parts, dql.shape[2]), f32))
        out_ref[d] = jnp.concatenate(pieces, axis=0).astype(bf16)


def two_terms(x):
    high = x.astype(bf16)
    return high, (x - high.astype(f32)).astype(bf16)


def final_kernel(
    cfg, me_ref, x_ref, dv3_ref, dvc_ref, dk3_ref, dq1_ref, wv, wqk, dh1_ref,
    dx_ref, sums_ref, gqk_ref, *refs
):
    n, core, hyper, rows, parts, scale, segment = cfg
    outs, acc, low, dv = refs[:-3], *refs[-3:]
    tokens = x_ref.shape[0] // 2
    each = tokens // parts
    dv[...] = (dvc_ref[...] + dv3_ref[...]).astype(bf16)
    acc[...] = tn(x_ref[...], dv[...])
    if hyper:
        emit(acc, 0, rows, rows, outs[0], outs[1], 0, me_ref[0], n, core, 2)
    else:
        outs[0][...] = acc[...]
    done(*outs)
    for s in range(2):
        for l in range(parts):
            span = slice(s * tokens + l * each, s * tokens + (l + 1) * each)
            at = s * parts + l
            sums_ref[at : at + 1, :] = jnp.sum(
                x_ref[span, :].astype(f32), axis=0, keepdims=True
            )
    done(sums_ref)
    low[1] = dk3_ref[...].astype(bf16)
    low[0] = dq1_ref[...].astype(bf16)
    ready(wqk, wv, dh1_ref)
    acc[...] = dh1_ref[...] + nt(dv[...], wv[...])

    @pl.loop(0, 2)
    def _(t):
        gqk_ref[t] = tn(x_ref[...], low[t]) * scale
        acc[...] += nt(low[t], wqk[t]) * scale

    dx_ref[...] = acc[...]


def landmark_sums(got_ref, factor):
    ready(got_ref)
    n, _, width = got_ref.shape
    zero = jnp.zeros((8, width), f32)
    return factor * lax.fori_loop(0, n, lambda d, a: a + got_ref[d].astype(f32), zero)


def landmark_kernel(cfg, me_ref, got_ref, sums_ref, gqk_ref, small_ref, *refs):
    n, core, hyper, rows, parts, scale, segment = cfg
    outs, acc = refs[:-1], refs[-1]
    me = me_ref[0]
    count = 2 * parts
    land = landmark_sums(got_ref, scale / segment)
    s_high, s_low = two_terms(sums_ref[0:count, :])
    left = jnp.concatenate([s_high, s_low, s_high], axis=0)
    for turn, base in enumerate((0, count)):
        high, low = two_terms(land[base : base + count, :])
        acc[...] = gqk_ref[turn] + tn(left, jnp.concatenate([high, high, low], axis=0))
        if hyper:
            keep, send = outs[2 * turn : 2 * turn + 2]
            emit(acc, 0, rows, rows, keep, send, 0, me, n, core, turn)
        else:
            outs[turn][...] = acc[...]
    if hyper:
        ready(small_ref)
        mine = me & 1
        span = slice(rows, rows + 8)

        def step(i, c):
            slot = scatter_slot(jnp.bitwise_xor(me - mine, 2 * i), n, core, 0)
            outs[0][slot, span, 0:GW] = small_ref[2 * i + mine]
            outs[1][slot, span, 0:GW] = small_ref[2 * i + 1 - mine]
            return c

        lax.fori_loop(0, n // 2, step, 0)


def tokens_kernel(cfg, got_ref, wqk, dx_ref, out_ref):
    n, core, hyper, rows, parts, scale, segment = cfg
    tokens = dx_ref.shape[0] // 2
    each = tokens // parts
    count = 2 * parts
    land = landmark_sums(got_ref, scale / segment)
    change = 0.0
    for turn, base in enumerate((0, count)):
        both = nt(jnp.concatenate(two_terms(land[base : base + count, :]), axis=0), wqk[turn])
        change = change + both[0:count] + both[count : 2 * count]
    for s in range(2):
        for l in range(parts):
            span = slice(s * tokens + l * each, s * tokens + (l + 1) * each)
            at = s * parts + l
            out_ref[span, :] = (dx_ref[span, :] + change[at : at + 1, :]).astype(bf16)


def merge_kernel(counts, *refs):
    ready(*refs[: 2 * sum(counts)])
    outs = refs[2 * sum(counts) :]
    at = 0
    for job, count in enumerate(counts):
        ins = refs[2 * at : 2 * (at + count)]
        at += count
        row = 0
        kept, sent = outs[2 * job], outs[2 * job + 1]
        for keep, got in zip(ins[0::2], ins[1::2]):
            span = slice(row, row + keep.shape[1])
            row += keep.shape[1]
            half = keep.shape[0] // 2

            @pl.loop(0, half)
            def _(j):
                kept[j, span] = keep[j].astype(f32) + got[j].astype(f32)
                sent[j, span] = (
                    keep[half + j].astype(f32) + got[half + j].astype(f32)
                ).astype(bf16)

        done(sent)


def last_kernel(splits, *refs):
    ins, outs = refs[: 2 * len(splits)], list(refs[2 * len(splits) :])
    for i, split in enumerate(splits):
        keep, got = ins[2 * i], ins[2 * i + 1]
        row = 0
        for count in split:
            span = slice(row, row + count)
            outs.pop(0)[...] = keep[0, span].astype(f32) + got[0, span].astype(f32)
            row += count


def unpack_kernel(chunks, got_ref, up_ref, down_ref, out_ref):
    out_ref[...] = got_ref[2 * chunks].astype(f32)
    rows, width = got_ref.shape[1:]
    for c in range(chunks):
        up_ref[:, c * width : (c + 1) * width] = got_ref[chunks + c].astype(f32)
        down_ref[c * rows : (c + 1) * rows, :] = got_ref[c].astype(f32)


def exchange(x):
    return lax.all_to_all(x, AX, 0, 0, tiled=True)


def per_device(
    tokens, w_query, w_key, w_value, w_out, conv_kernel, norm1_gain, w_up, w_down, norm2_gain, cotangent
):
    sequences, held, width = tokens.shape
    blk, head = lax.axis_size("blk"), lax.axis_size("head")
    n = blk * head
    heads_dev = conv_kernel.shape[0]
    heads = heads_dev * head
    rows = w_query.shape[0]
    hidden = w_up.shape[1]
    chunks = hidden // width
    segment = held * n // M
    parts = max(1, held // segment)
    groups = width // GW
    hyper = rows % 8 == 0 and n == 32
    core = 0 if n <= 32 else head.bit_length() - 1
    scale = HD**-0.25
    total = sequences * held
    me = (lax.axis_index("blk") * head + lax.axis_index("head")).astype(jnp.int32)
    me = me.reshape(1)
    x = tokens.reshape(total, width)

    if hyper:
        now, later = vmem_call(
            functools.partial(prepare_kernel, chunks),
            (
                shape_of((3 * rows + 8, width), bf16),
                shape_of(((2 * chunks + 1) * rows, width), bf16),
            ),
            (
                conv_kernel, jnp.stack([norm1_gain, norm2_gain]),
                w_query, w_key, w_value, w_out, w_up, w_down,
            ),
            scratch=[pltpu.VMEM((8, 128), f32)],
        )
        pieces, mid = cube_gather(now, n, core)
        later, _ = lax.optimization_barrier((later, mid))
        later = lax.all_gather(later, AX, axis=0).reshape(n, 2 * chunks + 1, rows, width)
        weights = (later,)
        weight_parts = {
            6: [
                (slice(None), slice(2 * chunks, None)),
                (slice(None), slice(chunks, 2 * chunks)),
                (slice(None), slice(0, chunks)),
            ]
        }
    else:
        taps = jnp.concatenate([conv_kernel, conv_kernel[:, ::-1]], axis=0)
        both = jnp.stack([norm1_gain, norm2_gain])
        extras = jnp.concatenate(
            [
                jnp.pad(taps, ((0, 0), (0, width - KW))),
                jnp.pad(both, ((0, 0), (0, width - rows))),
            ],
            axis=0,
        )
        pieces = [
            lax.all_gather(w, AX, axis=0, tiled=True) for w in (w_query, w_key, w_value)
        ] + [lax.all_gather(extras, AX, axis=0)]
        wo = lax.all_gather(w_out, AX, axis=0, tiled=True)
        wu = lax.all_gather(w_up, AX, axis=0, tiled=True)
        wu = wu.reshape(width, chunks, width).transpose(1, 0, 2)
        wd = lax.all_gather(w_down, AX, axis=0, tiled=True).reshape(chunks, width, width)
        weights = (wo, wu, wd)
        weight_parts = None

    cfg = (n, core, hyper, rows, parts, scale, segment, heads_dev, head)
    square_low = shape_of((total, width), bf16)
    square_full = shape_of((total, width), f32)
    weight = shape_of((width, width), bf16)
    weight_full = shape_of((width, width), f32)
    toeplitz = shape_of((heads, CT, CE), bf16)
    queries, keys, lands, wqk = vmem_call(
        functools.partial(query_key_kernel, cfg),
        (
            square_low, square_low, shape_of((n, 8, width), bf16 if held >= segment else f32),
            shape_of((2, width, width), bf16),
        ),
        (me, x, *pieces),
        scalars=1,
    )
    lands = exchange(lands)
    values, toep, peot, gains, wv = vmem_call(
        functools.partial(value_kernel, cfg),
        (square_low, toeplitz, toeplitz, shape_of((8, width), f32), weight),
        (me, x, *pieces),
        scalars=1,
    )
    lands, values = lax.optimization_barrier((lands, values))
    ahead = [(i, i + 1) for i in range(n - 1)]
    behind = [(i + 1, i) for i in range(n - 1)]

    def halo(y):
        y = y.reshape(sequences, held, width)
        low = lax.ppermute(y[:, held - REACH :], AX, ahead)
        high = lax.ppermute(y[:, :REACH], AX, behind)
        return low, high

    matrix = shape_of((M, M), f32)
    slots = shape_of((n, SLOT, 128), bf16)
    half_slots = shape_of((n, HD // 2, 128), bf16)
    land = shape_of((2 * M, width), bf16)
    q_land, k_land, p3, sent = vmem_call(
        functools.partial(score3_kernel, heads, parts),
        (land, land, shape_of((2, groups, GW, held), bf16), slots),
        (keys, values, lands),
        scratch=[pltpu.VMEM((4, n * parts, width), f32)],
    )
    got_sums = exchange(sent)
    inverse, newton_keep, kernel_two = vmem_call(
        functools.partial(newton_kernel, heads),
        (matrix, shape_of((NEWTON, 5, M, M), f32), shape_of((4, M, M), f32)),
        (me, q_land, k_land),
        scalars=1,
    )
    stat, summary = vmem_call(
        combine_kernel, (slots, shape_of((M, 128), f32)), (got_sums, inverse)
    )
    stat = exchange(stat)
    v_low, v_high = halo(values)
    convolved, k1 = vmem_call(
        kernel1_kernel,
        (square_full, shape_of((2, groups, GW, held), bf16)),
        (queries, values, v_low, v_high, k_land, toep),
        scratch=[pltpu.VMEM((2, held + 2 * REACH, width), bf16)],
    )
    stat, k1 = lax.optimization_barrier((stat, k1))
    wide = pltpu.VMEM((chunks, total, width), bf16)
    low_buffer = pltpu.VMEM((total, width), bf16)
    if hyper:
        grad_shapes = [shape_of((n, 2 * chunks + 1, rows, width), bf16)]
        grad_parts, lent = {5: weight_parts[6]}, {5: 6}
    else:
        grad_shapes = [shape_of(w.shape, bf16) for w in weights]
        grad_parts, lent = None, {5: 6, 6: 7, 7: 8}
    mbd, layer_out, d_h1, d_heads, gain_sums, *grads = vmem_call(
        functools.partial(layer_kernel, chunks, heads),
        [
            shape_of((2, groups, GW, GW), bf16), square_low, square_full, square_low,
            shape_of((8, width), f32),
        ]
        + grad_shapes,
        (k1, convolved, stat, x, gains, cotangent.reshape(total, width), *weights),
        scratch=[
            low_buffer, wide, wide, low_buffer, low_buffer, low_buffer,
            pltpu.VMEM((total, width), f32),
            pltpu.VMEM((total, 128), f32),
            pltpu.VMEM((width, width), f32),
        ],
        parts=weight_parts,
        out_parts=grad_parts,
        lent=lent,
    )
    d_low, d_high = halo(d_heads)
    spread = shape_of((2, M, width), f32)
    d_q1, d_kl1, sent_back = vmem_call(
        functools.partial(attend_back_kernel, heads),
        (square_full, spread, half_slots),
        (d_heads, k1, mbd, k_land, queries),
    )
    got_back = exchange(sent_back)
    extended = pltpu.VMEM((2, held + 2 * REACH, width), bf16)
    d_vc, conv_sums = vmem_call(
        conv_back_kernel,
        (square_full, shape_of((groups, HP, GW), f32)),
        (d_heads, d_low, d_high, values, v_low, v_high, peot),
        scratch=[extended, extended, pltpu.VMEM((HP * CT, GW), f32)],
    )
    got_back, d_vc = lax.optimization_barrier((got_back, d_vc))
    d_sum, d_inverse = vmem_call(
        owner_back_kernel, (slots, matrix), (got_back, inverse, summary)
    )
    d_sum = exchange(d_sum)
    d_ql2, d_kl2 = vmem_call(
        functools.partial(newton_back_kernel, heads),
        (spread, spread),
        (me, d_inverse, inverse, newton_keep, kernel_two),
        scalars=1,
    )
    d_k3, d_v3, sent_land = vmem_call(
        functools.partial(score3_back_kernel, heads, parts),
        (square_full, square_full, shape_of((n, 8, width), bf16)),
        (sent, stat, d_sum, p3, keys, values, q_land, d_ql2, d_kl2, d_kl1),
        scratch=[pltpu.VMEM((2, M, width), f32)],
    )
    got_land = exchange(sent_land)
    if hyper:
        early = lax.psum_scatter(grads[0], AX, scatter_dimension=0, tiled=False)
    small = gain_sums[0:2].reshape(2, n, rows).transpose(1, 0, 2).reshape(n, 2 * rows)
    tap_sums = conv_sums[:, :, CT - 1 : CT - 1 + KW].reshape(head, heads_dev * KW)
    tap_sums = jnp.broadcast_to(tap_sums[None], (blk, head, heads_dev * KW)).reshape(n, -1)
    small = jnp.concatenate([small, tap_sums], axis=1)
    small = jnp.pad(small, ((0, 0), (0, GW - small.shape[1])))
    extra_rows = (8, 0, 0)
    if hyper:
        slot_shapes = [
            [shape_of((n // 2, rows + extra, width), bf16)] * 2 for extra in extra_rows
        ]
    else:
        slot_shapes = [[shape_of((width, width), f32)]] * 3
    final_cfg = (n, core, hyper, rows, parts, scale, segment)
    d_x, x_sums, g_both, *value_slots = vmem_call(
        functools.partial(final_kernel, final_cfg),
        [square_full, shape_of((8, width), f32), shape_of((2, width, width), f32)] + slot_shapes[2],
        (me, x, d_v3, d_vc, d_k3, d_q1, wv, wqk, d_h1),
        scalars=1,
        scratch=[
            pltpu.VMEM((width, width), f32),
            pltpu.VMEM((2, total, width), bf16),
            pltpu.VMEM((total, width), bf16),
        ],
    )
    projections = vmem_call(
        functools.partial(landmark_kernel, final_cfg),
        slot_shapes[0] + slot_shapes[1],
        (
            me, got_land, x_sums, g_both,
            jnp.broadcast_to(small[:, None], (n, 8, GW)).astype(bf16),
        ),
        scalars=1,
        scratch=[pltpu.VMEM((width, width), f32)],
    )
    projections = list(projections) + value_slots
    after, _ = lax.optimization_barrier((got_land, projections))
    d_tokens = vmem_call(
        functools.partial(tokens_kernel, final_cfg), square_low, (after, wqk, d_x)
    )
    d_tokens = d_tokens.reshape(tokens.shape)
    if hyper:
        grad_up, grad_down, grad_out = vmem_call(
            functools.partial(unpack_kernel, chunks),
            (
                shape_of((rows, hidden), f32), shape_of((chunks * rows, width), f32),
                shape_of((rows, width), f32),
            ),
            (early,),
        )
        grad_query, small, grad_key, grad_value = cube_scatter(
            [
                [(projections[0], projections[1])],
                [(projections[2], projections[3])],
                [(projections[4], projections[5])],
            ],
            ((rows, 8, rows), (rows,)),
            n,
            core,
        )
        small = small[0]
    else:

        def scatter(g):
            return lax.psum_scatter(g, AX, scatter_dimension=0, tiled=True)

        grad_out = scatter(grads[0].astype(f32))
        grad_up = scatter(grads[1].astype(f32).transpose(1, 0, 2).reshape(width, hidden))
        grad_down = scatter(grads[2].astype(f32).reshape(hidden, width))
        grad_query, grad_key, grad_value = (scatter(g) for g in projections)
        small = scatter(small)[0]
    return (
        layer_out.reshape(tokens.shape),
        d_tokens,
        grad_query,
        grad_key,
        grad_value,
        grad_out,
        small[2 * rows : 2 * rows + heads_dev * KW].reshape(heads_dev, KW),
        small[:rows],
        grad_up,
        grad_down,
        small[rows : 2 * rows],
    )


def solution(mesh):
    lined = P(None, AX, None)
    rowed = P(AX, None)
    gain = P(AX)
    taps = P("head", None)
    in_specs = (lined, rowed, rowed, rowed, rowed, taps, gain, rowed, rowed, gain, lined)
    out_specs = (lined, lined, rowed, rowed, rowed, rowed, taps, gain, rowed, rowed, gain)
    return jax.shard_map(
        per_device, mesh=mesh, in_specs=in_specs, out_specs=out_specs, check_vma=False
    )
```

```python
import functools

import jax
import jax.numpy as jnp
from jax import lax
from jax.experimental import pallas as pl
from jax.experimental.pallas import tpu as pltpu
from jax.sharding import PartitionSpec as P

HD = 64
M = 64
KW = 33
NEWTON = 6
REACH = KW // 2
AX = ("blk", "head")
EPS = 1e-05
GW = 256
HP = GW // HD
CT = 128
CE = CT + 2 * REACH

bf16 = jnp.bfloat16
f32 = jnp.float32
HIGHEST = lax.Precision.HIGHEST


def nn(a, b):
    return lax.dot_general(a, b, (((1,), (0,)), ((), ())), preferred_element_type=f32)


def nt(a, b):
    return lax.dot_general(a, b, (((1,), (1,)), ((), ())), preferred_element_type=f32)


def tn(a, b):
    return lax.dot_general(a, b, (((0,), (0,)), ((), ())), preferred_element_type=f32)


def exact(a, b, dims=((1,), (0,))):
    return lax.dot_general(a, b, (dims, ((), ())), preferred_element_type=f32, precision=HIGHEST)


def iota(shape, dim):
    return lax.broadcasted_iota(jnp.int32, shape, dim)


class Fetched:
    def __init__(self, source, buf, sems, parts):
        self.buf, self.shape, self.dtype = buf, buf.shape, buf.dtype
        self.copies = [
            pltpu.make_async_copy(source.at[part], buf.at[part], sem)
            for part, sem in zip(parts, sems)
        ]
        self.waiting = list(range(len(parts)))
        for copy in self.copies:
            copy.start()

    def ready(self, *which):
        for i in which or tuple(self.waiting):
            if i in self.waiting:
                self.copies[i].wait()
                self.waiting.remove(i)

    def __getitem__(self, index):
        self.ready()
        return self.buf[index]


class Stored:
    def __init__(self, target, buf, sems, parts):
        self.buf, self.shape, self.dtype = buf, buf.shape, buf.dtype
        self.copies = [
            pltpu.make_async_copy(buf.at[part], target.at[part], sem)
            for part, sem in zip(parts, sems)
        ]
        self.left = list(range(len(parts)))

    def done(self, *which):
        for i in which or tuple(self.left):
            if i in self.left:
                self.copies[i].start()
                self.left.remove(i)

    def __getitem__(self, index):
        return self.buf[index]

    def __setitem__(self, index, value):
        self.buf[index] = value


def ready(*refs):
    for ref in refs:
        if isinstance(ref, Fetched):
            ref.ready()


def done(*refs):
    for ref in refs:
        if isinstance(ref, Stored):
            ref.done()


def resident_call(kernel, outs, args):
    vmem = pl.BlockSpec(memory_space=pltpu.VMEM)
    return pl.pallas_call(
        kernel,
        out_shape=outs,
        in_specs=[vmem] * len(args),
        out_specs=jax.tree.map(lambda _: vmem, outs),
        compiler_params=pltpu.CompilerParams(vmem_limit_bytes=8 << 20),
    )(*args)


def vmem_call(kernel, outs, args, scalars=0, scratch=(), parts=None, out_parts=None, lent=None):
    lent = lent or {}
    parts, out_parts = parts or {}, out_parts or {}
    arrays = args[scalars:]
    whole = [(slice(None),)]
    pieces = [parts.get(i, whole) for i in range(len(arrays))]
    results = jax.tree.leaves(outs)
    own_results = [r for i, r in enumerate(results) if i not in lent]
    buffers = [pltpu.VMEM(a.shape, a.dtype) for a in [*arrays, *own_results]]
    out_pieces = [out_parts.get(i, whole) for i in range(len(results))]
    semaphores = pltpu.SemaphoreType.DMA((sum(len(p) for p in pieces + out_pieces),))

    def run(*refs):
        refs = list(refs)
        take = lambda k: [refs.pop(0) for _ in range(k)]
        ins, sources, targets = take(scalars), take(len(arrays)), take(len(results))
        kept, in_bufs, own_bufs = take(len(scratch)), take(len(arrays)), take(len(own_results))
        out_bufs = [
            in_bufs[lent[i]] if i in lent else own_bufs.pop(0) for i in range(len(results))
        ]
        (sems,) = refs
        free = iter(range(sum(len(p) for p in pieces + out_pieces)))
        own = lambda piece: [sems.at[next(free)] for _ in piece]
        for source, buf, piece in zip(sources, in_bufs, pieces):
            ins.append(Fetched(source, buf, own(piece), piece))
        stored = [
            Stored(target, buf, own(piece), piece)
            for target, buf, piece in zip(targets, out_bufs, out_pieces)
        ]
        kernel(*ins, *stored, *kept)
        ready(*ins)
        done(*stored)
        for ref in stored:
            for copy in ref.copies:
                copy.wait()

    hbm = pl.BlockSpec(memory_space=pl.ANY)
    return pl.pallas_call(
        run,
        out_shape=outs,
        in_specs=[pl.BlockSpec(memory_space=pltpu.SMEM)] * scalars + [hbm] * len(arrays),
        out_specs=jax.tree.map(lambda _: hbm, outs),
        scratch_shapes=list(scratch) + buffers + [semaphores],
        compiler_params=pltpu.CompilerParams(vmem_limit_bytes=60 << 20),
    )(*args)


def shape_of(dims, dtype):
    return jax.ShapeDtypeStruct(tuple(dims), dtype)


def cube_masks(n):
    masks = [1 << b for b in range(n.bit_length() - 1)]
    if len(masks) >= 2:
        masks[-1] |= masks[-2]
    return masks


def coefficients(v, n):
    bits = [(v >> b) & 1 for b in range(n.bit_length() - 1)]
    if len(bits) >= 2:
        bits[-2] = bits[-2] ^ bits[-1]
    return bits


def scatter_order(n, core, turn):
    rest = [b for b in range(n.bit_length() - 1) if b != core]
    return (rest, [rest[1], rest[0], *rest[2:]], [*rest[2:], *rest[:2]])[turn]


def gather_order(n, core, turn):
    return list(reversed(scatter_order(n, core, turn)))


def swap(x, n, dim):
    mask = cube_masks(n)[dim]
    return lax.ppermute(x, AX, [(i, i ^ mask) for i in range(n)])


def gather_slot(v, n, core, turn):
    bits = coefficients(v, n)
    slot = 0
    for place, dim in enumerate(gather_order(n, core, turn)):
        slot = slot + (bits[dim] << place)
    return slot


def scatter_slot(v, n, core, turn):
    bits = coefficients(v, n)
    slot = 0
    for place, dim in enumerate(reversed(scatter_order(n, core, turn))):
        slot = slot + (bits[dim] << place)
    return slot


def cube_gather(piece, n, core):
    buf = piece[None]
    first, second = gather_order(n, core, 0), gather_order(n, core, 1)
    mid = None
    for dim in first[:-2]:
        buf = jnp.concatenate([buf, swap(buf, n, dim)], axis=0)
        mid = buf if mid is None else mid
    half = piece.shape[1] // 2
    bufs = [buf[:, :, :half], buf[:, :, half:]]
    for dims in zip(first[-2:], second[-2:]):
        got = [swap(x, n, dim) for x, dim in zip(bufs, dims)]
        bufs = [jnp.concatenate(pair, axis=0) for pair in zip(bufs, got)]
    return bufs + [swap(x, n, core) for x in bufs], mid


def merged(jobs, call):
    shapes = []
    for pairs in jobs:
        slots = pairs[0][0].shape[0]
        joint = (sum(k.shape[1] for k, _ in pairs), pairs[0][0].shape[2])
        shapes += [shape_of((slots // 2,) + joint, t) for t in (f32, bf16)]
    args = [x for pairs in jobs for pair in pairs for x in pair]
    kernel = functools.partial(merge_kernel, [len(pairs) for pairs in jobs])
    outs = call(kernel, shapes, args)
    return list(zip(outs[0::2], outs[1::2]))


def cube_scatter(jobs, splits, n, core):
    orders = [[core, *scatter_order(n, core, turn)] for turn in range(len(jobs))]
    jobs = [[(k, swap(s, n, core)) for k, s in job] for job in jobs]
    for step in range(1, len(orders[0])):
        state = merged(jobs, vmem_call if step == 1 else resident_call)
        if step == 3:
            orders = orders[:1] + orders[2:]
        jobs = [[(k, swap(s, n, o[step]))] for (k, s), o in zip(state, orders)]
        if step == 2:
            jobs = [jobs[0] + jobs[1]] + jobs[2:]
    width = jobs[0][0][0].shape[2]
    shapes = [shape_of((count, width), f32) for split in splits for count in split]
    args = [x for pairs in jobs for pair in pairs for x in pair]
    return resident_call(functools.partial(last_kernel, splits), shapes, args)


def emit(acc, first_row, rows, stride, keep, send, rows_at, me, n, core, turn, count=None, first=0):
    count = n if count is None else count
    mine = me & 1
    span = slice(rows_at, rows_at + rows)

    def step(i, c):
        d = 2 * i
        slot = scatter_slot(jnp.bitwise_xor(me - mine, first + d), n, core, turn)
        low = pl.multiple_of(first_row + (d + mine) * stride, 8)
        high = pl.multiple_of(first_row + (d + 1 - mine) * stride, 8)
        keep[slot, span, :] = acc[pl.ds(low, rows), :].astype(bf16)
        send[slot, span, :] = acc[pl.ds(high, rows), :].astype(bf16)
        return c

    lax.fori_loop(0, count // 2, step, 0)


def aligned(i, size):
    return pl.ds(pl.multiple_of(i * size, size), size)


def block_mask():
    return (iota((GW, GW), 0) // HD) == (iota((GW, GW), 1) // HD)


def block_diagonal(x):
    wide = jnp.concatenate([x] * HP, axis=0)
    return jnp.where(block_mask(), wide, jnp.zeros_like(wide))


def diagonal_half(x, j):
    return x[j * HD : (j + 1) * HD, 128 * (j // 2) : 128 * (j // 2) + 128]


def low_lanes(x, j):
    return pltpu.roll(x, HD, 1) if j % 2 else x


def high_lanes(x, j):
    return x if j % 2 else pltpu.roll(x, HD, 1)


SLOT = HD // 2 + 8


def packed(x):
    half = HD // 2
    lane = iota((half, 128), 1)
    return jnp.where(lane < HD, x[0:half], pltpu.roll(x[half:HD], HD, 1))


def unpacked(x):
    half = HD // 2
    both = jnp.concatenate([x[0:half], pltpu.roll(x[0:half], HD, 1)], axis=0)
    return jnp.where(iota((HD, 128), 1) < HD, both, 0.0)


def stacked(rows, height=8):
    rows = list(rows) + [jnp.zeros_like(rows[0])] * (height - len(rows))
    return jnp.concatenate(rows, axis=0)


def identity(size):
    return (iota((size, size), 0) == iota((size, size), 1)).astype(bf16)


def block_from_slots(read):
    rows = []
    for j in range(HP):
        half = unpacked(read(j).astype(f32))
        if j % 2:
            half = pltpu.roll(half, HD, 1)
        zero = jnp.zeros_like(half)
        rows.append(jnp.concatenate([half, zero] if j < 2 else [zero, half], axis=1))
    return jnp.concatenate(rows, axis=0).astype(bf16)


def prepare_kernel(chunks, taps_ref, gains_ref, wq, wk, wv, wo, wu, wd, now_ref, later_ref, ext):
    rows, width = wq.shape
    heads_dev, reach = taps_ref.shape
    ext[...] = jnp.zeros_like(ext)
    ext[0:heads_dev, 0:reach] = taps_ref[...].astype(f32)
    back = (iota((128, 128), 0) + iota((128, 128), 1) == KW - 1).astype(bf16)
    turned = nn(ext[...].astype(bf16), back)
    ext[heads_dev : 2 * heads_dev, :] = turned[0:heads_dev]
    ext[6:8, 0:rows] = gains_ref[...].astype(f32)
    for i, w in enumerate((wq, wk, wv)):
        now_ref[i * rows : (i + 1) * rows, :] = w[...]
    now_ref[3 * rows : 3 * rows + 8, 0:128] = ext[...].astype(bf16)
    now_ref[3 * rows : 3 * rows + 8, 128:] = jnp.zeros((8, width - 128), bf16)
    done(now_ref)
    later_ref[0 : chunks * rows, :] = wd[...]
    for k in range(chunks):
        at = (chunks + k) * rows
        later_ref[at : at + rows, :] = wu[:, k * width : (k + 1) * width]
    later_ref[2 * chunks * rows : (2 * chunks + 1) * rows, :] = wo[...]


def piece_pair(ins, turn, pair, span, lanes, me, n, core):
    mine = me & 1
    slot = gather_slot(jnp.bitwise_xor(me - mine, 2 * pair), n, core, turn)
    own = ins[turn][slot, span, lanes]
    other = ins[2 + turn][slot, span, lanes]
    return jnp.where(mine == 0, own, other), jnp.where(mine == 0, other, own)


def natural(ins, units, me, n, core, rows, width):
    half = width // 2

    def place_rows(pair, c):
        to = pl.ds(pl.multiple_of(2 * rows * pair, 16), 2 * rows)
        for turn in range(2):
            for unit, out in units:
                span = slice(unit * rows, (unit + 1) * rows)
                both = piece_pair(ins, turn, pair, span, slice(None), me, n, core)
                out[to, turn * half : (turn + 1) * half] = jnp.concatenate(both, axis=0)
        return c

    lax.fori_loop(0, n // 2, place_rows, 0)


def query_key_kernel(cfg, me_ref, x_ref, *refs):
    n, core, hyper, rows, parts, scale, segment, heads_dev, head_size = cfg
    ins, refs = refs[:4], refs[4:]
    q_ref, k_ref, land_ref, wqk = refs
    me = me_ref[0]
    width = x_ref.shape[1]
    ready(*ins)
    if hyper:
        natural(ins, ((0, wqk.buf.at[0]), (1, wqk.buf.at[1])), me, n, core, rows, width)
    else:
        for unit, piece in enumerate(ins[:2]):
            wqk[unit] = piece[...]
    done(wqk)
    q_ref[...] = (nn(x_ref[...], wqk[0]) * scale).astype(bf16)
    done(q_ref)
    k_ref[...] = (nn(x_ref[...], wqk[1]) * scale).astype(bf16)
    done(k_ref)
    pieces = []
    each = x_ref.shape[0] // (2 * parts)
    for ref in (q_ref, k_ref):
        for at_row in range(2 * parts):
            span = ref[at_row * each : (at_row + 1) * each, :].astype(f32)
            pieces.append(jnp.sum(span, axis=0, keepdims=True) * (1.0 / segment))
    if parts < 2:
        pieces.append(jnp.zeros((8 - 4 * parts, width), f32))
    shared = jnp.concatenate(pieces, axis=0).astype(land_ref.dtype)
    for d in range(n):
        land_ref[d] = shared


def value_kernel(cfg, me_ref, x_ref, *refs):
    n, core, hyper, rows, parts, scale, segment, heads_dev, head_size = cfg
    ins, refs = refs[:4], refs[4:]
    v_ref, toep_ref, peot_ref, gain_ref, wv = refs
    me = me_ref[0]
    width = x_ref.shape[1]
    ready(*ins)
    if hyper:
        natural(ins, ((2, wv),), me, n, core, rows, width)

        def small_pair(pair):
            span = slice(3 * rows, 3 * rows + 8)
            return piece_pair(ins, 0, pair, span, slice(0, GW), me, n, core)

    else:
        wv[...] = ins[2][...]

        def small_pair(pair):
            return ins[3][2 * pair, :, 0:GW], ins[3][2 * pair + 1, :, 0:GW]

    done(wv)
    v_ref[...] = nn(x_ref[...], wv[...]).astype(bf16)
    done(v_ref)
    place = (iota((128, width), 1) % rows == iota((128, width), 0)).astype(bf16)

    def add(d, small, gains):
        inside = iota((8, width), 1) // rows == d
        return gains + jnp.where(inside, nn(small[:, 0:128], place), 0.0)

    def add_pair(pair, gains):
        first, second = small_pair(pair)
        return add(2 * pair + 1, second, add(2 * pair, first, gains))

    gain_ref[...] = lax.fori_loop(0, n // 2, add_pair, jnp.zeros(gain_ref.shape, f32))
    for d in range(head_size):
        taps = small_pair(d // 2)[d % 2].astype(f32)
        for i in range(heads_dev):
            for row, out in ((i, toep_ref), (heads_dev + i, peot_ref)):
                spread = jnp.broadcast_to(taps[row : row + 1, :], (CT, GW))
                spread = pltpu.roll(spread, 0, 1, stride=1, stride_axis=0)
                out[d * heads_dev + i] = spread[:, 0:CE].astype(bf16)


def newton_kernel(heads, me_ref, ql_ref, kl_ref, inv_ref, keep_ref, two_ref):
    unit = lax.rem(me_ref[0], 2 * heads)
    second = unit >= heads
    head = jnp.where(second, unit - heads, unit)
    width = ql_ref.shape[1]
    pick = (iota((width, HD), 0) == iota((width, HD), 1) + head * HD).astype(bf16)

    def mine(ref):
        rows = jnp.where(second, ref[M : 2 * M, :].astype(f32), ref[0:M, :].astype(f32))
        return nn(rows.astype(bf16), pick).astype(bf16)

    query, key = mine(ql_ref), mine(kl_ref)
    score = nt(query, key)
    e = jnp.exp(score - jnp.max(score, axis=1, keepdims=True))
    kernel = e / jnp.sum(e, axis=1, keepdims=True)
    column = jnp.sum(kernel, axis=0, keepdims=True)
    largest = jnp.max(column, axis=1, keepdims=True)
    eye = (iota((M, M), 0) == iota((M, M), 1)).astype(f32)
    z = kernel.T / largest
    two_ref[0] = kernel
    two_ref[1] = column + jnp.zeros_like(kernel)
    two_ref[2] = query.astype(f32)
    two_ref[3] = key.astype(f32)

    def iterate(step, z):
        p = exact(kernel, z)
        a = 7.0 * eye - p
        b = 15.0 * eye - exact(p, a)
        c = 13.0 * eye - exact(p, b)
        for i, value in enumerate((z, p, a, b, c)):
            keep_ref[step, i] = value
        return 0.25 * exact(z, c)

    inv_ref[...] = lax.fori_loop(0, NEWTON, iterate, z)


def newton_back_kernel(
    heads, me_ref, dinv_ref, inv_ref, keep_ref, two_ref, dq_ref, dk_ref
):
    turned = ((0,), (0,))
    across = ((1,), (1,))
    ready(keep_ref)
    kernel = two_ref[0]

    def iterate(i, state):
        dz, dkernel = state
        step = NEWTON - 1 - i
        z, p, a, b, c = (keep_ref[step, k] for k in range(5))
        dc = 0.25 * exact(z, dz, turned)
        db = -exact(p, dc, turned)
        da = -exact(p, db, turned)
        dp = -exact(dc, b, across) - exact(db, a, across) - da
        dkernel = dkernel + exact(dp, z, across)
        return 0.25 * exact(dz, c, across) + exact(kernel, dp, turned), dkernel

    dz, dkernel = lax.fori_loop(0, NEWTON, iterate, (dinv_ref[...], jnp.zeros_like(kernel)))
    column = two_ref[1]
    largest = jnp.max(column[0:1, :], axis=1, keepdims=True)
    dkernel = dkernel + dz.T / largest
    dlargest = -jnp.sum(dz * kernel.T, keepdims=True) / (largest * largest)
    top = (column == largest).astype(f32)
    ties = jnp.sum(top[0:1, :], axis=1, keepdims=True)
    dkernel = dkernel + dlargest * top / ties
    dscore = kernel * (dkernel - jnp.sum(dkernel * kernel, axis=1, keepdims=True))
    dquery = exact(dscore, two_ref[3])
    dkey = exact(dscore, two_ref[2], turned)
    unit = me_ref[0]
    width = dq_ref.shape[2]
    second = lax.rem(unit, 2 * heads) >= heads
    head = jnp.where(second, unit - heads, unit)
    place = (iota((HD, width), 1) == iota((HD, width), 0) + head * HD).astype(f32)
    live = unit < 2 * heads
    for out, value in ((dq_ref, dquery), (dk_ref, dkey)):
        wide = exact(jnp.where(live, value, 0.0), place)
        out[0] = jnp.where(second, 0.0, wide)
        out[1] = jnp.where(second, wide, 0.0)


def score3_kernel(heads, parts, k_ref, v_ref, got_ref, ql_ref, kl_ref, p_ref, out_ref, lands):
    tokens = k_ref.shape[0] // 2
    n = out_ref.shape[0]
    width = k_ref.shape[1]
    ready(got_ref)
    for d in range(n):
        got = got_ref[d].astype(f32)
        for i in range(4):
            lands[i, d * parts : (d + 1) * parts, :] = got[i * parts : (i + 1) * parts]
    for i, out in ((0, ql_ref), (2, kl_ref)):
        both = lands[i : i + 2]
        if n * parts != M:
            both = jnp.sum(both.reshape(2, M, n * parts // M, width), axis=2)
        out[...] = both.reshape(2 * M, width).astype(bf16)
    for u in range(2 * heads, n):
        out_ref[u] = jnp.zeros((SLOT, 128), bf16)
    ready(k_ref, v_ref)
    done(ql_ref, kl_ref)

    @pl.loop(0, 2)
    def _(s):
        for g in range(k_ref.shape[1] // GW):
            lanes = slice(g * GW, (g + 1) * GW)
            rows = aligned(s, tokens)
            land = block_diagonal(ql_ref[aligned(s, M), lanes])
            score = nt(land, k_ref[rows, lanes])
            top = jnp.max(score, axis=1, keepdims=True).astype(bf16).astype(f32)
            e = jnp.exp(score - top)
            total = jnp.sum(e, axis=1, keepdims=True)
            low = e.astype(bf16)
            p_ref[s, g] = low
            part = nn(low, v_ref[rows, lanes])
            high = total.astype(bf16).astype(f32)
            which = iota((GW, 8), 1)
            stats = jnp.where(which == 0, top, 0.0)
            stats = jnp.where(which == 1, high, stats)
            stats = jnp.where(which == 2, total - high, stats).astype(bf16)
            stats = tn(stats, identity(GW))
            for j in range(HP):
                slot = packed(low_lanes(diagonal_half(part, j), j))
                stat = low_lanes(stats[:, 128 * (j // 2) : 128 * (j // 2) + 128], j)
                slot = jnp.concatenate([slot, stat], axis=0)
                out_ref[s * heads + g * HP + j] = slot.astype(bf16)


def combine_kernel(got_ref, inv_ref, out_ref, sum_ref):
    n = got_ref.shape[0]
    half = HD // 2
    ready(got_ref)
    tops = jnp.concatenate([got_ref[d, half : half + 8].astype(f32)[0:1] for d in range(n)], axis=0)
    top = jnp.max(tops, axis=0, keepdims=True)
    weights = jnp.exp(tops - top)
    sums = []
    for d in range(n):
        stat = got_ref[d, half : half + 8].astype(f32)
        sums.append(stat[1:2] + stat[2:3])
    total = jnp.sum(weights * jnp.concatenate(sums, axis=0), axis=0, keepdims=True)
    total = jnp.where(total > 0.0, total, 1.0)
    weights = (weights / total).T
    lane = iota((half, 128), 1)
    acc = jnp.zeros((half, 128), f32)
    for d in range(n):
        by = weights[:, d : d + 1]
        by = jnp.where(lane < HD, by[0:half], by[half:HD])
        acc = acc + by * got_ref[d, 0:half].astype(f32)
    summary = unpacked(acc)
    sum_ref[...] = summary
    mixed = exact(inv_ref[...], summary)
    high = total.astype(bf16).astype(f32)
    slot = jnp.concatenate([packed(mixed), stacked([top, high, total - high])], axis=0)
    slot = slot.astype(bf16)
    for d in range(n):
        out_ref[d] = slot


def fill_extended(ext, ref, low_ref, high_ref, tokens):
    for s in range(2):
        ext[s, 0:REACH, :] = low_ref[s]
        ext[s, REACH : REACH + tokens, :] = ref[s * tokens : (s + 1) * tokens, :]
        ext[s, REACH + tokens : 2 * REACH + tokens, :] = high_ref[s]


def convolve(ext, toep_ref, s, g, tile):
    piece = ext[s, tile * CT : tile * CT + CE, aligned(g, GW)]
    lane = iota((CT, GW), 1) // HD
    out = nn(toep_ref[g * HP], piece)
    for j in range(1, HP):
        out = jnp.where(lane == j, nn(toep_ref[g * HP + j], piece), out)
    return out


def softmax1(land, queries):
    tokens = queries.shape[0]
    score = nt(land, queries).reshape(HP, M, tokens)
    e = jnp.exp(score - jnp.max(score, axis=1, keepdims=True))
    return (e / jnp.sum(e, axis=1, keepdims=True)).reshape(GW, tokens)


def kernel1_kernel(q_ref, v_ref, low_ref, high_ref, kl_ref, toep_ref, conv_ref, k1_ref, ext):
    tokens = q_ref.shape[0] // 2
    fill_extended(ext, v_ref, low_ref, high_ref, tokens)
    ready(q_ref, kl_ref, toep_ref)

    @pl.loop(0, 2)
    def _(s):
        for g in range(q_ref.shape[1] // GW):
            lanes = slice(g * GW, (g + 1) * GW)
            rows = aligned(s, tokens)
            land = block_diagonal(kl_ref[aligned(s, M), lanes])
            k1_ref[s, g] = softmax1(land, q_ref[rows, lanes]).astype(bf16)
            for tile in range(tokens // CT):
                at = pl.ds(pl.multiple_of(s * tokens + tile * CT, CT), CT)
                conv_ref[at, lanes] = convolve(ext, toep_ref, s, g, tile)


def norm(h):
    center = h - jnp.mean(h, axis=1, keepdims=True)
    rstd = lax.rsqrt(jnp.mean(center * center, axis=1, keepdims=True) + EPS)
    return center * rstd, rstd


def norm_back(dx, hat, rstd):
    return rstd * (
        dx - jnp.mean(dx, axis=1, keepdims=True) - hat * jnp.mean(dx * hat, axis=1, keepdims=True)
    )


RT = 128


def row_tiles(total, body):
    def step(i, c):
        body(pl.ds(pl.multiple_of(i * RT, RT), RT))
        return c

    lax.fori_loop(0, total // RT, step, 0, unroll=2)


def layer_kernel(chunks, heads, k1_ref, conv_ref, mixed_ref, x_ref, gain_ref, cot_ref, *refs):
    scratch, refs = refs[-9:], refs[:-9]
    heads_ref, act, du, n1b, dd, db, hat1, rstd1, acc = scratch
    hyper = len(refs) == 7
    weights, refs = (refs[:1], refs[1:]) if hyper else (refs[:3], refs[3:])
    mbd_ref, out_ref, dh1_ref, dheads_ref, gn_ref = refs[:5]
    grads = refs[5:]
    total, width = x_ref.shape
    tokens = total // 2

    if hyper:
        (fetched,) = weights
        all_ref = fetched.buf
        n, _, rows, _ = all_ref.shape
        per = n // chunks

        def w_up(c):
            return all_ref[:, chunks + c].reshape(width, width)

        def w_down(c):
            return all_ref[pl.ds(c * per, per), 0:chunks].reshape(width, width)

        def w_out():
            return all_ref[:, 2 * chunks].reshape(width, width)

        def put_up(c, g):
            all_ref[:, chunks + c] = g.reshape(n, rows, width)

        def put_down(c, g):
            all_ref[pl.ds(c * per, per), 0:chunks] = g.reshape(per, chunks, rows, width)

        def put_out(g):
            all_ref[:, 2 * chunks] = g.reshape(n, rows, width)

        out_ready, up_ready, down_ready = (functools.partial(fetched.ready, i) for i in range(3))
        out_done, up_done, down_done = (functools.partial(grads[0].done, i) for i in range(3))
    else:
        wo_ref, wu_ref, wd_ref = (w.buf for w in weights)
        w_up = lambda c: wu_ref[c]
        w_down = lambda c: wd_ref[c]
        w_out = lambda: wo_ref[...]

        def put_up(c, g):
            wu_ref[c] = g

        def put_down(c, g):
            wd_ref[c] = g

        def put_out(g):
            wo_ref[...] = g

        out_ready, up_ready, down_ready = (w.ready for w in weights)
        out_done, up_done, down_done = (g.done for g in grads)

    ready(k1_ref, conv_ref, mixed_ref)
    down = conv_ref.buf

    @pl.loop(0, 2)
    def _(s):
        for g in range(width // GW):
            lanes = slice(g * GW, (g + 1) * GW)
            span = aligned(s, tokens)
            mbd = block_from_slots(lambda j: mixed_ref[s * heads + g * HP + j, 0 : HD // 2])
            mbd_ref[s, g] = mbd
            heads_ref[span, lanes] = (tn(k1_ref[s, g], mbd) + down[span, lanes]).astype(bf16)

    done(mbd_ref)
    ready(gain_ref)
    g1 = gain_ref[6:7, :]
    g2 = gain_ref[7:8, :]
    gn_ref[...] = jnp.zeros(gn_ref.shape, f32)
    out_ready()
    ready(x_ref)
    down[...] = nn(heads_ref[...], w_out())

    def first(r):
        hat, rstd = norm(x_ref[r, :].astype(f32) + down[r, :])
        hat1[r, :] = hat
        rstd1[r, :] = jnp.broadcast_to(rstd, (RT, 128))
        value = hat * g1
        n1b[r, :] = value.astype(bf16)
        down[r, :] = value

    row_tiles(total, first)
    up_ready()
    down_ready()
    ready(cot_ref)

    @pl.loop(0, chunks)
    def _(c):
        up = nn(n1b[...], w_up(c))
        cdf = 0.5 * (1.0 + lax.erf(up * (0.5**0.5)))
        density = jnp.exp(-0.5 * up * up) * 0.3989422804014327
        value = (up * cdf).astype(bf16)
        act[c] = value
        du[c] = (cdf + up * density).astype(bf16)
        down[...] += nn(value, w_down(c))

    dh2 = dh1_ref.buf

    def second(r):
        hat, rstd = norm(down[r, :])
        out_ref[r, :] = (hat * g2).astype(bf16)
        g = cot_ref[r, :].astype(f32)
        gn_ref[1:2, :] += jnp.sum(g * hat, axis=0, keepdims=True)
        d = norm_back(g * g2, hat, rstd)
        dh2[r, :] = d
        dd[r, :] = d.astype(bf16)

    row_tiles(total, second)
    done(out_ref)

    @pl.loop(0, chunks)
    def _(c):
        part = (nt(dd[...], w_down(c)) * du[c].astype(f32)).astype(bf16)
        du[c] = part
        dh2[...] += nt(part, w_up(c))

    def third(r):
        hat = hat1[r, :]
        d = dh2[r, :]
        gn_ref[0:1, :] += jnp.sum(d * hat, axis=0, keepdims=True)
        d = norm_back(d * g1, hat, rstd1[r, :][:, 0:1])
        dh2[r, :] = d
        db[r, :] = d.astype(bf16)

    row_tiles(total, third)
    done(dh1_ref, gn_ref)
    dheads_ref[...] = nt(db[...], w_out()).astype(bf16)
    done(dheads_ref)

    @pl.loop(0, chunks)
    def _(c):
        acc[...] = tn(act[c], dd[...])
        put_down(c, acc[...].astype(bf16))

    down_done()

    @pl.loop(0, chunks)
    def _(c):
        acc[...] = tn(n1b[...], du[c])
        put_up(c, acc[...].astype(bf16))

    up_done()
    acc[...] = tn(heads_ref[...], db[...])
    put_out(acc[...].astype(bf16))
    out_done()


def attend_back_kernel(heads, dh_ref, k1_ref, mbd_ref, kl_ref, q_ref, dq_ref, dkl_ref, out_ref):
    tokens = q_ref.shape[0] // 2
    n = out_ref.shape[0]
    for u in range(2 * heads, n):
        out_ref[u] = jnp.zeros((HD // 2, 128), bf16)
    mask = block_mask()
    ready(dh_ref, k1_ref, mbd_ref, kl_ref, q_ref)

    @pl.loop(0, 2)
    def _(s):
        for g in range(q_ref.shape[1] // GW):
            lanes = slice(g * GW, (g + 1) * GW)
            rows = aligned(s, tokens)
            dh = dh_ref[rows, lanes]
            land = block_diagonal(kl_ref[aligned(s, M), lanes])
            low = k1_ref[s, g]
            k1 = low.astype(f32)
            dk1 = nt(mbd_ref[s, g], dh)
            row = jnp.sum((k1 * dk1).reshape(HP, M, tokens), axis=1, keepdims=True)
            centered = (dk1.reshape(HP, M, tokens) - row).reshape(GW, tokens)
            ds = (k1 * centered).astype(bf16)
            dq_ref[rows, lanes] = tn(ds, land)
            dland = jnp.where(mask, nn(ds, q_ref[rows, lanes]), 0.0)
            dkl_ref[s, :, lanes] = jnp.sum(dland.reshape(HP, M, GW), axis=0)
            dmixed = nn(low, dh)
            for j in range(HP):
                slot = packed(low_lanes(diagonal_half(dmixed, j), j))
                out_ref[s * heads + g * HP + j] = slot.astype(bf16)


def conv_back_kernel(
    dh_ref, dlow_ref, dhigh_ref, v_ref, low_ref, high_ref, peot_ref, dv_ref, gc_ref, dext, ext, gram
):
    tokens = v_ref.shape[0] // 2
    groups = v_ref.shape[1] // GW
    fill_extended(dext, dh_ref, dlow_ref, dhigh_ref, tokens)
    fill_extended(ext, v_ref, low_ref, high_ref, tokens)
    ready(peot_ref)
    lane = iota((CT, GW), 1) // HD
    ready(dh_ref)
    back = (iota((CT, CT), 0) + iota((CT, CT), 1) == CT - 1).astype(f32)

    @pl.loop(0, groups)
    def _(g):
        lanes = aligned(g, GW)
        gram[...] = jnp.zeros_like(gram)

        @pl.loop(0, 2)
        def _(s):
            for tile in range(tokens // CT):
                at = pl.ds(pl.multiple_of(s * tokens + tile * CT, CT), CT)
                dv_ref[at, lanes] = convolve(dext, peot_ref, s, g, tile)
                dh = dh_ref[at, lanes]
                each = jnp.concatenate(
                    [jnp.where(lane == j, dh, jnp.zeros_like(dh)) for j in range(HP)], axis=0
                )
                gram[:, 0:CE] += nt(each, ext[s, tile * CT : tile * CT + CE, lanes])

        rows = []
        for j in range(HP):
            turned = exact(back, gram[j * CT : (j + 1) * CT, :])
            rolled = pltpu.roll(turned, 0, 1, stride=1, stride_axis=0)
            rows.append(jnp.sum(rolled, axis=0, keepdims=True))
        gc_ref[g] = jnp.concatenate(rows, axis=0)


def owner_back_kernel(got_ref, inv_ref, sum_ref, out_ref, dinv_ref):
    n = got_ref.shape[0]
    ready(got_ref)
    dmixed = unpacked(
        lax.fori_loop(
            0, n, lambda d, a: a + got_ref[d].astype(f32), jnp.zeros((HD // 2, 128), f32)
        )
    )
    dsum = exact(inv_ref[...], dmixed, ((0,), (0,))).astype(bf16).astype(f32)
    ones = jnp.ones((8, 128), f32)
    row = exact(ones, dsum * sum_ref[...], ((1,), (1,)))[0:1]
    row = jnp.concatenate([row, jnp.zeros_like(row)], axis=1)
    high = row.astype(bf16).astype(f32)
    slot = jnp.concatenate([packed(dsum), stacked([high, row - high])], axis=0).astype(bf16)
    for d in range(n):
        out_ref[d] = slot
    done(out_ref)
    dinv_ref[...] = exact(dmixed, sum_ref[...], ((1,), (1,)))


def score3_back_kernel(
    heads, parts, sent_ref, stat_ref, dsum_ref, p_ref, k_ref, v_ref, ql_ref, dq2_ref, dk2_ref,
    dk1_ref, dk_ref, dv_ref, out_ref, dql,
):
    tokens = k_ref.shape[0] // 2
    n = out_ref.shape[0]
    mask = block_mask()
    ready(sent_ref, stat_ref, dsum_ref, p_ref, k_ref, v_ref, ql_ref, dq2_ref)

    @pl.loop(0, 2)
    def _(s):
        for g in range(k_ref.shape[1] // GW):
            lanes = slice(g * GW, (g + 1) * GW)
            rows = aligned(s, tokens)
            factors, terms = [], []
            for j in range(HP):
                u = s * heads + g * HP + j
                stat_rows = slice(HD // 2, HD // 2 + 8)
                local = sent_ref[u, stat_rows].astype(f32)[0:1]
                stat = stat_ref[u, stat_rows].astype(f32)
                factors.append(jnp.exp(local - stat[0:1]) / (stat[1:2] + stat[2:3]))
                d = dsum_ref[u, stat_rows].astype(f32)
                terms.append(d[0:1] + d[1:2])

            def joined(parts):
                lane = iota((1, 128), 1)
                halves = [
                    jnp.where(lane < HD, parts[j], pltpu.roll(parts[j + 1], HD, 1))
                    for j in range(0, HP, 2)
                ]
                return jnp.concatenate(halves, axis=1)

            rows_in = []
            for value in (joined(factors), joined(terms)):
                for _ in range(3):
                    term = value.astype(bf16).astype(f32)
                    rows_in.append(term)
                    value = value - term
            columns = nt(identity(GW), stacked(rows_in).astype(bf16))
            factor = columns[:, 0:1] + columns[:, 1:2] + columns[:, 2:3]
            term = columns[:, 3:4] + columns[:, 4:5] + columns[:, 5:6]
            k3 = p_ref[s, g].astype(f32) * factor
            dbd = block_from_slots(lambda j: dsum_ref[s * heads + g * HP + j, 0 : HD // 2])
            dk3 = nt(dbd, v_ref[rows, lanes])
            ds = (k3 * (dk3 - term)).astype(bf16)
            dland = jnp.where(mask, nn(ds, k_ref[rows, lanes]), 0.0)
            dql[s, :, lanes] = jnp.sum(dland.reshape(HP, M, GW), axis=0) + dq2_ref[s, :, lanes]
            land = block_diagonal(ql_ref[aligned(s, M), lanes])
            dk_ref[rows, lanes] = tn(ds, land)
            dv_ref[rows, lanes] = tn(k3.astype(bf16), dbd)
    for d in range(n):
        first = d * parts * M // (n * parts)
        span = slice(first, first + parts)
        pieces = [dql[0, span, :], dql[1, span, :]]
        pieces += [dk2_ref[s, span, :] + dk1_ref[s, span, :] for s in range(2)]
        if parts < 2:
            pieces.append(jnp.zeros((8 - 4 * parts, dql.shape[2]), f32))
        out_ref[d] = jnp.concatenate(pieces, axis=0).astype(bf16)


def two_terms(x):
    high = x.astype(bf16)
    return high, (x - high.astype(f32)).astype(bf16)


def final_kernel(
    cfg, me_ref, x_ref, dv3_ref, dvc_ref, dk3_ref, dq1_ref, wv, wqk, dh1_ref,
    dx_ref, sums_ref, gqk_ref, *refs
):
    n, core, hyper, rows, parts, scale, segment = cfg
    outs, acc, low, dv = refs[:-3], *refs[-3:]
    tokens = x_ref.shape[0] // 2
    each = tokens // parts
    dv[...] = (dvc_ref[...] + dv3_ref[...]).astype(bf16)
    acc[...] = tn(x_ref[...], dv[...])
    if hyper:
        emit(acc, 0, rows, rows, outs[0], outs[1], 0, me_ref[0], n, core, 2)
    else:
        outs[0][...] = acc[...]
    done(*outs)
    for s in range(2):
        for l in range(parts):
            span = slice(s * tokens + l * each, s * tokens + (l + 1) * each)
            at = s * parts + l
            sums_ref[at : at + 1, :] = jnp.sum(
                x_ref[span, :].astype(f32), axis=0, keepdims=True
            )
    done(sums_ref)
    low[1] = dk3_ref[...].astype(bf16)
    low[0] = dq1_ref[...].astype(bf16)
    ready(wqk, wv, dh1_ref)
    acc[...] = dh1_ref[...] + nt(dv[...], wv[...])

    @pl.loop(0, 2)
    def _(t):
        gqk_ref[t] = tn(x_ref[...], low[t]) * scale
        acc[...] += nt(low[t], wqk[t]) * scale

    dx_ref[...] = acc[...]


def landmark_sums(got_ref, factor):
    ready(got_ref)
    n, _, width = got_ref.shape
    zero = jnp.zeros((8, width), f32)
    return factor * lax.fori_loop(0, n, lambda d, a: a + got_ref[d].astype(f32), zero)


def landmark_kernel(cfg, me_ref, got_ref, sums_ref, gqk_ref, small_ref, *refs):
    n, core, hyper, rows, parts, scale, segment = cfg
    outs, acc = refs[:-1], refs[-1]
    me = me_ref[0]
    count = 2 * parts
    land = landmark_sums(got_ref, scale / segment)
    s_high, s_low = two_terms(sums_ref[0:count, :])
    left = jnp.concatenate([s_high, s_low, s_high], axis=0)
    for turn, base in enumerate((0, count)):
        high, low = two_terms(land[base : base + count, :])
        acc[...] = gqk_ref[turn] + tn(left, jnp.concatenate([high, high, low], axis=0))
        if hyper:
            keep, send = outs[2 * turn : 2 * turn + 2]
            emit(acc, 0, rows, rows, keep, send, 0, me, n, core, turn)
        else:
            outs[turn][...] = acc[...]
    if hyper:
        ready(small_ref)
        mine = me & 1
        span = slice(rows, rows + 8)

        def step(i, c):
            slot = scatter_slot(jnp.bitwise_xor(me - mine, 2 * i), n, core, 0)
            outs[0][slot, span, 0:GW] = small_ref[2 * i + mine]
            outs[1][slot, span, 0:GW] = small_ref[2 * i + 1 - mine]
            return c

        lax.fori_loop(0, n // 2, step, 0)


def tokens_kernel(cfg, got_ref, wqk, dx_ref, out_ref):
    n, core, hyper, rows, parts, scale, segment = cfg
    tokens = dx_ref.shape[0] // 2
    each = tokens // parts
    count = 2 * parts
    land = landmark_sums(got_ref, scale / segment)
    change = 0.0
    for turn, base in enumerate((0, count)):
        both = nt(jnp.concatenate(two_terms(land[base : base + count, :]), axis=0), wqk[turn])
        change = change + both[0:count] + both[count : 2 * count]
    for s in range(2):
        for l in range(parts):
            span = slice(s * tokens + l * each, s * tokens + (l + 1) * each)
            at = s * parts + l
            out_ref[span, :] = (dx_ref[span, :] + change[at : at + 1, :]).astype(bf16)


def merge_kernel(counts, *refs):
    ready(*refs[: 2 * sum(counts)])
    outs = refs[2 * sum(counts) :]
    at = 0
    for job, count in enumerate(counts):
        ins = refs[2 * at : 2 * (at + count)]
        at += count
        row = 0
        kept, sent = outs[2 * job], outs[2 * job + 1]
        for keep, got in zip(ins[0::2], ins[1::2]):
            span = slice(row, row + keep.shape[1])
            row += keep.shape[1]
            half = keep.shape[0] // 2

            @pl.loop(0, half)
            def _(j):
                kept[j, span] = keep[j].astype(f32) + got[j].astype(f32)
                sent[j, span] = (
                    keep[half + j].astype(f32) + got[half + j].astype(f32)
                ).astype(bf16)

        done(sent)


def last_kernel(splits, *refs):
    ins, outs = refs[: 2 * len(splits)], list(refs[2 * len(splits) :])
    for i, split in enumerate(splits):
        keep, got = ins[2 * i], ins[2 * i + 1]
        row = 0
        for count in split:
            span = slice(row, row + count)
            outs.pop(0)[...] = keep[0, span].astype(f32) + got[0, span].astype(f32)
            row += count


def unpack_kernel(chunks, got_ref, up_ref, down_ref, out_ref):
    out_ref[...] = got_ref[2 * chunks].astype(f32)
    rows, width = got_ref.shape[1:]
    for c in range(chunks):
        up_ref[:, c * width : (c + 1) * width] = got_ref[chunks + c].astype(f32)
        down_ref[c * rows : (c + 1) * rows, :] = got_ref[c].astype(f32)


def exchange(x):
    return lax.all_to_all(x, AX, 0, 0, tiled=True)


def per_device(
    tokens, w_query, w_key, w_value, w_out, conv_kernel, norm1_gain, w_up, w_down, norm2_gain, cotangent
):
    sequences, held, width = tokens.shape
    blk, head = lax.axis_size("blk"), lax.axis_size("head")
    n = blk * head
    heads_dev = conv_kernel.shape[0]
    heads = heads_dev * head
    rows = w_query.shape[0]
    hidden = w_up.shape[1]
    chunks = hidden // width
    segment = held * n // M
    parts = max(1, held // segment)
    groups = width // GW
    hyper = rows % 8 == 0 and n == 32
    core = 0 if n <= 32 else head.bit_length() - 1
    scale = HD**-0.25
    total = sequences * held
    me = (lax.axis_index("blk") * head + lax.axis_index("head")).astype(jnp.int32)
    me = me.reshape(1)
    x = tokens.reshape(total, width)

    if hyper:
        now, later = vmem_call(
            functools.partial(prepare_kernel, chunks),
            (
                shape_of((3 * rows + 8, width), bf16),
                shape_of(((2 * chunks + 1) * rows, width), bf16),
            ),
            (
                conv_kernel, jnp.stack([norm1_gain, norm2_gain]),
                w_query, w_key, w_value, w_out, w_up, w_down,
            ),
            scratch=[pltpu.VMEM((8, 128), f32)],
        )
        pieces, mid = cube_gather(now, n, core)
        later, _ = lax.optimization_barrier((later, mid))
        later = lax.all_gather(later, AX, axis=0).reshape(n, 2 * chunks + 1, rows, width)
        weights = (later,)
        weight_parts = {
            6: [
                (slice(None), slice(2 * chunks, None)),
                (slice(None), slice(chunks, 2 * chunks)),
                (slice(None), slice(0, chunks)),
            ]
        }
    else:
        taps = jnp.concatenate([conv_kernel, conv_kernel[:, ::-1]], axis=0)
        both = jnp.stack([norm1_gain, norm2_gain])
        extras = jnp.concatenate(
            [
                jnp.pad(taps, ((0, 0), (0, width - KW))),
                jnp.pad(both, ((0, 0), (0, width - rows))),
            ],
            axis=0,
        )
        pieces = [
            lax.all_gather(w, AX, axis=0, tiled=True) for w in (w_query, w_key, w_value)
        ] + [lax.all_gather(extras, AX, axis=0)]
        wo = lax.all_gather(w_out, AX, axis=0, tiled=True)
        wu = lax.all_gather(w_up, AX, axis=0, tiled=True)
        wu = wu.reshape(width, chunks, width).transpose(1, 0, 2)
        wd = lax.all_gather(w_down, AX, axis=0, tiled=True).reshape(chunks, width, width)
        weights = (wo, wu, wd)
        weight_parts = None

    cfg = (n, core, hyper, rows, parts, scale, segment, heads_dev, head)
    square_low = shape_of((total, width), bf16)
    square_full = shape_of((total, width), f32)
    weight = shape_of((width, width), bf16)
    weight_full = shape_of((width, width), f32)
    toeplitz = shape_of((heads, CT, CE), bf16)
    queries, keys, lands, wqk = vmem_call(
        functools.partial(query_key_kernel, cfg),
        (
            square_low, square_low, shape_of((n, 8, width), bf16 if held >= segment else f32),
            shape_of((2, width, width), bf16),
        ),
        (me, x, *pieces),
        scalars=1,
    )
    lands = exchange(lands)
    values, toep, peot, gains, wv = vmem_call(
        functools.partial(value_kernel, cfg),
        (square_low, toeplitz, toeplitz, shape_of((8, width), f32), weight),
        (me, x, *pieces),
        scalars=1,
    )
    lands, values = lax.optimization_barrier((lands, values))
    ahead = [(i, i + 1) for i in range(n - 1)]
    behind = [(i + 1, i) for i in range(n - 1)]

    def halo(y):
        y = y.reshape(sequences, held, width)
        low = lax.ppermute(y[:, held - REACH :], AX, ahead)
        high = lax.ppermute(y[:, :REACH], AX, behind)
        return low, high

    matrix = shape_of((M, M), f32)
    slots = shape_of((n, SLOT, 128), bf16)
    half_slots = shape_of((n, HD // 2, 128), bf16)
    land = shape_of((2 * M, width), bf16)
    q_land, k_land, p3, sent = vmem_call(
        functools.partial(score3_kernel, heads, parts),
        (land, land, shape_of((2, groups, GW, held), bf16), slots),
        (keys, values, lands),
        scratch=[pltpu.VMEM((4, n * parts, width), f32)],
    )
    got_sums = exchange(sent)
    inverse, newton_keep, kernel_two = vmem_call(
        functools.partial(newton_kernel, heads),
        (matrix, shape_of((NEWTON, 5, M, M), f32), shape_of((4, M, M), f32)),
        (me, q_land, k_land),
        scalars=1,
    )
    v_low, v_high = halo(values)
    got_sums, v_low, v_high = lax.optimization_barrier((got_sums, v_low, v_high))
    stat, summary = vmem_call(
        combine_kernel, (slots, shape_of((M, 128), f32)), (got_sums, inverse)
    )
    stat = exchange(stat)
    convolved, k1 = vmem_call(
        kernel1_kernel,
        (square_full, shape_of((2, groups, GW, held), bf16)),
        (queries, values, v_low, v_high, k_land, toep),
        scratch=[pltpu.VMEM((2, held + 2 * REACH, width), bf16)],
    )
    stat, k1 = lax.optimization_barrier((stat, k1))
    wide = pltpu.VMEM((chunks, total, width), bf16)
    low_buffer = pltpu.VMEM((total, width), bf16)
    if hyper:
        grad_shapes = [shape_of((n, 2 * chunks + 1, rows, width), bf16)]
        grad_parts, lent = {5: weight_parts[6]}, {5: 6}
    else:
        grad_shapes = [shape_of(w.shape, bf16) for w in weights]
        grad_parts, lent = None, {5: 6, 6: 7, 7: 8}
    mbd, layer_out, d_h1, d_heads, gain_sums, *grads = vmem_call(
        functools.partial(layer_kernel, chunks, heads),
        [
            shape_of((2, groups, GW, GW), bf16), square_low, square_full, square_low,
            shape_of((8, width), f32),
        ]
        + grad_shapes,
        (k1, convolved, stat, x, gains, cotangent.reshape(total, width), *weights),
        scratch=[
            low_buffer, wide, wide, low_buffer, low_buffer, low_buffer,
            pltpu.VMEM((total, width), f32),
            pltpu.VMEM((total, 128), f32),
            pltpu.VMEM((width, width), f32),
        ],
        parts=weight_parts,
        out_parts=grad_parts,
        lent=lent,
    )
    d_low, d_high = halo(d_heads)
    spread = shape_of((2, M, width), f32)
    d_q1, d_kl1, sent_back = vmem_call(
        functools.partial(attend_back_kernel, heads),
        (square_full, spread, half_slots),
        (d_heads, k1, mbd, k_land, queries),
    )
    got_back = exchange(sent_back)
    extended = pltpu.VMEM((2, held + 2 * REACH, width), bf16)
    d_vc, conv_sums = vmem_call(
        conv_back_kernel,
        (square_full, shape_of((groups, HP, GW), f32)),
        (d_heads, d_low, d_high, values, v_low, v_high, peot),
        scratch=[extended, extended, pltpu.VMEM((HP * CT, GW), f32)],
    )
    got_back, d_vc = lax.optimization_barrier((got_back, d_vc))
    d_sum, d_inverse = vmem_call(
        owner_back_kernel, (slots, matrix), (got_back, inverse, summary)
    )
    d_sum = exchange(d_sum)
    d_ql2, d_kl2 = vmem_call(
        functools.partial(newton_back_kernel, heads),
        (spread, spread),
        (me, d_inverse, inverse, newton_keep, kernel_two),
        scalars=1,
    )
    d_k3, d_v3, sent_land = vmem_call(
        functools.partial(score3_back_kernel, heads, parts),
        (square_full, square_full, shape_of((n, 8, width), bf16)),
        (sent, stat, d_sum, p3, keys, values, q_land, d_ql2, d_kl2, d_kl1),
        scratch=[pltpu.VMEM((2, M, width), f32)],
    )
    got_land = exchange(sent_land)
    if hyper:
        early = lax.psum_scatter(grads[0], AX, scatter_dimension=0, tiled=False)
    small = gain_sums[0:2].reshape(2, n, rows).transpose(1, 0, 2).reshape(n, 2 * rows)
    tap_sums = conv_sums[:, :, CT - 1 : CT - 1 + KW].reshape(head, heads_dev * KW)
    tap_sums = jnp.broadcast_to(tap_sums[None], (blk, head, heads_dev * KW)).reshape(n, -1)
    small = jnp.concatenate([small, tap_sums], axis=1)
    small = jnp.pad(small, ((0, 0), (0, GW - small.shape[1])))
    extra_rows = (8, 0, 0)
    if hyper:
        slot_shapes = [
            [shape_of((n // 2, rows + extra, width), bf16)] * 2 for extra in extra_rows
        ]
    else:
        slot_shapes = [[shape_of((width, width), f32)]] * 3
    final_cfg = (n, core, hyper, rows, parts, scale, segment)
    d_x, x_sums, g_both, *value_slots = vmem_call(
        functools.partial(final_kernel, final_cfg),
        [square_full, shape_of((8, width), f32), shape_of((2, width, width), f32)] + slot_shapes[2],
        (me, x, d_v3, d_vc, d_k3, d_q1, wv, wqk, d_h1),
        scalars=1,
        scratch=[
            pltpu.VMEM((width, width), f32),
            pltpu.VMEM((2, total, width), bf16),
            pltpu.VMEM((total, width), bf16),
        ],
    )
    projections = vmem_call(
        functools.partial(landmark_kernel, final_cfg),
        slot_shapes[0] + slot_shapes[1],
        (
            me, got_land, x_sums, g_both,
            jnp.broadcast_to(small[:, None], (n, 8, GW)).astype(bf16),
        ),
        scalars=1,
        scratch=[pltpu.VMEM((width, width), f32)],
    )
    projections = list(projections) + value_slots
    after, _ = lax.optimization_barrier((got_land, projections))
    d_tokens = vmem_call(
        functools.partial(tokens_kernel, final_cfg), square_low, (after, wqk, d_x)
    )
    d_tokens = d_tokens.reshape(tokens.shape)
    if hyper:
        grad_up, grad_down, grad_out = vmem_call(
            functools.partial(unpack_kernel, chunks),
            (
                shape_of((rows, hidden), f32), shape_of((chunks * rows, width), f32),
                shape_of((rows, width), f32),
            ),
            (early,),
        )
        grad_query, small, grad_key, grad_value = cube_scatter(
            [
                [(projections[0], projections[1])],
                [(projections[2], projections[3])],
                [(projections[4], projections[5])],
            ],
            ((rows, 8, rows), (rows,)),
            n,
            core,
        )
        small = small[0]
    else:

        def scatter(g):
            return lax.psum_scatter(g, AX, scatter_dimension=0, tiled=True)

        grad_out = scatter(grads[0].astype(f32))
        grad_up = scatter(grads[1].astype(f32).transpose(1, 0, 2).reshape(width, hidden))
        grad_down = scatter(grads[2].astype(f32).reshape(hidden, width))
        grad_query, grad_key, grad_value = (scatter(g) for g in projections)
        small = scatter(small)[0]
    return (
        layer_out.reshape(tokens.shape),
        d_tokens,
        grad_query,
        grad_key,
        grad_value,
        grad_out,
        small[2 * rows : 2 * rows + heads_dev * KW].reshape(heads_dev, KW),
        small[:rows],
        grad_up,
        grad_down,
        small[rows : 2 * rows],
    )


def solution(mesh):
    lined = P(None, AX, None)
    rowed = P(AX, None)
    gain = P(AX)
    taps = P("head", None)
    in_specs = (lined, rowed, rowed, rowed, rowed, taps, gain, rowed, rowed, gain, lined)
    out_specs = (lined, lined, rowed, rowed, rowed, rowed, taps, gain, rowed, rowed, gain)
    return jax.shard_map(
        per_device, mesh=mesh, in_specs=in_specs, out_specs=out_specs, check_vma=False
    )
```

```python
import functools

import jax
import jax.numpy as jnp
from jax import lax
from jax.experimental import pallas as pl
from jax.experimental.pallas import tpu as pltpu
from jax.sharding import PartitionSpec as P

HD = 64
M = 64
KW = 33
NEWTON = 6
REACH = KW // 2
AX = ("blk", "head")
EPS = 1e-05
GW = 256
HP = GW // HD
CT = 128
CE = CT + 2 * REACH

bf16 = jnp.bfloat16
f32 = jnp.float32
HIGHEST = lax.Precision.HIGHEST


def nn(a, b):
    return lax.dot_general(a, b, (((1,), (0,)), ((), ())), preferred_element_type=f32)


def nt(a, b):
    return lax.dot_general(a, b, (((1,), (1,)), ((), ())), preferred_element_type=f32)


def tn(a, b):
    return lax.dot_general(a, b, (((0,), (0,)), ((), ())), preferred_element_type=f32)


def exact(a, b, dims=((1,), (0,))):
    return lax.dot_general(a, b, (dims, ((), ())), preferred_element_type=f32, precision=HIGHEST)


def iota(shape, dim):
    return lax.broadcasted_iota(jnp.int32, shape, dim)


class Fetched:
    def __init__(self, source, buf, sems, parts):
        self.buf, self.shape, self.dtype = buf, buf.shape, buf.dtype
        self.copies = [
            pltpu.make_async_copy(source.at[part], buf.at[part], sem)
            for part, sem in zip(parts, sems)
        ]
        self.waiting = list(range(len(parts)))
        for copy in self.copies:
            copy.start()

    def ready(self, *which):
        for i in which or tuple(self.waiting):
            if i in self.waiting:
                self.copies[i].wait()
                self.waiting.remove(i)

    def __getitem__(self, index):
        self.ready()
        return self.buf[index]


class Stored:
    def __init__(self, target, buf, sems, parts):
        self.buf, self.shape, self.dtype = buf, buf.shape, buf.dtype
        self.copies = [
            pltpu.make_async_copy(buf.at[part], target.at[part], sem)
            for part, sem in zip(parts, sems)
        ]
        self.left = list(range(len(parts)))

    def done(self, *which):
        for i in which or tuple(self.left):
            if i in self.left:
                self.copies[i].start()
                self.left.remove(i)

    def __getitem__(self, index):
        return self.buf[index]

    def __setitem__(self, index, value):
        self.buf[index] = value


def ready(*refs):
    for ref in refs:
        if isinstance(ref, Fetched):
            ref.ready()


def done(*refs):
    for ref in refs:
        if isinstance(ref, Stored):
            ref.done()


def resident_call(kernel, outs, args):
    vmem = pl.BlockSpec(memory_space=pltpu.VMEM)
    return pl.pallas_call(
        kernel,
        out_shape=outs,
        in_specs=[vmem] * len(args),
        out_specs=jax.tree.map(lambda _: vmem, outs),
        compiler_params=pltpu.CompilerParams(vmem_limit_bytes=8 << 20),
    )(*args)


def vmem_call(kernel, outs, args, scalars=0, scratch=(), parts=None, out_parts=None, lent=None):
    lent = lent or {}
    parts, out_parts = parts or {}, out_parts or {}
    arrays = args[scalars:]
    whole = [(slice(None),)]
    pieces = [parts.get(i, whole) for i in range(len(arrays))]
    results = jax.tree.leaves(outs)
    own_results = [r for i, r in enumerate(results) if i not in lent]
    buffers = [pltpu.VMEM(a.shape, a.dtype) for a in [*arrays, *own_results]]
    out_pieces = [out_parts.get(i, whole) for i in range(len(results))]
    semaphores = pltpu.SemaphoreType.DMA((sum(len(p) for p in pieces + out_pieces),))

    def run(*refs):
        refs = list(refs)
        take = lambda k: [refs.pop(0) for _ in range(k)]
        ins, sources, targets = take(scalars), take(len(arrays)), take(len(results))
        kept, in_bufs, own_bufs = take(len(scratch)), take(len(arrays)), take(len(own_results))
        out_bufs = [
            in_bufs[lent[i]] if i in lent else own_bufs.pop(0) for i in range(len(results))
        ]
        (sems,) = refs
        free = iter(range(sum(len(p) for p in pieces + out_pieces)))
        own = lambda piece: [sems.at[next(free)] for _ in piece]
        for source, buf, piece in zip(sources, in_bufs, pieces):
            ins.append(Fetched(source, buf, own(piece), piece))
        stored = [
            Stored(target, buf, own(piece), piece)
            for target, buf, piece in zip(targets, out_bufs, out_pieces)
        ]
        kernel(*ins, *stored, *kept)
        ready(*ins)
        done(*stored)
        for ref in stored:
            for copy in ref.copies:
                copy.wait()

    hbm = pl.BlockSpec(memory_space=pl.ANY)
    return pl.pallas_call(
        run,
        out_shape=outs,
        in_specs=[pl.BlockSpec(memory_space=pltpu.SMEM)] * scalars + [hbm] * len(arrays),
        out_specs=jax.tree.map(lambda _: hbm, outs),
        scratch_shapes=list(scratch) + buffers + [semaphores],
        compiler_params=pltpu.CompilerParams(vmem_limit_bytes=60 << 20),
    )(*args)


def shape_of(dims, dtype):
    return jax.ShapeDtypeStruct(tuple(dims), dtype)


def cube_masks(n):
    masks = [1 << b for b in range(n.bit_length() - 1)]
    if len(masks) >= 2:
        masks[-1] |= masks[-2]
    return masks


def coefficients(v, n):
    bits = [(v >> b) & 1 for b in range(n.bit_length() - 1)]
    if len(bits) >= 2:
        bits[-2] = bits[-2] ^ bits[-1]
    return bits


def scatter_order(n, core, turn):
    rest = [b for b in range(n.bit_length() - 1) if b != core]
    return (rest, [rest[1], rest[0], *rest[2:]], [*rest[2:], *rest[:2]])[turn]


def gather_order(n, core, turn):
    return list(reversed(scatter_order(n, core, turn)))


def swap(x, n, dim):
    mask = cube_masks(n)[dim]
    return lax.ppermute(x, AX, [(i, i ^ mask) for i in range(n)])


def gather_slot(v, n, core, turn):
    bits = coefficients(v, n)
    slot = 0
    for place, dim in enumerate(gather_order(n, core, turn)):
        slot = slot + (bits[dim] << place)
    return slot


def scatter_slot(v, n, core, turn):
    bits = coefficients(v, n)
    slot = 0
    for place, dim in enumerate(reversed(scatter_order(n, core, turn))):
        slot = slot + (bits[dim] << place)
    return slot


def cube_gather(piece, n, core):
    buf = piece[None]
    first, second = gather_order(n, core, 0), gather_order(n, core, 1)
    mid = None
    for dim in first[:-2]:
        buf = jnp.concatenate([buf, swap(buf, n, dim)], axis=0)
        mid = buf if mid is None else mid
    half = piece.shape[1] // 2
    bufs = [buf[:, :, :half], buf[:, :, half:]]
    for dims in zip(first[-2:], second[-2:]):
        got = [swap(x, n, dim) for x, dim in zip(bufs, dims)]
        bufs = [jnp.concatenate(pair, axis=0) for pair in zip(bufs, got)]
    return bufs + [swap(x, n, core) for x in bufs], mid


def merged(jobs, call):
    shapes = []
    for pairs in jobs:
        slots = pairs[0][0].shape[0]
        joint = (sum(k.shape[1] for k, _ in pairs), pairs[0][0].shape[2])
        shapes += [shape_of((slots // 2,) + joint, t) for t in (f32, bf16)]
    args = [x for pairs in jobs for pair in pairs for x in pair]
    kernel = functools.partial(merge_kernel, [len(pairs) for pairs in jobs])
    outs = call(kernel, shapes, args)
    return list(zip(outs[0::2], outs[1::2]))


def cube_scatter(jobs, splits, n, core):
    orders = [[core, *scatter_order(n, core, turn)] for turn in range(len(jobs))]
    jobs = [[(k, swap(s, n, core)) for k, s in job] for job in jobs]
    for step in range(1, len(orders[0])):
        state = merged(jobs, vmem_call if step == 1 else resident_call)
        if step == 3:
            orders = orders[:1] + orders[2:]
        jobs = [[(k, swap(s, n, o[step]))] for (k, s), o in zip(state, orders)]
        if step == 2:
            jobs = [jobs[0] + jobs[1]] + jobs[2:]
    width = jobs[0][0][0].shape[2]
    shapes = [shape_of((count, width), f32) for split in splits for count in split]
    args = [x for pairs in jobs for pair in pairs for x in pair]
    return resident_call(functools.partial(last_kernel, splits), shapes, args)


def emit(acc, first_row, rows, stride, keep, send, rows_at, me, n, core, turn, count=None, first=0):
    count = n if count is None else count
    mine = me & 1
    span = slice(rows_at, rows_at + rows)

    def step(i, c):
        d = 2 * i
        slot = scatter_slot(jnp.bitwise_xor(me - mine, first + d), n, core, turn)
        low = pl.multiple_of(first_row + (d + mine) * stride, 8)
        high = pl.multiple_of(first_row + (d + 1 - mine) * stride, 8)
        keep[slot, span, :] = acc[pl.ds(low, rows), :].astype(bf16)
        send[slot, span, :] = acc[pl.ds(high, rows), :].astype(bf16)
        return c

    lax.fori_loop(0, count // 2, step, 0)


def aligned(i, size):
    return pl.ds(pl.multiple_of(i * size, size), size)


def block_mask():
    return (iota((GW, GW), 0) // HD) == (iota((GW, GW), 1) // HD)


def block_diagonal(x):
    wide = jnp.concatenate([x] * HP, axis=0)
    return jnp.where(block_mask(), wide, jnp.zeros_like(wide))


def diagonal_half(x, j):
    return x[j * HD : (j + 1) * HD, 128 * (j // 2) : 128 * (j // 2) + 128]


def low_lanes(x, j):
    return pltpu.roll(x, HD, 1) if j % 2 else x


def high_lanes(x, j):
    return x if j % 2 else pltpu.roll(x, HD, 1)


SLOT = HD // 2 + 8


def packed(x):
    half = HD // 2
    lane = iota((half, 128), 1)
    return jnp.where(lane < HD, x[0:half], pltpu.roll(x[half:HD], HD, 1))


def unpacked(x):
    half = HD // 2
    both = jnp.concatenate([x[0:half], pltpu.roll(x[0:half], HD, 1)], axis=0)
    return jnp.where(iota((HD, 128), 1) < HD, both, 0.0)


def stacked(rows, height=8):
    rows = list(rows) + [jnp.zeros_like(rows[0])] * (height - len(rows))
    return jnp.concatenate(rows, axis=0)


def identity(size):
    return (iota((size, size), 0) == iota((size, size), 1)).astype(bf16)


def block_from_slots(read):
    rows = []
    for j in range(HP):
        half = unpacked(read(j).astype(f32))
        if j % 2:
            half = pltpu.roll(half, HD, 1)
        zero = jnp.zeros_like(half)
        rows.append(jnp.concatenate([half, zero] if j < 2 else [zero, half], axis=1))
    return jnp.concatenate(rows, axis=0).astype(bf16)


def prepare_kernel(chunks, taps_ref, gains_ref, wq, wk, wv, wo, wu, wd, now_ref, later_ref, ext):
    rows, width = wq.shape
    heads_dev, reach = taps_ref.shape
    ext[...] = jnp.zeros_like(ext)
    ext[0:heads_dev, 0:reach] = taps_ref[...].astype(f32)
    back = (iota((128, 128), 0) + iota((128, 128), 1) == KW - 1).astype(bf16)
    turned = nn(ext[...].astype(bf16), back)
    ext[heads_dev : 2 * heads_dev, :] = turned[0:heads_dev]
    ext[6:8, 0:rows] = gains_ref[...].astype(f32)
    for i, w in enumerate((wq, wk, wv)):
        now_ref[i * rows : (i + 1) * rows, :] = w[...]
    now_ref[3 * rows : 3 * rows + 8, 0:128] = ext[...].astype(bf16)
    now_ref[3 * rows : 3 * rows + 8, 128:] = jnp.zeros((8, width - 128), bf16)
    done(now_ref)
    later_ref[0 : chunks * rows, :] = wd[...]
    for k in range(chunks):
        at = (chunks + k) * rows
        later_ref[at : at + rows, :] = wu[:, k * width : (k + 1) * width]
    later_ref[2 * chunks * rows : (2 * chunks + 1) * rows, :] = wo[...]


def piece_pair(ins, turn, pair, span, lanes, me, n, core):
    mine = me & 1
    slot = gather_slot(jnp.bitwise_xor(me - mine, 2 * pair), n, core, turn)
    own = ins[turn][slot, span, lanes]
    other = ins[2 + turn][slot, span, lanes]
    return jnp.where(mine == 0, own, other), jnp.where(mine == 0, other, own)


def natural(ins, units, me, n, core, rows, width):
    half = width // 2

    def place_rows(pair, c):
        to = pl.ds(pl.multiple_of(2 * rows * pair, 16), 2 * rows)
        for turn in range(2):
            for unit, out in units:
                span = slice(unit * rows, (unit + 1) * rows)
                both = piece_pair(ins, turn, pair, span, slice(None), me, n, core)
                out[to, turn * half : (turn + 1) * half] = jnp.concatenate(both, axis=0)
        return c

    lax.fori_loop(0, n // 2, place_rows, 0)


def query_key_kernel(cfg, me_ref, *refs):
    n, core, hyper, rows, parts, scale, segment, heads_dev, head_size = cfg
    ins, x_ref, refs = refs[:4], refs[4], refs[5:]
    q_ref, k_ref, land_ref, wqk = refs
    me = me_ref[0]
    width = x_ref.shape[1]
    if hyper:
        for ref in ins:
            ref.ready(0)
        bufs = [ref.buf for ref in ins]
        natural(bufs, ((0, wqk.buf.at[0]), (1, wqk.buf.at[1])), me, n, core, rows, width)
    else:
        for unit, piece in enumerate(ins[:2]):
            wqk[unit] = piece[...]
    done(wqk)
    q_ref[...] = (nn(x_ref[...], wqk[0]) * scale).astype(bf16)
    done(q_ref)
    k_ref[...] = (nn(x_ref[...], wqk[1]) * scale).astype(bf16)
    done(k_ref)
    pieces = []
    each = x_ref.shape[0] // (2 * parts)
    for ref in (q_ref, k_ref):
        for at_row in range(2 * parts):
            span = ref[at_row * each : (at_row + 1) * each, :].astype(f32)
            pieces.append(jnp.sum(span, axis=0, keepdims=True) * (1.0 / segment))
    if parts < 2:
        pieces.append(jnp.zeros((8 - 4 * parts, width), f32))
    shared = jnp.concatenate(pieces, axis=0).astype(land_ref.dtype)
    for d in range(n):
        land_ref[d] = shared


def value_kernel(cfg, me_ref, x_ref, *refs):
    n, core, hyper, rows, parts, scale, segment, heads_dev, head_size = cfg
    ins, refs = refs[:4], refs[4:]
    v_ref, toep_ref, peot_ref, gain_ref, wv = refs
    me = me_ref[0]
    width = x_ref.shape[1]
    ready(*ins)
    if hyper:
        natural(ins, ((2, wv),), me, n, core, rows, width)

        def small_pair(pair):
            span = slice(3 * rows, 3 * rows + 8)
            return piece_pair(ins, 0, pair, span, slice(0, GW), me, n, core)

    else:
        wv[...] = ins[2][...]

        def small_pair(pair):
            return ins[3][2 * pair, :, 0:GW], ins[3][2 * pair + 1, :, 0:GW]

    done(wv)
    v_ref[...] = nn(x_ref[...], wv[...]).astype(bf16)
    done(v_ref)
    place = (iota((128, width), 1) % rows == iota((128, width), 0)).astype(bf16)

    def add(d, small, gains):
        inside = iota((8, width), 1) // rows == d
        return gains + jnp.where(inside, nn(small[:, 0:128], place), 0.0)

    def add_pair(pair, gains):
        first, second = small_pair(pair)
        return add(2 * pair + 1, second, add(2 * pair, first, gains))

    gain_ref[...] = lax.fori_loop(0, n // 2, add_pair, jnp.zeros(gain_ref.shape, f32))
    for d in range(head_size):
        taps = small_pair(d // 2)[d % 2].astype(f32)
        for i in range(heads_dev):
            for row, out in ((i, toep_ref), (heads_dev + i, peot_ref)):
                spread = jnp.broadcast_to(taps[row : row + 1, :], (CT, GW))
                spread = pltpu.roll(spread, 0, 1, stride=1, stride_axis=0)
                out[d * heads_dev + i] = spread[:, 0:CE].astype(bf16)


def newton_kernel(heads, me_ref, ql_ref, kl_ref, inv_ref, keep_ref, two_ref):
    unit = lax.rem(me_ref[0], 2 * heads)
    second = unit >= heads
    head = jnp.where(second, unit - heads, unit)
    width = ql_ref.shape[1]
    pick = (iota((width, HD), 0) == iota((width, HD), 1) + head * HD).astype(bf16)

    def mine(ref):
        rows = jnp.where(second, ref[M : 2 * M, :].astype(f32), ref[0:M, :].astype(f32))
        return nn(rows.astype(bf16), pick).astype(bf16)

    query, key = mine(ql_ref), mine(kl_ref)
    score = nt(query, key)
    e = jnp.exp(score - jnp.max(score, axis=1, keepdims=True))
    kernel = e / jnp.sum(e, axis=1, keepdims=True)
    column = jnp.sum(kernel, axis=0, keepdims=True)
    largest = jnp.max(column, axis=1, keepdims=True)
    eye = (iota((M, M), 0) == iota((M, M), 1)).astype(f32)
    z = kernel.T / largest
    two_ref[0] = kernel
    two_ref[1] = column + jnp.zeros_like(kernel)
    two_ref[2] = query.astype(f32)
    two_ref[3] = key.astype(f32)

    def iterate(step, z):
        p = exact(kernel, z)
        a = 7.0 * eye - p
        b = 15.0 * eye - exact(p, a)
        c = 13.0 * eye - exact(p, b)
        for i, value in enumerate((z, p, a, b, c)):
            keep_ref[step, i] = value
        return 0.25 * exact(z, c)

    inv_ref[...] = lax.fori_loop(0, NEWTON, iterate, z)


def newton_back_kernel(
    heads, me_ref, dinv_ref, inv_ref, keep_ref, two_ref, dq_ref, dk_ref
):
    turned = ((0,), (0,))
    across = ((1,), (1,))
    ready(keep_ref)
    kernel = two_ref[0]

    def iterate(i, state):
        dz, dkernel = state
        step = NEWTON - 1 - i
        z, p, a, b, c = (keep_ref[step, k] for k in range(5))
        dc = 0.25 * exact(z, dz, turned)
        db = -exact(p, dc, turned)
        da = -exact(p, db, turned)
        dp = -exact(dc, b, across) - exact(db, a, across) - da
        dkernel = dkernel + exact(dp, z, across)
        return 0.25 * exact(dz, c, across) + exact(kernel, dp, turned), dkernel

    dz, dkernel = lax.fori_loop(0, NEWTON, iterate, (dinv_ref[...], jnp.zeros_like(kernel)))
    column = two_ref[1]
    largest = jnp.max(column[0:1, :], axis=1, keepdims=True)
    dkernel = dkernel + dz.T / largest
    dlargest = -jnp.sum(dz * kernel.T, keepdims=True) / (largest * largest)
    top = (column == largest).astype(f32)
    ties = jnp.sum(top[0:1, :], axis=1, keepdims=True)
    dkernel = dkernel + dlargest * top / ties
    dscore = kernel * (dkernel - jnp.sum(dkernel * kernel, axis=1, keepdims=True))
    dquery = exact(dscore, two_ref[3])
    dkey = exact(dscore, two_ref[2], turned)
    unit = me_ref[0]
    width = dq_ref.shape[2]
    second = lax.rem(unit, 2 * heads) >= heads
    head = jnp.where(second, unit - heads, unit)
    place = (iota((HD, width), 1) == iota((HD, width), 0) + head * HD).astype(f32)
    live = unit < 2 * heads
    for out, value in ((dq_ref, dquery), (dk_ref, dkey)):
        wide = exact(jnp.where(live, value, 0.0), place)
        out[0] = jnp.where(second, 0.0, wide)
        out[1] = jnp.where(second, wide, 0.0)


def score3_kernel(heads, parts, got_ref, k_ref, v_ref, ql_ref, kl_ref, p_ref, out_ref, lands):
    tokens = k_ref.shape[0] // 2
    n = out_ref.shape[0]
    width = k_ref.shape[1]
    ready(got_ref)
    for d in range(n):
        got = got_ref[d].astype(f32)
        for i in range(4):
            lands[i, d * parts : (d + 1) * parts, :] = got[i * parts : (i + 1) * parts]
    for i, out in ((0, ql_ref), (2, kl_ref)):
        both = lands[i : i + 2]
        if n * parts != M:
            both = jnp.sum(both.reshape(2, M, n * parts // M, width), axis=2)
        out[...] = both.reshape(2 * M, width).astype(bf16)
    for u in range(2 * heads, n):
        out_ref[u] = jnp.zeros((SLOT, 128), bf16)
    ready(k_ref, v_ref)
    done(ql_ref, kl_ref)

    @pl.loop(0, 2)
    def _(s):
        for g in range(k_ref.shape[1] // GW):
            lanes = slice(g * GW, (g + 1) * GW)
            rows = aligned(s, tokens)
            land = block_diagonal(ql_ref[aligned(s, M), lanes])
            score = nt(land, k_ref[rows, lanes])
            top = jnp.max(score, axis=1, keepdims=True).astype(bf16).astype(f32)
            e = jnp.exp(score - top)
            total = jnp.sum(e, axis=1, keepdims=True)
            low = e.astype(bf16)
            p_ref[s, g] = low
            part = nn(low, v_ref[rows, lanes])
            high = total.astype(bf16).astype(f32)
            which = iota((GW, 8), 1)
            stats = jnp.where(which == 0, top, 0.0)
            stats = jnp.where(which == 1, high, stats)
            stats = jnp.where(which == 2, total - high, stats).astype(bf16)
            stats = tn(stats, identity(GW))
            for j in range(HP):
                slot = packed(low_lanes(diagonal_half(part, j), j))
                stat = low_lanes(stats[:, 128 * (j // 2) : 128 * (j // 2) + 128], j)
                slot = jnp.concatenate([slot, stat], axis=0)
                out_ref[s * heads + g * HP + j] = slot.astype(bf16)


def combine_kernel(got_ref, inv_ref, out_ref, sum_ref):
    n = got_ref.shape[0]
    half = HD // 2
    ready(got_ref)
    tops = jnp.concatenate([got_ref[d, half : half + 8].astype(f32)[0:1] for d in range(n)], axis=0)
    top = jnp.max(tops, axis=0, keepdims=True)
    weights = jnp.exp(tops - top)
    sums = []
    for d in range(n):
        stat = got_ref[d, half : half + 8].astype(f32)
        sums.append(stat[1:2] + stat[2:3])
    total = jnp.sum(weights * jnp.concatenate(sums, axis=0), axis=0, keepdims=True)
    total = jnp.where(total > 0.0, total, 1.0)
    weights = (weights / total).T
    lane = iota((half, 128), 1)
    acc = jnp.zeros((half, 128), f32)
    for d in range(n):
        by = weights[:, d : d + 1]
        by = jnp.where(lane < HD, by[0:half], by[half:HD])
        acc = acc + by * got_ref[d, 0:half].astype(f32)
    summary = unpacked(acc)
    sum_ref[...] = summary
    mixed = exact(inv_ref[...], summary)
    high = total.astype(bf16).astype(f32)
    slot = jnp.concatenate([packed(mixed), stacked([top, high, total - high])], axis=0)
    slot = slot.astype(bf16)
    for d in range(n):
        out_ref[d] = slot


def fill_extended(ext, ref, low_ref, high_ref, tokens):
    for s in range(2):
        ext[s, 0:REACH, :] = low_ref[s]
        ext[s, REACH : REACH + tokens, :] = ref[s * tokens : (s + 1) * tokens, :]
        ext[s, REACH + tokens : 2 * REACH + tokens, :] = high_ref[s]


def convolve(ext, toep_ref, s, g, tile):
    piece = ext[s, tile * CT : tile * CT + CE, aligned(g, GW)]
    lane = iota((CT, GW), 1) // HD
    out = nn(toep_ref[g * HP], piece)
    for j in range(1, HP):
        out = jnp.where(lane == j, nn(toep_ref[g * HP + j], piece), out)
    return out


def softmax1(land, queries):
    tokens = queries.shape[0]
    score = nt(land, queries).reshape(HP, M, tokens)
    e = jnp.exp(score - jnp.max(score, axis=1, keepdims=True))
    return (e / jnp.sum(e, axis=1, keepdims=True)).reshape(GW, tokens)


def kernel1_kernel(q_ref, v_ref, low_ref, high_ref, kl_ref, toep_ref, conv_ref, k1_ref, ext):
    tokens = q_ref.shape[0] // 2
    fill_extended(ext, v_ref, low_ref, high_ref, tokens)
    ready(q_ref, kl_ref, toep_ref)

    @pl.loop(0, 2)
    def _(s):
        for g in range(q_ref.shape[1] // GW):
            lanes = slice(g * GW, (g + 1) * GW)
            rows = aligned(s, tokens)
            land = block_diagonal(kl_ref[aligned(s, M), lanes])
            k1_ref[s, g] = softmax1(land, q_ref[rows, lanes]).astype(bf16)
            for tile in range(tokens // CT):
                at = pl.ds(pl.multiple_of(s * tokens + tile * CT, CT), CT)
                conv_ref[at, lanes] = convolve(ext, toep_ref, s, g, tile)


def norm(h):
    center = h - jnp.mean(h, axis=1, keepdims=True)
    rstd = lax.rsqrt(jnp.mean(center * center, axis=1, keepdims=True) + EPS)
    return center * rstd, rstd


def norm_back(dx, hat, rstd):
    return rstd * (
        dx - jnp.mean(dx, axis=1, keepdims=True) - hat * jnp.mean(dx * hat, axis=1, keepdims=True)
    )


RT = 128


def row_tiles(total, body):
    def step(i, c):
        body(pl.ds(pl.multiple_of(i * RT, RT), RT))
        return c

    lax.fori_loop(0, total // RT, step, 0, unroll=2)


def layer_kernel(chunks, heads, k1_ref, conv_ref, mixed_ref, x_ref, gain_ref, cot_ref, *refs):
    scratch, refs = refs[-9:], refs[:-9]
    heads_ref, act, du, n1b, dd, db, hat1, rstd1, acc = scratch
    hyper = len(refs) == 7
    weights, refs = (refs[:1], refs[1:]) if hyper else (refs[:3], refs[3:])
    mbd_ref, out_ref, dh1_ref, dheads_ref, gn_ref = refs[:5]
    grads = refs[5:]
    total, width = x_ref.shape
    tokens = total // 2

    if hyper:
        (fetched,) = weights
        all_ref = fetched.buf
        n, _, rows, _ = all_ref.shape
        per = n // chunks

        def w_up(c):
            return all_ref[:, chunks + c].reshape(width, width)

        def w_down(c):
            return all_ref[pl.ds(c * per, per), 0:chunks].reshape(width, width)

        def w_out():
            return all_ref[:, 2 * chunks].reshape(width, width)

        def put_up(c, g):
            all_ref[:, chunks + c] = g.reshape(n, rows, width)

        def put_down(c, g):
            all_ref[pl.ds(c * per, per), 0:chunks] = g.reshape(per, chunks, rows, width)

        def put_out(g):
            all_ref[:, 2 * chunks] = g.reshape(n, rows, width)

        out_ready, up_ready, down_ready = (functools.partial(fetched.ready, i) for i in range(3))
        out_done, up_done, down_done = (functools.partial(grads[0].done, i) for i in range(3))
    else:
        wo_ref, wu_ref, wd_ref = (w.buf for w in weights)
        w_up = lambda c: wu_ref[c]
        w_down = lambda c: wd_ref[c]
        w_out = lambda: wo_ref[...]

        def put_up(c, g):
            wu_ref[c] = g

        def put_down(c, g):
            wd_ref[c] = g

        def put_out(g):
            wo_ref[...] = g

        out_ready, up_ready, down_ready = (w.ready for w in weights)
        out_done, up_done, down_done = (g.done for g in grads)

    ready(k1_ref, conv_ref, mixed_ref)
    down = conv_ref.buf

    @pl.loop(0, 2)
    def _(s):
        for g in range(width // GW):
            lanes = slice(g * GW, (g + 1) * GW)
            span = aligned(s, tokens)
            mbd = block_from_slots(lambda j: mixed_ref[s * heads + g * HP + j, 0 : HD // 2])
            mbd_ref[s, g] = mbd
            heads_ref[span, lanes] = (tn(k1_ref[s, g], mbd) + down[span, lanes]).astype(bf16)

    done(mbd_ref)
    ready(gain_ref)
    g1 = gain_ref[6:7, :]
    g2 = gain_ref[7:8, :]
    gn_ref[...] = jnp.zeros(gn_ref.shape, f32)
    out_ready()
    ready(x_ref)
    down[...] = nn(heads_ref[...], w_out())

    def first(r):
        hat, rstd = norm(x_ref[r, :].astype(f32) + down[r, :])
        hat1[r, :] = hat
        rstd1[r, :] = jnp.broadcast_to(rstd, (RT, 128))
        value = hat * g1
        n1b[r, :] = value.astype(bf16)
        down[r, :] = value

    row_tiles(total, first)
    up_ready()
    down_ready()
    ready(cot_ref)

    @pl.loop(0, chunks)
    def _(c):
        up = nn(n1b[...], w_up(c))
        cdf = 0.5 * (1.0 + lax.erf(up * (0.5**0.5)))
        density = jnp.exp(-0.5 * up * up) * 0.3989422804014327
        value = (up * cdf).astype(bf16)
        act[c] = value
        du[c] = (cdf + up * density).astype(bf16)
        down[...] += nn(value, w_down(c))

    dh2 = dh1_ref.buf

    def second(r):
        hat, rstd = norm(down[r, :])
        out_ref[r, :] = (hat * g2).astype(bf16)
        g = cot_ref[r, :].astype(f32)
        gn_ref[1:2, :] += jnp.sum(g * hat, axis=0, keepdims=True)
        d = norm_back(g * g2, hat, rstd)
        dh2[r, :] = d
        dd[r, :] = d.astype(bf16)

    row_tiles(total, second)
    done(out_ref)

    @pl.loop(0, chunks)
    def _(c):
        part = (nt(dd[...], w_down(c)) * du[c].astype(f32)).astype(bf16)
        du[c] = part
        dh2[...] += nt(part, w_up(c))

    def third(r):
        hat = hat1[r, :]
        d = dh2[r, :]
        gn_ref[0:1, :] += jnp.sum(d * hat, axis=0, keepdims=True)
        d = norm_back(d * g1, hat, rstd1[r, :][:, 0:1])
        dh2[r, :] = d
        db[r, :] = d.astype(bf16)

    row_tiles(total, third)
    done(dh1_ref, gn_ref)
    dheads_ref[...] = nt(db[...], w_out()).astype(bf16)
    done(dheads_ref)

    @pl.loop(0, chunks)
    def _(c):
        acc[...] = tn(act[c], dd[...])
        put_down(c, acc[...].astype(bf16))

    down_done()

    @pl.loop(0, chunks)
    def _(c):
        acc[...] = tn(n1b[...], du[c])
        put_up(c, acc[...].astype(bf16))

    up_done()
    acc[...] = tn(heads_ref[...], db[...])
    put_out(acc[...].astype(bf16))
    out_done()


def attend_back_kernel(heads, dh_ref, k1_ref, mbd_ref, kl_ref, q_ref, dq_ref, dkl_ref, out_ref):
    tokens = q_ref.shape[0] // 2
    n = out_ref.shape[0]
    for u in range(2 * heads, n):
        out_ref[u] = jnp.zeros((HD // 2, 128), bf16)
    mask = block_mask()
    ready(dh_ref, k1_ref, mbd_ref, kl_ref, q_ref)

    @pl.loop(0, 2)
    def _(s):
        for g in range(q_ref.shape[1] // GW):
            lanes = slice(g * GW, (g + 1) * GW)
            rows = aligned(s, tokens)
            dh = dh_ref[rows, lanes]
            land = block_diagonal(kl_ref[aligned(s, M), lanes])
            low = k1_ref[s, g]
            k1 = low.astype(f32)
            dk1 = nt(mbd_ref[s, g], dh)
            row = jnp.sum((k1 * dk1).reshape(HP, M, tokens), axis=1, keepdims=True)
            centered = (dk1.reshape(HP, M, tokens) - row).reshape(GW, tokens)
            ds = (k1 * centered).astype(bf16)
            dq_ref[rows, lanes] = tn(ds, land)
            dland = jnp.where(mask, nn(ds, q_ref[rows, lanes]), 0.0)
            dkl_ref[s, :, lanes] = jnp.sum(dland.reshape(HP, M, GW), axis=0)
            dmixed = nn(low, dh)
            for j in range(HP):
                slot = packed(low_lanes(diagonal_half(dmixed, j), j))
                out_ref[s * heads + g * HP + j] = slot.astype(bf16)


def conv_back_kernel(
    dh_ref, dlow_ref, dhigh_ref, v_ref, low_ref, high_ref, peot_ref, dv_ref, gc_ref, dext, ext, gram
):
    tokens = v_ref.shape[0] // 2
    groups = v_ref.shape[1] // GW
    fill_extended(dext, dh_ref, dlow_ref, dhigh_ref, tokens)
    fill_extended(ext, v_ref, low_ref, high_ref, tokens)
    ready(peot_ref)
    lane = iota((CT, GW), 1) // HD
    ready(dh_ref)
    back = (iota((CT, CT), 0) + iota((CT, CT), 1) == CT - 1).astype(f32)

    @pl.loop(0, groups)
    def _(g):
        lanes = aligned(g, GW)
        gram[...] = jnp.zeros_like(gram)

        @pl.loop(0, 2)
        def _(s):
            for tile in range(tokens // CT):
                at = pl.ds(pl.multiple_of(s * tokens + tile * CT, CT), CT)
                dv_ref[at, lanes] = convolve(dext, peot_ref, s, g, tile)
                dh = dh_ref[at, lanes]
                each = jnp.concatenate(
                    [jnp.where(lane == j, dh, jnp.zeros_like(dh)) for j in range(HP)], axis=0
                )
                gram[:, 0:CE] += nt(each, ext[s, tile * CT : tile * CT + CE, lanes])

        rows = []
        for j in range(HP):
            turned = exact(back, gram[j * CT : (j + 1) * CT, :])
            rolled = pltpu.roll(turned, 0, 1, stride=1, stride_axis=0)
            rows.append(jnp.sum(rolled, axis=0, keepdims=True))
        gc_ref[g] = jnp.concatenate(rows, axis=0)


def owner_back_kernel(got_ref, inv_ref, sum_ref, out_ref, dinv_ref):
    n = got_ref.shape[0]
    ready(got_ref)
    dmixed = unpacked(
        lax.fori_loop(
            0, n, lambda d, a: a + got_ref[d].astype(f32), jnp.zeros((HD // 2, 128), f32)
        )
    )
    dsum = exact(inv_ref[...], dmixed, ((0,), (0,))).astype(bf16).astype(f32)
    ones = jnp.ones((8, 128), f32)
    row = exact(ones, dsum * sum_ref[...], ((1,), (1,)))[0:1]
    row = jnp.concatenate([row, jnp.zeros_like(row)], axis=1)
    high = row.astype(bf16).astype(f32)
    slot = jnp.concatenate([packed(dsum), stacked([high, row - high])], axis=0).astype(bf16)
    for d in range(n):
        out_ref[d] = slot
    done(out_ref)
    dinv_ref[...] = exact(dmixed, sum_ref[...], ((1,), (1,)))


def score3_back_kernel(
    heads, parts, sent_ref, stat_ref, dsum_ref, p_ref, k_ref, v_ref, ql_ref, dq2_ref, dk2_ref,
    dk1_ref, dk_ref, dv_ref, out_ref, dql,
):
    tokens = k_ref.shape[0] // 2
    n = out_ref.shape[0]
    mask = block_mask()
    ready(sent_ref, stat_ref, dsum_ref, p_ref, k_ref, v_ref, ql_ref, dq2_ref)

    @pl.loop(0, 2)
    def _(s):
        for g in range(k_ref.shape[1] // GW):
            lanes = slice(g * GW, (g + 1) * GW)
            rows = aligned(s, tokens)
            factors, terms = [], []
            for j in range(HP):
                u = s * heads + g * HP + j
                stat_rows = slice(HD // 2, HD // 2 + 8)
                local = sent_ref[u, stat_rows].astype(f32)[0:1]
                stat = stat_ref[u, stat_rows].astype(f32)
                factors.append(jnp.exp(local - stat[0:1]) / (stat[1:2] + stat[2:3]))
                d = dsum_ref[u, stat_rows].astype(f32)
                terms.append(d[0:1] + d[1:2])

            def joined(parts):
                lane = iota((1, 128), 1)
                halves = [
                    jnp.where(lane < HD, parts[j], pltpu.roll(parts[j + 1], HD, 1))
                    for j in range(0, HP, 2)
                ]
                return jnp.concatenate(halves, axis=1)

            rows_in = []
            for value in (joined(factors), joined(terms)):
                for _ in range(3):
                    term = value.astype(bf16).astype(f32)
                    rows_in.append(term)
                    value = value - term
            columns = nt(identity(GW), stacked(rows_in).astype(bf16))
            factor = columns[:, 0:1] + columns[:, 1:2] + columns[:, 2:3]
            term = columns[:, 3:4] + columns[:, 4:5] + columns[:, 5:6]
            k3 = p_ref[s, g].astype(f32) * factor
            dbd = block_from_slots(lambda j: dsum_ref[s * heads + g * HP + j, 0 : HD // 2])
            dk3 = nt(dbd, v_ref[rows, lanes])
            ds = (k3 * (dk3 - term)).astype(bf16)
            dland = jnp.where(mask, nn(ds, k_ref[rows, lanes]), 0.0)
            dql[s, :, lanes] = jnp.sum(dland.reshape(HP, M, GW), axis=0) + dq2_ref[s, :, lanes]
            land = block_diagonal(ql_ref[aligned(s, M), lanes])
            dk_ref[rows, lanes] = tn(ds, land)
            dv_ref[rows, lanes] = tn(k3.astype(bf16), dbd)
    for d in range(n):
        first = d * parts * M // (n * parts)
        span = slice(first, first + parts)
        pieces = [dql[0, span, :], dql[1, span, :]]
        pieces += [dk2_ref[s, span, :] + dk1_ref[s, span, :] for s in range(2)]
        if parts < 2:
            pieces.append(jnp.zeros((8 - 4 * parts, dql.shape[2]), f32))
        out_ref[d] = jnp.concatenate(pieces, axis=0).astype(bf16)


def two_terms(x):
    high = x.astype(bf16)
    return high, (x - high.astype(f32)).astype(bf16)


def final_kernel(
    cfg, me_ref, x_ref, dv3_ref, dvc_ref, dk3_ref, dq1_ref, wv, wqk, dh1_ref,
    dx_ref, sums_ref, gqk_ref, *refs
):
    n, core, hyper, rows, parts, scale, segment = cfg
    outs, acc, low, dv = refs[:-3], *refs[-3:]
    tokens = x_ref.shape[0] // 2
    each = tokens // parts
    dv[...] = (dvc_ref[...] + dv3_ref[...]).astype(bf16)
    acc[...] = tn(x_ref[...], dv[...])
    if hyper:
        emit(acc, 0, rows, rows, outs[0], outs[1], 0, me_ref[0], n, core, 2)
    else:
        outs[0][...] = acc[...]
    done(*outs)
    for s in range(2):
        for l in range(parts):
            span = slice(s * tokens + l * each, s * tokens + (l + 1) * each)
            at = s * parts + l
            sums_ref[at : at + 1, :] = jnp.sum(
                x_ref[span, :].astype(f32), axis=0, keepdims=True
            )
    done(sums_ref)
    low[1] = dk3_ref[...].astype(bf16)
    low[0] = dq1_ref[...].astype(bf16)
    ready(wqk, wv, dh1_ref)
    acc[...] = dh1_ref[...] + nt(dv[...], wv[...])

    @pl.loop(0, 2)
    def _(t):
        gqk_ref[t] = tn(x_ref[...], low[t]) * scale
        acc[...] += nt(low[t], wqk[t]) * scale

    dx_ref[...] = acc[...]


def landmark_sums(got_ref, factor):
    ready(got_ref)
    n, _, width = got_ref.shape
    zero = jnp.zeros((8, width), f32)
    return factor * lax.fori_loop(0, n, lambda d, a: a + got_ref[d].astype(f32), zero)


def landmark_kernel(cfg, me_ref, got_ref, sums_ref, gqk_ref, small_ref, *refs):
    n, core, hyper, rows, parts, scale, segment = cfg
    outs, acc = refs[:-1], refs[-1]
    me = me_ref[0]
    count = 2 * parts
    land = landmark_sums(got_ref, scale / segment)
    s_high, s_low = two_terms(sums_ref[0:count, :])
    left = jnp.concatenate([s_high, s_low, s_high], axis=0)
    for turn, base in enumerate((0, count)):
        high, low = two_terms(land[base : base + count, :])
        acc[...] = gqk_ref[turn] + tn(left, jnp.concatenate([high, high, low], axis=0))
        if hyper:
            keep, send = outs[2 * turn : 2 * turn + 2]
            emit(acc, 0, rows, rows, keep, send, 0, me, n, core, turn)
        else:
            outs[turn][...] = acc[...]
    if hyper:
        ready(small_ref)
        mine = me & 1
        span = slice(rows, rows + 8)

        def step(i, c):
            slot = scatter_slot(jnp.bitwise_xor(me - mine, 2 * i), n, core, 0)
            outs[0][slot, span, 0:GW] = small_ref[2 * i + mine]
            outs[1][slot, span, 0:GW] = small_ref[2 * i + 1 - mine]
            return c

        lax.fori_loop(0, n // 2, step, 0)


def tokens_kernel(cfg, got_ref, wqk, dx_ref, out_ref):
    n, core, hyper, rows, parts, scale, segment = cfg
    tokens = dx_ref.shape[0] // 2
    each = tokens // parts
    count = 2 * parts
    land = landmark_sums(got_ref, scale / segment)
    change = 0.0
    for turn, base in enumerate((0, count)):
        both = nt(jnp.concatenate(two_terms(land[base : base + count, :]), axis=0), wqk[turn])
        change = change + both[0:count] + both[count : 2 * count]
    for s in range(2):
        for l in range(parts):
            span = slice(s * tokens + l * each, s * tokens + (l + 1) * each)
            at = s * parts + l
            out_ref[span, :] = (dx_ref[span, :] + change[at : at + 1, :]).astype(bf16)


def merge_kernel(counts, *refs):
    ready(*refs[: 2 * sum(counts)])
    outs = refs[2 * sum(counts) :]
    at = 0
    for job, count in enumerate(counts):
        ins = refs[2 * at : 2 * (at + count)]
        at += count
        row = 0
        kept, sent = outs[2 * job], outs[2 * job + 1]
        for keep, got in zip(ins[0::2], ins[1::2]):
            span = slice(row, row + keep.shape[1])
            row += keep.shape[1]
            half = keep.shape[0] // 2

            @pl.loop(0, half)
            def _(j):
                kept[j, span] = keep[j].astype(f32) + got[j].astype(f32)
                sent[j, span] = (
                    keep[half + j].astype(f32) + got[half + j].astype(f32)
                ).astype(bf16)

        done(sent)


def last_kernel(splits, *refs):
    ins, outs = refs[: 2 * len(splits)], list(refs[2 * len(splits) :])
    for i, split in enumerate(splits):
        keep, got = ins[2 * i], ins[2 * i + 1]
        row = 0
        for count in split:
            span = slice(row, row + count)
            outs.pop(0)[...] = keep[0, span].astype(f32) + got[0, span].astype(f32)
            row += count


def unpack_kernel(chunks, got_ref, up_ref, down_ref, out_ref):
    out_ref[...] = got_ref[2 * chunks].astype(f32)
    rows, width = got_ref.shape[1:]
    for c in range(chunks):
        up_ref[:, c * width : (c + 1) * width] = got_ref[chunks + c].astype(f32)
        down_ref[c * rows : (c + 1) * rows, :] = got_ref[c].astype(f32)


def exchange(x):
    return lax.all_to_all(x, AX, 0, 0, tiled=True)


def per_device(
    tokens, w_query, w_key, w_value, w_out, conv_kernel, norm1_gain, w_up, w_down, norm2_gain, cotangent
):
    sequences, held, width = tokens.shape
    blk, head = lax.axis_size("blk"), lax.axis_size("head")
    n = blk * head
    heads_dev = conv_kernel.shape[0]
    heads = heads_dev * head
    rows = w_query.shape[0]
    hidden = w_up.shape[1]
    chunks = hidden // width
    segment = held * n // M
    parts = max(1, held // segment)
    groups = width // GW
    hyper = rows % 8 == 0 and n == 32
    core = 0 if n <= 32 else head.bit_length() - 1
    scale = HD**-0.25
    total = sequences * held
    me = (lax.axis_index("blk") * head + lax.axis_index("head")).astype(jnp.int32)
    me = me.reshape(1)
    x = tokens.reshape(total, width)

    if hyper:
        now, later = vmem_call(
            functools.partial(prepare_kernel, chunks),
            (
                shape_of((3 * rows + 8, width), bf16),
                shape_of(((2 * chunks + 1) * rows, width), bf16),
            ),
            (
                conv_kernel, jnp.stack([norm1_gain, norm2_gain]),
                w_query, w_key, w_value, w_out, w_up, w_down,
            ),
            scratch=[pltpu.VMEM((8, 128), f32)],
        )
        pieces, mid = cube_gather(now, n, core)
        later, _ = lax.optimization_barrier((later, mid))
        later = lax.all_gather(later, AX, axis=0).reshape(n, 2 * chunks + 1, rows, width)
        weights = (later,)
        weight_parts = {
            6: [
                (slice(None), slice(2 * chunks, None)),
                (slice(None), slice(chunks, 2 * chunks)),
                (slice(None), slice(0, chunks)),
            ]
        }
    else:
        taps = jnp.concatenate([conv_kernel, conv_kernel[:, ::-1]], axis=0)
        both = jnp.stack([norm1_gain, norm2_gain])
        extras = jnp.concatenate(
            [
                jnp.pad(taps, ((0, 0), (0, width - KW))),
                jnp.pad(both, ((0, 0), (0, width - rows))),
            ],
            axis=0,
        )
        pieces = [
            lax.all_gather(w, AX, axis=0, tiled=True) for w in (w_query, w_key, w_value)
        ] + [lax.all_gather(extras, AX, axis=0)]
        wo = lax.all_gather(w_out, AX, axis=0, tiled=True)
        wu = lax.all_gather(w_up, AX, axis=0, tiled=True)
        wu = wu.reshape(width, chunks, width).transpose(1, 0, 2)
        wd = lax.all_gather(w_down, AX, axis=0, tiled=True).reshape(chunks, width, width)
        weights = (wo, wu, wd)
        weight_parts = None

    cfg = (n, core, hyper, rows, parts, scale, segment, heads_dev, head)
    square_low = shape_of((total, width), bf16)
    square_full = shape_of((total, width), f32)
    weight = shape_of((width, width), bf16)
    weight_full = shape_of((width, width), f32)
    toeplitz = shape_of((heads, CT, CE), bf16)
    piece_parts = None
    if hyper:
        spans = (slice(0, 2 * rows), slice(2 * rows, None))
        piece_parts = {i: [(slice(None), span) for span in spans] for i in range(4)}
    queries, keys, lands, wqk = vmem_call(
        functools.partial(query_key_kernel, cfg),
        (
            square_low, square_low, shape_of((n, 8, width), bf16 if held >= segment else f32),
            shape_of((2, width, width), bf16),
        ),
        (me, *pieces, x),
        scalars=1,
        parts=piece_parts,
    )
    lands = exchange(lands)
    values, toep, peot, gains, wv = vmem_call(
        functools.partial(value_kernel, cfg),
        (square_low, toeplitz, toeplitz, shape_of((8, width), f32), weight),
        (me, x, *pieces),
        scalars=1,
    )
    lands, values = lax.optimization_barrier((lands, values))
    ahead = [(i, i + 1) for i in range(n - 1)]
    behind = [(i + 1, i) for i in range(n - 1)]

    def halo(y):
        y = y.reshape(sequences, held, width)
        low = lax.ppermute(y[:, held - REACH :], AX, ahead)
        high = lax.ppermute(y[:, :REACH], AX, behind)
        return low, high

    matrix = shape_of((M, M), f32)
    slots = shape_of((n, SLOT, 128), bf16)
    half_slots = shape_of((n, HD // 2, 128), bf16)
    land = shape_of((2 * M, width), bf16)
    q_land, k_land, p3, sent = vmem_call(
        functools.partial(score3_kernel, heads, parts),
        (land, land, shape_of((2, groups, GW, held), bf16), slots),
        (lands, keys, values),
        scratch=[pltpu.VMEM((4, n * parts, width), f32)],
    )
    got_sums = exchange(sent)
    inverse, newton_keep, kernel_two = vmem_call(
        functools.partial(newton_kernel, heads),
        (matrix, shape_of((NEWTON, 5, M, M), f32), shape_of((4, M, M), f32)),
        (me, q_land, k_land),
        scalars=1,
    )
    v_low, v_high = halo(values)
    got_sums, v_low, v_high = lax.optimization_barrier((got_sums, v_low, v_high))
    stat, summary = vmem_call(
        combine_kernel, (slots, shape_of((M, 128), f32)), (got_sums, inverse)
    )
    stat = exchange(stat)
    convolved, k1 = vmem_call(
        kernel1_kernel,
        (square_full, shape_of((2, groups, GW, held), bf16)),
        (queries, values, v_low, v_high, k_land, toep),
        scratch=[pltpu.VMEM((2, held + 2 * REACH, width), bf16)],
    )
    stat, k1 = lax.optimization_barrier((stat, k1))
    wide = pltpu.VMEM((chunks, total, width), bf16)
    low_buffer = pltpu.VMEM((total, width), bf16)
    if hyper:
        grad_shapes = [shape_of((n, 2 * chunks + 1, rows, width), bf16)]
        grad_parts, lent = {5: weight_parts[6]}, {5: 6}
    else:
        grad_shapes = [shape_of(w.shape, bf16) for w in weights]
        grad_parts, lent = None, {5: 6, 6: 7, 7: 8}
    mbd, layer_out, d_h1, d_heads, gain_sums, *grads = vmem_call(
        functools.partial(layer_kernel, chunks, heads),
        [
            shape_of((2, groups, GW, GW), bf16), square_low, square_full, square_low,
            shape_of((8, width), f32),
        ]
        + grad_shapes,
        (k1, convolved, stat, x, gains, cotangent.reshape(total, width), *weights),
        scratch=[
            low_buffer, wide, wide, low_buffer, low_buffer, low_buffer,
            pltpu.VMEM((total, width), f32),
            pltpu.VMEM((total, 128), f32),
            pltpu.VMEM((width, width), f32),
        ],
        parts=weight_parts,
        out_parts=grad_parts,
        lent=lent,
    )
    d_low, d_high = halo(d_heads)
    spread = shape_of((2, M, width), f32)
    d_q1, d_kl1, sent_back = vmem_call(
        functools.partial(attend_back_kernel, heads),
        (square_full, spread, half_slots),
        (d_heads, k1, mbd, k_land, queries),
    )
    got_back = exchange(sent_back)
    extended = pltpu.VMEM((2, held + 2 * REACH, width), bf16)
    d_vc, conv_sums = vmem_call(
        conv_back_kernel,
        (square_full, shape_of((groups, HP, GW), f32)),
        (d_heads, d_low, d_high, values, v_low, v_high, peot),
        scratch=[extended, extended, pltpu.VMEM((HP * CT, GW), f32)],
    )
    got_back, d_vc = lax.optimization_barrier((got_back, d_vc))
    d_sum, d_inverse = vmem_call(
        owner_back_kernel, (slots, matrix), (got_back, inverse, summary)
    )
    d_sum = exchange(d_sum)
    d_ql2, d_kl2 = vmem_call(
        functools.partial(newton_back_kernel, heads),
        (spread, spread),
        (me, d_inverse, inverse, newton_keep, kernel_two),
        scalars=1,
    )
    d_k3, d_v3, sent_land = vmem_call(
        functools.partial(score3_back_kernel, heads, parts),
        (square_full, square_full, shape_of((n, 8, width), bf16)),
        (sent, stat, d_sum, p3, keys, values, q_land, d_ql2, d_kl2, d_kl1),
        scratch=[pltpu.VMEM((2, M, width), f32)],
    )
    got_land = exchange(sent_land)
    if hyper:
        early = lax.psum_scatter(grads[0], AX, scatter_dimension=0, tiled=False)
    small = gain_sums[0:2].reshape(2, n, rows).transpose(1, 0, 2).reshape(n, 2 * rows)
    tap_sums = conv_sums[:, :, CT - 1 : CT - 1 + KW].reshape(head, heads_dev * KW)
    tap_sums = jnp.broadcast_to(tap_sums[None], (blk, head, heads_dev * KW)).reshape(n, -1)
    small = jnp.concatenate([small, tap_sums], axis=1)
    small = jnp.pad(small, ((0, 0), (0, GW - small.shape[1])))
    extra_rows = (8, 0, 0)
    if hyper:
        slot_shapes = [
            [shape_of((n // 2, rows + extra, width), bf16)] * 2 for extra in extra_rows
        ]
    else:
        slot_shapes = [[shape_of((width, width), f32)]] * 3
    final_cfg = (n, core, hyper, rows, parts, scale, segment)
    d_x, x_sums, g_both, *value_slots = vmem_call(
        functools.partial(final_kernel, final_cfg),
        [square_full, shape_of((8, width), f32), shape_of((2, width, width), f32)] + slot_shapes[2],
        (me, x, d_v3, d_vc, d_k3, d_q1, wv, wqk, d_h1),
        scalars=1,
        scratch=[
            pltpu.VMEM((width, width), f32),
            pltpu.VMEM((2, total, width), bf16),
            pltpu.VMEM((total, width), bf16),
        ],
    )
    projections = vmem_call(
        functools.partial(landmark_kernel, final_cfg),
        slot_shapes[0] + slot_shapes[1],
        (
            me, got_land, x_sums, g_both,
            jnp.broadcast_to(small[:, None], (n, 8, GW)).astype(bf16),
        ),
        scalars=1,
        scratch=[pltpu.VMEM((width, width), f32)],
    )
    projections = list(projections) + value_slots
    after, _ = lax.optimization_barrier((got_land, projections))
    d_tokens = vmem_call(
        functools.partial(tokens_kernel, final_cfg), square_low, (after, wqk, d_x)
    )
    d_tokens = d_tokens.reshape(tokens.shape)
    if hyper:
        grad_up, grad_down, grad_out = vmem_call(
            functools.partial(unpack_kernel, chunks),
            (
                shape_of((rows, hidden), f32), shape_of((chunks * rows, width), f32),
                shape_of((rows, width), f32),
            ),
            (early,),
        )
        grad_query, small, grad_key, grad_value = cube_scatter(
            [
                [(projections[0], projections[1])],
                [(projections[2], projections[3])],
                [(projections[4], projections[5])],
            ],
            ((rows, 8, rows), (rows,)),
            n,
            core,
        )
        small = small[0]
    else:

        def scatter(g):
            return lax.psum_scatter(g, AX, scatter_dimension=0, tiled=True)

        grad_out = scatter(grads[0].astype(f32))
        grad_up = scatter(grads[1].astype(f32).transpose(1, 0, 2).reshape(width, hidden))
        grad_down = scatter(grads[2].astype(f32).reshape(hidden, width))
        grad_query, grad_key, grad_value = (scatter(g) for g in projections)
        small = scatter(small)[0]
    return (
        layer_out.reshape(tokens.shape),
        d_tokens,
        grad_query,
        grad_key,
        grad_value,
        grad_out,
        small[2 * rows : 2 * rows + heads_dev * KW].reshape(heads_dev, KW),
        small[:rows],
        grad_up,
        grad_down,
        small[rows : 2 * rows],
    )


def solution(mesh):
    lined = P(None, AX, None)
    rowed = P(AX, None)
    gain = P(AX)
    taps = P("head", None)
    in_specs = (lined, rowed, rowed, rowed, rowed, taps, gain, rowed, rowed, gain, lined)
    out_specs = (lined, lined, rowed, rowed, rowed, rowed, taps, gain, rowed, rowed, gain)
    return jax.shard_map(
        per_device, mesh=mesh, in_specs=in_specs, out_specs=out_specs, check_vma=False
    )
```
